128 devices in a mesh: vel: 32 (over x_hi, y, z), space: 4 (over x_lo, core).
Axes of the slice: x: 4 (x_hi: 2, x_lo: 2; x = x_hi * 2 + x_lo), y: 4, z: 4, core: 2. Of those that a mesh axis runs over, the one named last changes fastest.
Arguments:
- dist: float32 [4096, 32, 1024], P('vel', 'space'), may hold values from -6 to 6
- vel_index: int32 [3, 4096], P(None, 'vel'), may hold values from 0 to 15, as said below
- relax: float32 [32, 1024], P('space'), may hold values from 0.05 to 0.9
- wall_mask: int32 [32, 1024], P('space'), may hold values 0 or 1
- macro_inverse: float32 [13, 13], replicated, may hold values from -1.5 to 1.5
Outputs:
- dist_out: float32 [4096, 32, 1024], P('vel', 'space')
- macro_fields: float32 [13, 32, 1024], P(None, 'space', 'vel')
- change_norm: float32 [2], replicated
The draws below stay inside these ranges and needn't reach their ends.
Inputs may be any that keep to these rules, and one draw needn't show every extreme that they name: `vel_index`: each point of the velocity grid of 4096 points appears in exactly one column.
All inputs are finite; a program needn't handle non-finite values. No bound on the sum of `wall_mask` on one device may be relied on, other than what follows from the above.
Results may differ from the reference program's by a relative error of at most 0.0003.
Values sent between devices are 32-bit elements; how exact they have to be, the bound alone decides.
A program may use at most 128 MiB of HBM per device.

```python
import math
import jax
import jax.numpy as jnp
from jax import lax

NVX = 16
NV = 4096
NY = 64
NZ = 16
NX = 32
NYZ = 1024
MOM = 13
SWEEPS = 3
ITERS = 2


def draw_vel_index(key, part):
    order = jax.random.permutation(key, NV).astype(jnp.int32)
    plane = NVX * NVX
    return jnp.stack([order // plane, order // NVX % NVX, order % NVX], 0).astype(jnp.int32)


def draw_macro_inverse(key, part):
    first, second = jax.random.split(jax.random.fold_in(key, 71))
    diagonal = jax.random.uniform(first, (MOM,), jnp.float32, 0.8, 1.2)
    spread = 0.35
    others = jnp.clip(jax.random.normal(second, (MOM, MOM), jnp.float32), -3.6, 3.6) * (spread / 3.6)
    identity = jnp.eye(MOM, dtype=jnp.float32)
    return (identity * diagonal[None, :] + others * (1.0 - identity)).astype(jnp.float32)


def place_ends(values, stream_key, smallest, largest):
    index_at = [jax.random.randint(jax.random.fold_in(stream_key, axis), (), 0, length) for axis, length in enumerate(values.shape)]
    longest = values.shape.index(max(values.shape))
    next_to = index_at[:longest] + [(index_at[longest] + 1) % values.shape[longest]] + index_at[longest + 1:]
    return values.at[tuple(index_at)].set(smallest).at[tuple(next_to)].set(largest)


def level_of(rng, shape, cuts, low, high):
    def one(axis_at, shards_of):
        heights = jax.random.uniform(jax.random.fold_in(jax.random.fold_in(rng, 6), axis_at), (shards_of,), jnp.float32, low / len(cuts), high / len(cuts))
        return jnp.repeat(jnp.exp(heights), shape[axis_at] // shards_of).reshape((-1,) + (1,) * (len(shape) - axis_at - 1))

    factor_of = one(*cuts[0])
    for cut in cuts[1:]:
        factor_of = factor_of * one(*cut)
    return factor_of


def bell_draw(own_key, extent, scale, most, shards=(), kind=jnp.bfloat16):
    array = scale * jax.random.normal(own_key, extent, jnp.float32)
    if shards:
        array = array * level_of(own_key, extent, shards, -0.22, 0.18)
    return jnp.clip(array, -most, most).astype(kind)


def setup_inputs(seed: int = 0) -> dict:
    seeds = jax.random.split(jax.random.key(seed), 6)
    return {
        "dist": bell_draw(seeds[0], (NV, NX, NYZ), 1.0, 6.0, ((0, 32), (1, 4)), jnp.float32),
        "vel_index": draw_vel_index(jax.random.fold_in(seeds[5], 71), 0),
        "relax": jnp.clip(jnp.exp(math.log(0.9) - 2.8903717 * jax.random.uniform(seeds[2], (NX, NYZ), jnp.float32) ** level_of(seeds[2], (NX, NYZ), ((0, 4),), -0.2, 0.2)), 0.05, 0.9),
        "wall_mask": place_ends((jax.random.randint(seeds[3], (NX, NYZ), 0, 8) < 1).astype(jnp.int32), jax.random.fold_in(seeds[3], 1), 0, 1),
        "macro_inverse": draw_macro_inverse(jax.random.fold_in(seeds[5], 71), 0),
    }


speed_range = 4.0
time_step = 0.08
coupling = 0.5

def velocities(vel_index):
    return speed_range * (2.0 * vel_index.astype(jnp.float32) + 1.0 - NVX) / NVX

def bases(velocity):
    cxv, cyv, czv = (velocity[0], velocity[1], velocity[2])
    square = cxv * cxv + cyv * cyv + czv * czv
    weights = (2.0 * speed_range / NVX) ** 3 * math.pi ** (-1.5) * jnp.exp(-square)
    heat = square - 2.5
    functions = jnp.stack([jnp.ones_like(cxv), cxv, cyv, czv, 2.0 * square / 3.0 - 1.0, 2.0 * cxv * cyv, 2.0 * cxv * czv, 2.0 * cyv * czv, cxv * cxv - cyv * cyv, cyv * cyv - czv * czv, cxv * heat, cyv * heat, czv * heat], 0)
    moment_rows = functions * weights[None, :]
    factor = 4.0 / 15.0
    shakhov = jnp.stack([jnp.ones_like(cxv), 2.0 * cxv, 2.0 * cyv, 2.0 * czv, square - 1.5, factor * cxv * heat, factor * cyv * heat, factor * czv * heat], 1)
    walls = jnp.stack([jnp.ones_like(cxv), square - 1.5], 1)
    return (moment_rows, shakhov, walls)

def upwind(block, speed, axis):
    lower = jnp.roll(block, 1, axis)
    higher = jnp.roll(block, -1, axis)
    return jnp.where(speed > 0, block - lower, higher - block)

def stream(block, velocity):
    cxv = velocity[0][:, None, None, None]
    cyv = velocity[1][:, None, None, None]
    czv = velocity[2][:, None, None, None]
    total = cxv * upwind(block, cxv, 1) + cyv * upwind(block, cyv, 2) + czv * upwind(block, czv, 3)
    return block - time_step * total

def smooth(source):
    field = source
    for sweep in range(SWEEPS):
        beside_all = jnp.zeros_like(field)
        for axis in (1, 2, 3):
            beside_all = beside_all + jnp.roll(field, 1, axis) + jnp.roll(field, -1, axis)
        field = (source + coupling * beside_all) / (1.0 + 6.0 * coupling)
    return field

def reference(dist, vel_index, relax, wall_mask, macro_inverse):
    highest = lax.Precision.HIGHEST
    blocksize = min(256, NV)
    nblocks = NV // blocksize
    cells = NX * NY * NZ
    velocity = velocities(vel_index)
    moment_rows, shakhov, walls = bases(velocity)
    vel_blocks = velocity.reshape(3, nblocks, blocksize).transpose(1, 0, 2)
    row_blocks = moment_rows.reshape(MOM, nblocks, blocksize).transpose(1, 0, 2)
    shak_blocks = shakhov.reshape(nblocks, blocksize, 8)
    wall_blocks = walls.reshape(nblocks, blocksize, 2)
    state = dist.reshape(nblocks, blocksize, NX, NY, NZ)
    relax_flat = relax.reshape(1, cells)
    wall_flat = wall_mask.reshape(1, cells)
    norms = []
    updated = None
    for step in range(ITERS):

        def accumulate(carry, pieces):
            block, vblock, rblock = pieces
            read = stream(block, vblock)
            return (carry + jnp.dot(rblock, read.reshape(blocksize, cells), precision=highest), None)
        moments = lax.scan(accumulate, jnp.zeros((MOM, cells), jnp.float32), (state, vel_blocks, row_blocks))[0]
        local = jnp.dot(macro_inverse, moments, precision=highest)
        smoothed = smooth(local[1:5].reshape(4, NX, NY, NZ)).reshape(4, cells)
        updated = jnp.concatenate([local[0:1], smoothed, local[5:]], 0)
        norms.append(jnp.sqrt(jnp.sum((updated - moments) ** 2)))
        fields = jnp.concatenate([updated[0:5], updated[10:13]], 0)
        wall_fields = jnp.stack([updated[0], updated[4]], 0)

        def renew(pieces):
            block, vblock, sblock, wblock = pieces
            read = stream(block, vblock).reshape(blocksize, cells)
            target = jnp.dot(sblock, fields, precision=highest)
            wall_value = jnp.dot(wblock, wall_fields, precision=highest)
            result = jnp.where(wall_flat > 0, wall_value, read + relax_flat * (target - read))
            return result.reshape(blocksize, NX, NY, NZ)
        state = lax.map(renew, (state, vel_blocks, shak_blocks, wall_blocks))
    return (state.reshape(NV, NX, NY * NZ), updated.reshape(MOM, NX, NY * NZ), jnp.stack(norms))
```

```python
import functools
import math

import jax
import jax.numpy as jnp
import numpy as np
from jax import lax
from jax.experimental import pallas as pl
from jax.experimental.pallas import tpu as pltpu
from jax.sharding import PartitionSpec as P

NVX = 16
NZ = 16
MOM = 13
SWEEPS = 3
speed_range = 4.0
time_step = 0.08
coupling = 0.5

MESH = pl.DeviceIdType.MESH
F32 = jnp.float32
BF16 = jnp.bfloat16
X = 8
CELLS = 1024
LT = CELLS // 128
NVD = 32
LV = 128
CH = 56
FIELD_ROWS = (1, 2, 3, 4, 0, 10, 11, 12)
OTHER_ROWS = (0, 5, 6, 7, 8, 9, 10, 11, 12)
HIGHEST = lax.Precision.HIGHEST


def functions_of(cx, cy, cz, xp):
    square = cx * cx + cy * cy + cz * cz
    weights = (2.0 * speed_range / NVX) ** 3 * math.pi ** (-1.5) * xp.exp(-square)
    heat = square - 2.5
    one = xp.ones_like(cx)
    rows = xp.stack(
        [
            one, cx, cy, cz, 2.0 * square / 3.0 - 1.0,
            2.0 * cx * cy, 2.0 * cx * cz, 2.0 * cy * cz,
            cx * cx - cy * cy, cy * cy - cz * cz,
            cx * heat, cy * heat, cz * heat,
        ],
        0,
    )
    factor = 4.0 / 15.0
    target = xp.stack(
        [2.0 * cx, 2.0 * cy, 2.0 * cz, square - 1.5, one, factor * cx * heat, factor * cy * heat, factor * cz * heat], 0
    )
    zero = xp.zeros_like(cx)
    centre = 1.0 - time_step * (xp.abs(cx) + xp.abs(cy) + xp.abs(cz))
    stencil = xp.stack(
        [
            centre,
            time_step * xp.maximum(cx, zero), time_step * xp.maximum(-cx, zero),
            time_step * xp.maximum(cy, zero), time_step * xp.maximum(-cy, zero),
            time_step * xp.maximum(cz, zero), time_step * xp.maximum(-cz, zero),
        ],
        0,
    )
    return rows * weights[None], target, stencil


def coupling_table():
    line = speed_range * (2.0 * np.arange(NVX) + 1.0 - NVX) / NVX
    cx, cy, cz = (a.reshape(-1) for a in np.meshgrid(line, line, line, indexing="ij"))
    rows, target, stencil = functions_of(cx, cy, cz, np)
    n = np.einsum("rv,ov,kv->ork", rows, stencil, target)
    planes = list(range(X)) + [-3, -2, -1, X, X + 1, X + 2]
    out = np.zeros((184, 5, 8, 24))
    for i, p in enumerate(planes):
        at = slice(13 * i, 13 * i + 13)
        out[at, 0, :, p + 8] += n[0]
        out[at, 0, :, p + 7] += n[1]
        out[at, 0, :, p + 9] += n[2]
        for j in range(4):
            out[at, 1 + j, :, p + 8] += n[3 + j]
    return np.ascontiguousarray(out.reshape(184, 5, 192).transpose(1, 0, 2)).astype(np.float32)


def split(a):
    hi = a.astype(BF16)
    return hi, (a - hi.astype(F32)).astype(BF16)


def split_table(a):
    hi = lax.reduce_precision(a, exponent_bits=8, mantissa_bits=7)
    return hi.astype(BF16), (a - hi).astype(BF16)


def yz_shifts(x):
    n = x.shape[0]
    lane = lax.broadcasted_iota(jnp.int32, (n, 128), 1)
    t = [x[:, 128 * i:128 * (i + 1)] for i in range(LT)]
    up = [pltpu.roll(a, 16, 1) for a in t]
    down = [pltpu.roll(a, 112, 1) for a in t]
    ylo = [jnp.where(lane < 16, up[i - 1], up[i]) for i in range(LT)]
    yhi = [jnp.where(lane >= 112, down[(i + 1) % LT], down[i]) for i in range(LT)]
    z = lane % NZ
    zlo = [jnp.where(z == 0, pltpu.roll(a, 113, 1), pltpu.roll(a, 1, 1)) for a in t]
    zhi = [jnp.where(z == NZ - 1, pltpu.roll(a, 15, 1), pltpu.roll(a, 127, 1)) for a in t]
    return t, ylo, yhi, zlo, zhi


def cat(parts):
    return jnp.concatenate(parts, axis=1)


def stencil_moments(q_ref, p):
    def rows(o):
        return q_ref[p, 16 * o:16 * o + 16, :]

    total = rows(0)
    ylo = yz_one(rows(3), 0)
    yhi = yz_one(rows(4), 1)
    zlo = yz_one(rows(5), 2)
    zhi = yz_one(rows(6), 3)
    return total + ylo + yhi + zlo + zhi


def yz_one(x, which):
    n = x.shape[0]
    lane = lax.broadcasted_iota(jnp.int32, (n, 128), 1)
    z = lane % NZ
    t = [x[:, 128 * i:128 * (i + 1)] for i in range(LT)]
    if which == 0:
        up = [pltpu.roll(a, 16, 1) for a in t]
        return cat([jnp.where(lane < 16, up[i - 1], up[i]) for i in range(LT)])
    if which == 1:
        down = [pltpu.roll(a, 112, 1) for a in t]
        return cat([jnp.where(lane >= 112, down[(i + 1) % LT], down[i]) for i in range(LT)])
    if which == 2:
        return cat([jnp.where(z == 0, pltpu.roll(a, 113, 1), pltpu.roll(a, 1, 1)) for a in t])
    return cat([jnp.where(z == NZ - 1, pltpu.roll(a, 15, 1), pltpu.roll(a, 127, 1)) for a in t])


def alpha_of(relax, wall):
    return jnp.where(wall > 0, 0.0, 1.0 - relax)


def stream_rows(src, p, g, ct):
    at = pl.ds(pl.multiple_of(8 * g, 8), 8)
    here, ylo, yhi, zlo, zhi = yz_shifts(src[p, at, :])
    before = src[p - 1, at, :]
    after = src[p + 1, at, :]
    k = [ct[o, at, :] for o in range(7)]
    out = []
    for i in range(LT):
        s = slice(128 * i, 128 * (i + 1))
        a = k[0] * here[i] + k[1] * before[:, s] + k[2] * after[:, s]
        b = k[3] * ylo[i] + k[4] * yhi[i] + k[5] * zlo[i] + k[6] * zhi[i]
        out.append(a + b)
    return out


def exchange(dist_hbm, rw, lm, ct, kx, kb, nc,
             a_out, g1_out, g2_out, mac_out, norm_out,
             dbuf, dt, at_, aa, hl, q1, q2, mine, edges, from_left, from_right, rwl, rwr,
             pbuf, rsbuf, ssum, fbuf, l1, h_out, h_left, h_right, u, b, g1, l2, nsend, nrecv, aleft, aright,
             sem_ld, s_nb, r_nb, s_rs, r_rs, s_ag, r_ag, s_nm, r_nm, sem_out):
    v = lax.axis_index("vel")
    s = lax.axis_index("space")
    left = (v, lax.rem(s + 3, 4))
    right = (v, lax.rem(s + 1, 4))

    loads = [pltpu.make_async_copy(dist_hbm.at[:, pl.ds(128 * t, 128)], dbuf.at[t], sem_ld.at[t]) for t in range(LT)]
    for c in loads:
        c.start()

    barrier = pltpu.get_barrier_semaphore()

    def greet(j, c):
        pl.semaphore_signal(barrier, inc=1, device_id=(lax.rem(v + j, NVD), s), device_id_type=MESH)
        return c

    lax.fori_loop(1, NVD, greet, 0)
    for j in (1, 2, 3):
        pl.semaphore_signal(barrier, inc=1, device_id=(v, lax.rem(s + j, 4)), device_id_type=MESH)

    zero_plane = jnp.zeros((LV, CELLS), F32)
    for p in (0, 1, 10, 11):
        dt[p] = zero_plane
    for p in (0, 1, 12, 13):
        at_[p] = zero_plane

    pl.semaphore_wait(barrier, NVD - 1 + 3)

    def swap(i, to_right, right_dst, to_left, left_dst):
        a = pltpu.make_async_remote_copy(to_right, right_dst, s_nb.at[2 * i], r_nb.at[2 * i],
                                         device_id=right, device_id_type=MESH)
        c = pltpu.make_async_remote_copy(to_left, left_dst, s_nb.at[2 * i + 1], r_nb.at[2 * i + 1],
                                         device_id=left, device_id_type=MESH)
        a.start()
        c.start()
        return a, c

    halo = swap(0, rw, rwl, rw, rwr)
    for c in loads:
        c.wait()

    def first(x, c):
        val = cat([dbuf[t, pl.ds(x, LV, stride=X), :] for t in range(LT)])
        dt[x + 2] = val
        hi, lo = split(val)
        hl[0:LV, :] = hi
        hl[LV:2 * LV, :] = lo
        q = jnp.dot(lm[...], hl[...], preferred_element_type=F32)
        q1[x] = q[0:112] + q[112:224]
        return c

    lax.fori_loop(0, X, first, 0)

    edges[0, 0:16, :] = q1[0, 32:48, :]
    edges[1, 0:16, :] = q1[X - 1, 16:32, :]

    def sum_first(x, c):
        mine[0, x] = stencil_moments(q1, x)
        return c

    lax.fori_loop(0, X, sum_first, 0)
    for x in range(X):
        if x > 0:
            mine[0, x] += q1[x - 1, 16:32, :]
        if x < X - 1:
            mine[0, x] += q1[x + 1, 32:48, :]

    for c in halo:
        c.wait()

    def second(i, c):
        x = i - 1

        def alpha_row(ref, row):
            return alpha_of(ref[pl.ds(row, 1), :], ref[pl.ds(row + X, 1), :])

        inside = jnp.clip(x, 0, X - 1)
        al = alpha_row(rw, inside)
        al = jnp.where(x < 0, alpha_row(rwl, X - 1), al)
        al = jnp.where(x >= X, alpha_row(rwr, 0), al)
        alb = jnp.broadcast_to(al, (8, CELLS))

        def group(g, cc):
            r = stream_rows(dt, i + 1, g, ct)
            at = pl.ds(pl.multiple_of(8 * g, 8), 8)
            at_[i + 2, at, :] = cat(r) * alb
            return cc

        lax.fori_loop(0, LV // 8, group, 0)
        hi, lo = split(at_[i + 2])
        hl[0:LV, :] = hi
        hl[LV:2 * LV, :] = lo
        q = jnp.dot(lm[...], hl[...], preferred_element_type=F32)
        q2[i] = q[0:112] + q[112:224]
        return c

    lax.fori_loop(0, X + 2, second, 0)

    edges[0, 16:32, :] = stencil_moments(q2, 0) + q2[1, 32:48, :]
    edges[0, 32:48, :] = q2[0, 32:48, :]
    edges[1, 16:32, :] = stencil_moments(q2, X + 1) + q2[X, 16:32, :]
    edges[1, 32:48, :] = q2[X + 1, 16:32, :]
    outer = swap(1, edges.at[1], from_left, edges.at[0], from_right)

    def sum_second(x, c):
        mine[1, x] = stencil_moments(q2, x + 1)
        return c

    lax.fori_loop(0, X, sum_second, 0)
    for x in range(X):
        if x > 0:
            mine[1, x] += q2[x, 16:32, :]
        if x < X - 1:
            mine[1, x] += q2[x + 2, 32:48, :]
    for c in outer:
        c.wait()
    mine[0, 0] += from_left[0:16, :]
    mine[1, 0] += from_left[16:32, :]
    mine[1, 1] += from_left[32:48, :]
    mine[0, X - 1] += from_right[0:16, :]
    mine[1, X - 1] += from_right[16:32, :]
    mine[1, X - 2] += from_right[32:48, :]
    pbuf[200:224, :] = jnp.zeros((24, CELLS), F32)
    for m in range(2):
        for x in range(X):
            pbuf[104 * m + 13 * x:104 * m + 13 * x + 13, :] = mine[m, x, 0:13, :]

    def chunk_of(o):
        return (pl.ds(pl.multiple_of(CH * (o // LT), 8), CH), pl.ds(pl.multiple_of(128 * lax.rem(o, LT), 128), 128))

    def send_part(j, c):
        o = lax.rem(v + j, NVD)
        rows, cols = chunk_of(o)
        pltpu.make_async_remote_copy(pbuf.at[rows, cols], rsbuf.at[j], s_rs, r_rs,
                                     device_id=(o, s), device_id_type=MESH).start()
        return c

    lax.fori_loop(1, NVD, send_part, 0)

    def third(i, c):
        def group(g, cc):
            r = stream_rows(at_, i + 1, g, ct)
            at = pl.ds(pl.multiple_of(8 * g, 8), 8)
            aa[i, at, :] = cat(r)
            return cc

        lax.fori_loop(0, LV // 8, group, 0)
        return c

    lax.fori_loop(0, X + 4, third, 0)
    edge_rows = swap(2, aa.at[pl.ds(10, 2)], aleft, aa.at[pl.ds(0, 2)], aright)

    all_parts = rsbuf.at[pl.ds(1, NVD - 1)]
    pltpu.make_async_copy(all_parts, all_parts, r_rs).wait()
    rows, cols = chunk_of(v)
    total = pbuf[rows, cols]

    def add_part(j, acc):
        return acc + rsbuf[j]

    total = lax.fori_loop(1, NVD, add_part, total)
    ssum[...] = total
    fbuf[rows, cols] = total
    def send_sum(j, c):
        o = lax.rem(v + j, NVD)
        pltpu.make_async_remote_copy(ssum, fbuf.at[rows, cols], s_ag, r_ag,
                                     device_id=(o, s), device_id_type=MESH).start()
        return c

    lax.fori_loop(1, NVD, send_sum, 0)
    pltpu.make_async_copy(all_parts, all_parts, s_rs).wait()
    pltpu.make_async_copy(all_parts, all_parts, r_ag).wait()

    f1 = fbuf[0:104, :]
    l1[...] = jnp.dot(kx[...], f1, precision=HIGHEST, preferred_element_type=F32)
    l20 = jnp.dot(kx[0:32, :], fbuf[104:208, :], precision=HIGHEST, preferred_element_type=F32)
    h_out[0:64, :] = l1[0:64, :]
    h_out[64:96, :] = l20
    halo2 = swap(3, h_out, h_left, h_out, h_right)
    for c in halo2:
        c.wait()

    zero8 = jnp.zeros((8, CELLS), F32)

    def clear_ends(k, c):
        for i in range(2):
            u[i, k, 0:8, :] = zero8
            u[i, k, 32:40, :] = zero8
        return c

    lax.fori_loop(0, 4, clear_ends, 0)

    def smooth():
        def start(k, c):
            u[0, k, 8:32, :] = b[k]
            return c

        lax.fori_loop(0, 4, start, 0)
        for sweep in range(SWEEPS):
            src, dst = sweep % 2, 1 - sweep % 2

            def row(k, c):
                for blk in range(3):
                    lo = 8 + 8 * blk
                    here, ylo, yhi, zlo, zhi = yz_shifts(u[src, k, lo:lo + 8, :])
                    before = u[src, k, lo - 1:lo + 7, :]
                    after = u[src, k, lo + 1:lo + 9, :]
                    side = cat([ylo[i] + yhi[i] + zlo[i] + zhi[i] for i in range(LT)])
                    near = before + after + side
                    u[dst, k, lo:lo + 8, :] = (b[k, 8 * blk:8 * blk + 8, :] + coupling * near) * (1.0 / (1.0 + 6.0 * coupling))
                return c

            lax.fori_loop(0, 4, row, 0)
        return SWEEPS % 2

    for k in range(4):
        b[k, 0:8, :] = h_left[8 * k:8 * k + 8, :]
        b[k, 8:16, :] = l1[8 * k:8 * k + 8, :]
        b[k, 16:24, :] = h_right[8 * k:8 * k + 8, :]
    last = smooth()

    plane = lax.broadcasted_iota(jnp.int32, (8, CELLS), 0)

    def gammas(ref):
        relax, wall = ref[0:X, :], ref[X:2 * X, :]
        beta = jnp.where(wall > 0, 0.0, relax)
        return beta, jnp.where(wall > 0, 1.0, relax)

    for blk, ref in enumerate((rwl, rw, rwr)):
        beta, both = gammas(ref)
        keep = plane >= 4 if blk == 0 else (plane < 4 if blk == 2 else None)
        for k in range(8):
            if k < 4:
                f = u[last, k, 8 + 8 * blk:16 + 8 * blk, :]
            elif blk == 0:
                f = h_left[8 * k:8 * k + 8, :]
            elif blk == 1:
                f = l1[8 * k:8 * k + 8, :]
            else:
                f = h_right[8 * k:8 * k + 8, :]
            val = f * (both if k in (3, 4) else beta)
            if keep is not None:
                val = jnp.where(keep, val, 0.0)
            g1[24 * k + 8 * blk:24 * k + 8 * blk + 8, :] = val
    send_g1 = pltpu.make_async_copy(g1, g1_out, sem_out.at[0])
    send_g1.start()

    def squares(l, sm):
        total = jnp.zeros((8, CELLS), F32)
        for i in range(9):
            d = l[64 + 8 * i:72 + 8 * i, :]
            total = total + d * d
        for k in range(4):
            d = u[sm, k, 16:24, :] - l[136 + 8 * k:144 + 8 * k, :]
            total = total + d * d
        out = total[:, 0:128]
        for i in range(1, LT):
            out = out + total[:, 128 * i:128 * (i + 1)]
        return out

    n1 = squares(l1, last)

    add = jnp.dot(nc[0], g1[...], precision=HIGHEST, preferred_element_type=F32)
    for j in range(4):
        add = add + jnp.dot(nc[1 + j], yz_one(g1[...], j), precision=HIGHEST, preferred_element_type=F32)
    m2 = fbuf[104:208, :] + add[0:104]
    l2[...] = jnp.dot(kx[...], m2, precision=HIGHEST, preferred_element_type=F32)
    edge = jnp.dot(kb[...], add[104:184], precision=HIGHEST, preferred_element_type=F32)
    for k in range(4):
        b[k, 0:8, :] = jnp.where(plane >= 5, h_left[64 + 8 * k:72 + 8 * k, :] + edge[8 * k:8 * k + 8], 0.0)
        b[k, 8:16, :] = l2[8 * k:8 * k + 8, :]
        b[k, 16:24, :] = jnp.where(plane < 3, h_right[64 + 8 * k:72 + 8 * k, :] + edge[32 + 8 * k:40 + 8 * k], 0.0)
    last = smooth()
    n2 = squares(l2, last)
    nsend[0] = n1
    nsend[1] = n2
    notes = []
    for j in (1, 2, 3):
        c = pltpu.make_async_remote_copy(nsend, nrecv.at[j - 1], s_nm.at[j - 1], r_nm.at[j - 1],
                                         device_id=(v, lax.rem(s + j, 4)), device_id_type=MESH)
        c.start()
        notes.append(c)

    beta, both = gammas(rw)
    for k in range(8):
        f = u[last, k, 16:24, :] if k < 4 else l2[8 * k:8 * k + 8, :]
        g2_out[8 * k:8 * k + 8, :] = f * (both if k in (3, 4) else beta)

    tile = pl.ds(pl.multiple_of(128 * (v // 4), 128), 128)
    turn = lax.rem(128 - 32 * lax.rem(v, 4), 128)
    for r in range(MOM):
        if 1 <= r <= 4:
            f = u[last, r - 1, 16:24, tile]
        elif r == 0:
            f = l2[32:40, tile]
        elif r >= 10:
            f = l2[40 + 8 * (r - 10):48 + 8 * (r - 10), tile]
        else:
            f = l2[168 + 8 * (r - 5):176 + 8 * (r - 5), tile]
        mac_out[r] = pltpu.roll(f, turn, 1)[:, 0:32]

    for c in edge_rows:
        c.wait()
    for i in range(2):
        aa[2 + i] += aleft[i]
        aa[8 + i] += aright[i]
    send_a = pltpu.make_async_copy(aa.at[pl.ds(2, X)], a_out, sem_out.at[1])
    send_a.start()

    for c in notes:
        c.wait()
    both_n = [nsend[i] + nrecv[0, i] + nrecv[1, i] + nrecv[2, i] for i in range(2)]
    sums = [jnp.sqrt(jnp.sum(t)) for t in both_n]
    lane = lax.broadcasted_iota(jnp.int32, (8, 128), 1)
    norm_out[...] = jnp.where(lane == 0, sums[0], sums[1])
    send_g1.wait()
    send_a.wait()
    pltpu.make_async_copy(all_parts, all_parts, s_ag).wait()


PAIRS = 4


def renew(a_hbm, g1_ref, g2_ref, rw_ref, lt_ref, out_hbm, abuf, obuf, stage, rhs, sem_in, sem_out):
    fetch = [
        pltpu.make_async_copy(a_hbm.at[:, :, pl.ds(256 * i, 256)], abuf.at[i], sem_in.at[i]) for i in range(PAIRS)
    ]
    for c in fetch:
        c.start()
    alpha = alpha_of(rw_ref[0:X, :], rw_ref[X:2 * X, :])

    for k in range(8):
        here, ylo, yhi, zlo, zhi = yz_shifts(g1_ref[24 * k + 8:24 * k + 16, :])
        before = g1_ref[24 * k + 7:24 * k + 15, :]
        after = g1_ref[24 * k + 9:24 * k + 17, :]
        for t in range(LT):
            cols = slice(128 * t, 128 * (t + 1))
            vals = (here[t], before[:, cols], after[:, cols], ylo[t], yhi[t], zlo[t], zhi[t])
            for o, val in enumerate(vals):
                stage[t, 64 * o + 8 * k:64 * o + 8 * k + 8, :] = val * alpha[:, cols]
            stage[t, 448 + 8 * k:456 + 8 * k, :] = g2_ref[8 * k:8 * k + 8, cols]

    def spread(x, c):
        for t in range(LT):
            hi, lo = split(stage[t, pl.ds(x, 64, stride=X), :])
            cols = slice(128 * t, 128 * (t + 1))
            rhs[x, 0:64, cols] = hi
            rhs[x, 64:128, cols] = lo
            rhs[x, 128:192, cols] = hi
            rhs[x, 192:256, cols] = lo
        return c

    lax.fori_loop(0, X, spread, 0)

    puts = []
    for i in range(PAIRS):
        fetch[i].wait()

        def plane(x, c):
            al = alpha_of(rw_ref[pl.ds(x, 1), 256 * i:256 * (i + 1)], rw_ref[pl.ds(x + X, 1), 256 * i:256 * (i + 1)])
            val = jnp.dot(lt_ref[...], rhs[x, :, 256 * i:256 * (i + 1)], preferred_element_type=F32) + al * abuf[i, x]
            obuf[2 * i, pl.ds(x, LV, stride=X), :] = val[:, 0:128]
            obuf[2 * i + 1, pl.ds(x, LV, stride=X), :] = val[:, 128:256]
            return c

        lax.fori_loop(0, X, plane, 0)
        for t in (2 * i, 2 * i + 1):
            c = pltpu.make_async_copy(obuf.at[t], out_hbm.at[:, pl.ds(128 * t, 128)], sem_out.at[t])
            c.start()
            puts.append(c)
    for c in puts:
        c.wait()


def shards(nc, dist, vel_index, relax, wall_mask, macro_inverse):
    velocity = speed_range * (2.0 * vel_index.astype(F32) + 1.0 - NVX) / NVX
    rows, target, stencil = functions_of(velocity[0], velocity[1], velocity[2], jnp)
    rows16 = jnp.concatenate([rows, jnp.zeros((3, LV), F32)], 0)
    lm = (stencil[:, None, :] * rows16[None]).reshape(112, LV)
    hi, lo = split_table(lm)
    lm = jnp.concatenate([jnp.concatenate([hi, hi], 1), jnp.concatenate([lo, jnp.zeros_like(lo)], 1)], 0)
    ct = jnp.broadcast_to(stencil[:, :, None], (7, LV, 128))
    lt = jnp.concatenate([(stencil[:, None, :] * target[None]).reshape(56, LV), target], 0).T
    hi, lo = split_table(lt)
    lt = jnp.concatenate([hi, hi, lo, lo], 1)

    eye = jnp.eye(X, dtype=F32)
    ident = jnp.eye(MOM, dtype=F32)
    table = jnp.concatenate(
        [macro_inverse[jnp.array(FIELD_ROWS)], (macro_inverse - ident)[jnp.array(OTHER_ROWS)], ident[1:5], macro_inverse[5:10]], 0
    )
    kx = (table[:, None, None, :] * eye[None, :, :, None]).reshape(26 * X, X * MOM)
    place = np.zeros((2, 8, 6), np.float32)
    for i in range(3):
        place[0, 5 + i, i] = 1.0
        place[1, i, 3 + i] = 1.0
    kb = (macro_inverse[1:5][None, :, None, None, :] * place[:, None, :, :, None]).reshape(64, 78)
    kb = jnp.concatenate([kb, jnp.zeros((64, 2), F32)], 1)
    rw = jnp.concatenate([relax, wall_mask.astype(F32)], 0)

    vmem = pl.BlockSpec(memory_space=pltpu.VMEM)
    hbm = pl.BlockSpec(memory_space=pl.ANY)
    dma = pltpu.SemaphoreType.DMA
    sds = jax.ShapeDtypeStruct
    a, g1, g2, mac, norm = pl.pallas_call(
        exchange,
        out_shape=(
            sds((X, LV, CELLS), F32), sds((192, CELLS), F32), sds((64, CELLS), F32),
            sds((MOM, X, 32), F32), sds((8, 128), F32),
        ),
        in_specs=[hbm] + [vmem] * 6,
        out_specs=(hbm, hbm, vmem, vmem, vmem),
        scratch_shapes=[
            pltpu.VMEM((LT, LV * X, 128), F32),
            pltpu.VMEM((X + 4, LV, CELLS), F32),
            pltpu.VMEM((X + 6, LV, CELLS), F32),
            pltpu.VMEM((X + 4, LV, CELLS), F32),
            pltpu.VMEM((2 * LV, CELLS), BF16),
            pltpu.VMEM((X, 112, CELLS), F32),
            pltpu.VMEM((X + 2, 112, CELLS), F32),
            pltpu.VMEM((2, X, 16, CELLS), F32),
            pltpu.VMEM((2, 48, CELLS), F32),
            pltpu.VMEM((48, CELLS), F32),
            pltpu.VMEM((48, CELLS), F32),
            pltpu.VMEM((2 * X, CELLS), F32),
            pltpu.VMEM((2 * X, CELLS), F32),
            pltpu.VMEM((4 * CH, CELLS), F32),
            pltpu.VMEM((NVD, CH, 128), F32),
            pltpu.VMEM((CH, 128), F32),
            pltpu.VMEM((4 * CH, CELLS), F32),
            pltpu.VMEM((26 * X, CELLS), F32),
            pltpu.VMEM((96, CELLS), F32),
            pltpu.VMEM((96, CELLS), F32),
            pltpu.VMEM((96, CELLS), F32),
            pltpu.VMEM((2, 4, 40, CELLS), F32),
            pltpu.VMEM((4, 24, CELLS), F32),
            pltpu.VMEM((192, CELLS), F32),
            pltpu.VMEM((26 * X, CELLS), F32),
            pltpu.VMEM((2, 8, 128), F32),
            pltpu.VMEM((3, 2, 8, 128), F32),
            pltpu.VMEM((2, LV, CELLS), F32),
            pltpu.VMEM((2, LV, CELLS), F32),
            dma((LT,)), dma((8,)), dma((8,)), dma, dma, dma, dma, dma((3,)), dma((3,)), dma((2,)),
        ],
        compiler_params=pltpu.CompilerParams(collective_id=0, has_side_effects=True, vmem_limit_bytes=60 * 2 ** 20),
        name="exchange",
    )(dist.reshape(LV * X, CELLS), rw, lm, ct, kx, kb, nc)

    out = pl.pallas_call(
        renew,
        out_shape=sds((LV * X, CELLS), F32),
        in_specs=[hbm] + [vmem] * 4,
        out_specs=hbm,
        scratch_shapes=[
            pltpu.VMEM((PAIRS, X, LV, 256), F32),
            pltpu.VMEM((LT, LV * X, 128), F32),
            pltpu.VMEM((LT, 512, 128), F32),
            pltpu.VMEM((X, 256, CELLS), BF16),
            dma((PAIRS,)), dma((LT,)),
        ],
        compiler_params=pltpu.CompilerParams(vmem_limit_bytes=40 * 2 ** 20),
        name="renew",
    )(a, g1, g2, rw, lt)
    return (out.reshape(LV, X, CELLS), mac, norm[0, 0:2])


def solution(mesh):
    nc = coupling_table()
    return jax.shard_map(
        lambda *args: shards(jnp.asarray(nc), *args),
        mesh=mesh,
        in_specs=(P("vel", "space", None), P(None, "vel"), P("space", None), P("space", None), P()),
        out_specs=(P("vel", "space", None), P(None, "space", "vel"), P()),
        check_vma=False,
    )
```

```python
import functools
import math

import jax
import jax.numpy as jnp
import numpy as np
from jax import lax
from jax.experimental import pallas as pl
from jax.experimental.pallas import tpu as pltpu
from jax.sharding import PartitionSpec as P

NVX = 16
NZ = 16
MOM = 13
SWEEPS = 3
speed_range = 4.0
time_step = 0.08
coupling = 0.5

MESH = pl.DeviceIdType.MESH
F32 = jnp.float32
BF16 = jnp.bfloat16
X = 8
CELLS = 1024
LT = CELLS // 128
RING = 4
PEERS = RING * RING
LV = 128
CH = 56
HALO = 4
EXT = X + 2 * HALO
FIELD_ROWS = (1, 2, 3, 4, 0, 10, 11, 12)
OTHER_ROWS = (0, 5, 6, 7, 8, 9, 10, 11, 12)
HIGHEST = lax.Precision.HIGHEST


def functions_of(cx, cy, cz, xp=jnp):
    square = cx * cx + cy * cy + cz * cz
    weights = (2.0 * speed_range / NVX) ** 3 * math.pi ** (-1.5) * xp.exp(-square)
    heat = square - 2.5
    one = xp.ones_like(cx)
    rows = [
        one, cx, cy, cz, 2.0 * square / 3.0 - 1.0,
        2.0 * cx * cy, 2.0 * cx * cz, 2.0 * cy * cz,
        cx * cx - cy * cy, cy * cy - cz * cz,
        cx * heat, cy * heat, cz * heat,
    ]
    factor = 4.0 / 15.0
    target = [2.0 * cx, 2.0 * cy, 2.0 * cz, square - 1.5, one, factor * cx * heat, factor * cy * heat, factor * cz * heat]
    stencil = [1.0 - time_step * (xp.abs(cx) + xp.abs(cy) + xp.abs(cz))]
    for c in (cx, cy, cz):
        stencil += [time_step * xp.maximum(c, 0.0), time_step * xp.maximum(-c, 0.0)]
    return [r * weights for r in rows], target, stencil


def selection():
    sel = np.zeros((26, MOM))
    own = np.zeros((26, MOM))
    for j in range(26):
        if j < 8:
            sel[j, FIELD_ROWS[j]] = 1
        elif j < 17:
            sel[j, OTHER_ROWS[j - 8]] = 1
            own[j, OTHER_ROWS[j - 8]] = -1
        elif j < 21:
            own[j, j - 16] = 1
        else:
            sel[j, j - 16] = 1
    eye = np.eye(X)
    sel = np.repeat(sel, X, 0)
    spread = np.tile(np.eye(MOM), (1, X))
    mask = np.repeat(np.tile(eye, (26, 1)), MOM, 1)
    fixed = np.einsum("jr,xp->jxpr", own, eye).reshape(26 * X, X * MOM)
    return [a.astype(np.float32) for a in (sel, spread, mask, fixed)]


def coupling_table():
    line = speed_range * (2.0 * np.arange(NVX) + 1.0 - NVX) / NVX
    cx, cy, cz = (a.reshape(-1) for a in np.meshgrid(line, line, line, indexing="ij"))
    rows, target, stencil = functions_of(cx, cy, cz, np)
    n = np.einsum("rv,ov,kv->ork", rows, stencil, target)
    near = np.zeros((X, MOM, 8, EXT))
    side = np.zeros((X, MOM, 4, 8, X))
    for x in range(X):
        near[x, :, :, x + HALO] += n[0]
        near[x, :, :, x + HALO - 1] += n[1]
        near[x, :, :, x + HALO + 1] += n[2]
        for j in range(4):
            side[x, :, j, :, x] += n[3 + j]
    table = np.concatenate([near.reshape(X * MOM, 8 * EXT), side.reshape(X * MOM, 32 * X)], 1)
    return table.astype(np.float32)


def split(a):
    hi = a.astype(BF16)
    return hi, (a - hi.astype(F32)).astype(BF16)


def cat(parts):
    return jnp.concatenate(parts, axis=1)


def tiles(x):
    return [x[:, 128 * i:128 * (i + 1)] for i in range(LT)]


def y_shifts(t):
    lane = lax.broadcasted_iota(jnp.int32, t[0].shape, 1)
    up = [pltpu.roll(a, 16, 1) for a in t]
    down = [pltpu.roll(a, 112, 1) for a in t]
    ylo = [jnp.where(lane < 16, up[i - 1], up[i]) for i in range(LT)]
    yhi = [jnp.where(lane >= 112, down[(i + 1) % LT], down[i]) for i in range(LT)]
    return ylo, yhi


def z_shifts(t):
    z = lax.broadcasted_iota(jnp.int32, t[0].shape, 1) % NZ
    zlo = [jnp.where(z == 0, pltpu.roll(a, 113, 1), pltpu.roll(a, 1, 1)) for a in t]
    zhi = [jnp.where(z == NZ - 1, pltpu.roll(a, 15, 1), pltpu.roll(a, 127, 1)) for a in t]
    return zlo, zhi


def yz_shifts(x):
    t = tiles(x)
    return (t,) + y_shifts(t) + z_shifts(t)


def stencil_moments(q_ref, p):
    def rows(o, at=p):
        return tiles(q_ref[at, 16 * o:16 * o + 16, :])

    ylo, _ = y_shifts(rows(3))
    _, yhi = y_shifts(rows(4))
    zlo, _ = z_shifts(rows(5))
    _, zhi = z_shifts(rows(6))
    here, before, after = rows(0), rows(1, p - 1), rows(2, p + 1)
    return cat([(here[i] + before[i] + after[i]) + (ylo[i] + yhi[i]) + (zlo[i] + zhi[i]) for i in range(LT)])


def alpha_of(relax, wall):
    return jnp.where(wall > 0, 0.0, 1.0 - relax)


def stream_plane(src, halves, p, h, ct, zmat, scale=None):
    lane = lax.broadcasted_iota(jnp.int32, (LV, 128), 1)
    k0, cx, cy, cz = (ct[i] for i in range(4))
    px, py, pz = cx > 0, cy > 0, cz > 0
    kx, ky, kz = jnp.abs(cx), jnp.abs(cy), jnp.abs(cz)
    t = [src[p, :, 128 * i:128 * (i + 1)] for i in range(LT)]
    z = [
        jnp.dot(
            cat([halves[h, 0:LV, 128 * i:128 * (i + 1)], halves[h, LV:2 * LV, 128 * i:128 * (i + 1)]]),
            zmat[...],
            preferred_element_type=F32,
        )
        for i in range(LT)
    ]
    up = [pltpu.roll(a, 16, 1) for a in t]
    down = [pltpu.roll(a, 112, 1) for a in t]
    out = []
    for i in range(LT):
        s = slice(128 * i, 128 * (i + 1))
        in_x = jnp.where(px, src[p - 1, :, s], src[p + 1, :, s])
        in_y = jnp.where(
            py,
            jnp.where(lane < 16, up[i - 1], up[i]),
            jnp.where(lane >= 112, down[(i + 1) % LT], down[i]),
        )
        in_z = jnp.where(pz, z[i][:, 0:128], z[i][:, 128:256])
        val = (k0 * t[i] + kx * in_x) + (ky * in_y + kz * in_z)
        out.append(val if scale is None else val * scale[:, s])
    return out


def exchange(dist_hbm, relax_ref, wall_ref, vel_ref, inv_ref, sel_ref, spread_ref, mask_ref, fixed_ref, nc,
             a_out, g1_out, g2_out, mac_out, norm_out,
             dbuf, dt, at_, aa, dhl, ahl, q1, q2, mine, edges, from_left, from_right, rw, rwl, rwr,
             mrows, lm, ct, zmat, kx, pbuf, rsbuf, ssum, xbuf, total, fbuf, l1, h_left, h_right, b2out, b2l, b2r,
             u, b, g1, rhs, add, l2, nsend, nrecv, aleft, aright,
             sem_ld, s_nb, r_nb, s_rs, r_rs, s_ag, r_ag, s_x, r_x, s_nm, r_nm, sem_out):
    v = lax.axis_index("vel")
    s = lax.axis_index("space")
    left = (v, lax.rem(s + 3, 4))
    right = (v, lax.rem(s + 1, 4))
    far = v // PEERS
    place = lax.rem(v, PEERS)
    partner = ((1 - far) * PEERS + place, s)

    def peer(o):
        return (far * PEERS + o, s)

    loads = [pltpu.make_async_copy(dist_hbm.at[:, pl.ds(128 * t, 128)], dbuf.at[t], sem_ld.at[t]) for t in range(LT)]
    for c in loads:
        c.start()

    barrier = pltpu.get_barrier_semaphore()

    def greet(j, c):
        pl.semaphore_signal(barrier, inc=1, device_id=peer(lax.rem(place + j, PEERS)), device_id_type=MESH)
        return c

    lax.fori_loop(1, PEERS, greet, 0)
    pl.semaphore_signal(barrier, inc=1, device_id=partner, device_id_type=MESH)
    for j in (1, 2, 3):
        pl.semaphore_signal(barrier, inc=1, device_id=(v, lax.rem(s + j, 4)), device_id_type=MESH)

    rw[0:X, :] = relax_ref[...]
    rw[X:2 * X, :] = wall_ref[...].astype(F32)
    vel = speed_range * (2.0 * vel_ref[...].astype(F32) + 1.0 - NVX) / NVX
    cx, cy, cz = vel[0:1], vel[1:2], vel[2:3]
    rows, _, stencil = functions_of(cx, cy, cz)
    mrows[...] = jnp.zeros_like(mrows)
    for r in range(MOM):
        mrows[r:r + 1, :] = rows[r]
    for o in range(7):
        hi, lo = split(mrows[...] * stencil[o])
        lm[16 * o:16 * o + 16, 0:LV] = hi
        lm[16 * o:16 * o + 16, LV:2 * LV] = hi
        lm[112 + 16 * o:128 + 16 * o, 0:LV] = lo
        lm[112 + 16 * o:128 + 16 * o, LV:2 * LV] = jnp.zeros_like(lo)
    for i, row in enumerate((stencil[0], time_step * cx, time_step * cy, time_step * cz)):
        ct[i] = jnp.transpose(jnp.broadcast_to(row, (LV, LV)))
    src_lane = lax.broadcasted_iota(jnp.int32, (LV, LV), 0)
    dst_lane = lax.broadcasted_iota(jnp.int32, (LV, LV), 1)
    dst_z = dst_lane % NZ
    lower = jnp.where(src_lane == jnp.where(dst_z == 0, dst_lane + NZ - 1, dst_lane - 1), 1.0, 0.0).astype(BF16)
    upper = jnp.where(src_lane == jnp.where(dst_z == NZ - 1, dst_lane - NZ + 1, dst_lane + 1), 1.0, 0.0).astype(BF16)
    for i in range(2):
        zmat[LV * i:LV * (i + 1), 0:LV] = lower
        zmat[LV * i:LV * (i + 1), LV:2 * LV] = upper
    part = jnp.dot(sel_ref[...], inv_ref[...], precision=HIGHEST, preferred_element_type=F32)
    part = jnp.dot(part, spread_ref[...], precision=HIGHEST, preferred_element_type=F32)
    kx[...] = part * mask_ref[...] + fixed_ref[...]
    zero_plane = jnp.zeros((LV, CELLS), F32)
    for p in (0, 9):
        dt[p] = zero_plane
        q1[p, 16:48, :] = jnp.zeros((32, CELLS), F32)
    for p in (0, 11):
        at_[p] = zero_plane
    for m in range(2):
        pbuf[m, 104:112, :] = jnp.zeros((8, CELLS), F32)

    pl.semaphore_wait(barrier, PEERS - 1 + 1 + 3)

    def swap(i, to_right, right_dst, to_left, left_dst):
        a = pltpu.make_async_remote_copy(to_right, right_dst, s_nb.at[2 * i], r_nb.at[2 * i],
                                         device_id=right, device_id_type=MESH)
        c = pltpu.make_async_remote_copy(to_left, left_dst, s_nb.at[2 * i + 1], r_nb.at[2 * i + 1],
                                         device_id=left, device_id_type=MESH)
        a.start()
        c.start()
        return a, c

    def settle(copies):
        for c in copies:
            c.wait()

    halo = swap(0, rw, rwl, rw, rwr)
    settle(loads)

    def first(x, c):
        val = cat([dbuf[t, pl.ds(x, LV, stride=X), :] for t in range(LT)])
        dt[x + 1] = val
        hi, lo = split(val)
        dhl[x, 0:LV, :] = hi
        dhl[x, LV:2 * LV, :] = lo
        q = jnp.dot(lm[...], dhl[x], preferred_element_type=F32)
        q1[x + 1] = q[0:112] + q[112:224]
        return c

    lax.fori_loop(0, X, first, 0)
    edges[0, 0:16, :] = q1[1, 32:48, :]
    edges[1, 0:16, :] = q1[X, 16:32, :]
    outer1 = swap(1, edges.at[1, pl.ds(0, 16)], from_left.at[pl.ds(0, 16)],
                  edges.at[0, pl.ds(0, 16)], from_right.at[pl.ds(0, 16)])

    def sum_first(x, c):
        mine[0, x] = stencil_moments(q1, x + 1)
        return c

    lax.fori_loop(0, X, sum_first, 0)
    settle(halo)

    def alpha_row(ref, x):
        return alpha_of(ref[pl.ds(x, 1), :], ref[pl.ds(x + X, 1), :])

    def products(i):
        hi, lo = split(at_[i + 1])
        ahl[i, 0:LV, :] = hi
        ahl[i, LV:2 * LV, :] = lo
        q = jnp.dot(lm[...], ahl[i], preferred_element_type=F32)
        q2[i] = q[0:112] + q[112:224]

    def second(j, c):
        x = lax.rem(X - j, X)
        val = stream_plane(dt, dhl, x + 1, x, ct, zmat, alpha_row(rw, x))
        for i in range(LT):
            at_[x + 2, :, 128 * i:128 * (i + 1)] = val[i]
        products(x + 1)
        return c

    lax.fori_loop(0, 2, second, 0)
    speed = ct[1]
    to_lower = jnp.where(speed > 0, 0.0, -speed)
    to_upper = jnp.where(speed > 0, speed, 0.0)
    al_l, al_r = alpha_row(rwl, X - 1), alpha_row(rwr, 0)
    for i in range(LT):
        c = slice(128 * i, 128 * (i + 1))
        at_[1, :, c] = to_lower * dt[1, :, c] * al_l[:, c]
        at_[X + 2, :, c] = to_upper * dt[X, :, c] * al_r[:, c]

    def ends(j, c):
        products((X + 1) * j)
        return c

    lax.fori_loop(0, 2, ends, 0)

    def third(i):
        val = stream_plane(at_, ahl, i + 1, i, ct, zmat)
        for t in range(LT):
            aa[i + 1, :, 128 * t:128 * (t + 1)] = val[t]

    def edge_third(j, c):
        third((X + 1) * j)
        return c

    lax.fori_loop(0, 2, edge_third, 0)
    for i in range(LT):
        c = slice(128 * i, 128 * (i + 1))
        aa[0, :, c] = to_lower * at_[1, :, c]
        aa[X + 3, :, c] = to_upper * at_[X + 2, :, c]

    settle(outer1)
    mine[0, 0] += from_left[0:16, :]
    mine[0, X - 1] += from_right[0:16, :]

    def pack(m):
        for x in range(X):
            pbuf[m, 13 * x:13 * x + 13, :] = mine[m, x, 0:13, :]

    def chunk_of(o):
        return (pl.ds(pl.multiple_of(CH * (o // LT), 8), CH), pl.ds(pl.multiple_of(128 * lax.rem(o, LT), 128), 128))

    def send_parts(m):
        def send(j, c):
            o = lax.rem(place + j, PEERS)
            r, k = chunk_of(o)
            pltpu.make_async_remote_copy(pbuf.at[m, r, k], rsbuf.at[m, j], s_rs.at[m], r_rs.at[m],
                                         device_id=peer(o), device_id_type=MESH).start()
            return c

        lax.fori_loop(1, PEERS, send, 0)

    def all_parts(m):
        return rsbuf.at[m, pl.ds(1, PEERS - 1)]

    def across(m):
        return pltpu.make_async_remote_copy(ssum.at[m], xbuf.at[m], s_x.at[m], r_x.at[m],
                                            device_id=partner, device_id_type=MESH)

    def own_sum(m):
        pltpu.make_async_copy(all_parts(m), all_parts(m), r_rs.at[m]).wait()
        r, k = chunk_of(place)
        acc = pbuf[m, r, k]
        for j in range(1, PEERS):
            acc = acc + rsbuf[m, j]
        ssum[m] = acc
        across(m).start()

    def send_total(m):
        across(m).wait()
        val = ssum[m] + xbuf[m]
        total[m] = val
        r, k = chunk_of(place)
        fbuf[m, r, k] = val

        def send(j, c):
            pltpu.make_async_remote_copy(total.at[m], fbuf.at[m, r, k], s_ag.at[m], r_ag.at[m],
                                         device_id=peer(lax.rem(place + j, PEERS)), device_id_type=MESH).start()
            return c

        lax.fori_loop(1, PEERS, send, 0)

    def all_totals(m):
        pltpu.make_async_copy(all_parts(m), all_parts(m), r_ag.at[m]).wait()

    def all_sent(m):
        pltpu.make_async_copy(all_parts(m), all_parts(m), s_rs.at[m]).wait()
        pltpu.make_async_copy(all_parts(m), all_parts(m), s_ag.at[m]).wait()

    pack(0)
    send_parts(0)
    edge_rows = [swap(4, aa.at[X + 2], aleft.at[0], aa.at[0], aright.at[0])]
    lax.fori_loop(2, 7, second, 0)
    own_sum(0)
    lax.fori_loop(7, X, second, 0)

    edges[0, 16:32, :] = stencil_edge(q2, 0) + q2[1, 32:48, :]
    edges[0, 32:48, :] = q2[0, 32:48, :]
    edges[1, 16:32, :] = stencil_edge(q2, X + 1) + q2[X, 16:32, :]
    edges[1, 32:48, :] = q2[X + 1, 16:32, :]
    outer2 = swap(2, edges.at[1, pl.ds(16, 32)], from_left.at[pl.ds(16, 32)],
                  edges.at[0, pl.ds(16, 32)], from_right.at[pl.ds(16, 32)])

    def sum_second(x, c):
        mine[1, x] = stencil_moments(q2, x + 1)
        return c

    lax.fori_loop(0, X, sum_second, 0)
    send_total(0)
    settle(outer2)
    mine[1, 0] += from_left[16:32, :]
    mine[1, 1] += from_left[32:48, :]
    mine[1, X - 1] += from_right[16:32, :]
    mine[1, X - 2] += from_right[32:48, :]
    pack(1)
    send_parts(1)
    edge_rows.append(swap(5, aa.at[X + 3], aleft.at[1], aa.at[1], aright.at[1]))

    def inner_third(i, c):
        third(i)
        return c

    lax.fori_loop(1, X + 1, inner_third, 0)
    own_sum(1)

    all_totals(0)
    l1[...] = jnp.dot(kx[...], fbuf[0, 0:104, :], precision=HIGHEST, preferred_element_type=F32)
    halo2 = swap(3, l1.at[pl.ds(0, 64)], h_left, l1.at[pl.ds(0, 64)], h_right)
    send_total(1)
    settle(halo2)

    zero8 = jnp.zeros((8, CELLS), F32)

    def clear_ends(k, c):
        for i in range(2):
            u[i, k, 0:8, :] = zero8
            u[i, k, 24:32, :] = zero8
        return c

    lax.fori_loop(0, 4, clear_ends, 0)

    def fill(k, lo_rows, own, hi_rows):
        b[k, 0:HALO, :] = lo_rows
        b[k, HALO:HALO + X, :] = own
        b[k, HALO + X:EXT, :] = hi_rows

    def smooth():
        def start(k, c):
            u[0, k, 8:24, :] = b[k]
            return c

        lax.fori_loop(0, 4, start, 0)
        for sweep in range(SWEEPS):
            src, dst = sweep % 2, 1 - sweep % 2

            def row(k, c):
                for blk in range(2):
                    lo = 8 + 8 * blk
                    here, ylo, yhi, zlo, zhi = yz_shifts(u[src, k, lo:lo + 8, :])
                    near = u[src, k, lo - 1:lo + 7, :] + u[src, k, lo + 1:lo + 9, :]
                    side = cat([(ylo[i] + yhi[i]) + (zlo[i] + zhi[i]) for i in range(LT)])
                    u[dst, k, lo:lo + 8, :] = (b[k, 8 * blk:8 * blk + 8, :] + coupling * (near + side)) * (1.0 / (1.0 + 6.0 * coupling))
                return c

            lax.fori_loop(0, 4, row, 0)
        return SWEEPS % 2

    for k in range(4):
        fill(k, h_left[8 * k + 4:8 * k + 8, :], l1[8 * k:8 * k + 8, :], h_right[8 * k:8 * k + 4, :])
    last = smooth()

    def gammas(relax, wall):
        return jnp.where(wall > 0, 0.0, relax), jnp.where(wall > 0, 1.0, relax)

    factors = [gammas(ref[0:X, :], ref[X:2 * X, :]) for ref in (rwl, rw, rwr)]
    for k in range(8):
        gl, go, gr = (f[1 if k in (3, 4) else 0] for f in factors)
        if k < 4:
            lo_rows = u[last, k, 8:8 + HALO, :]
            own = u[last, k, 8 + HALO:8 + HALO + X, :]
            hi_rows = u[last, k, 8 + HALO + X:8 + EXT, :]
        else:
            lo_rows = h_left[8 * k + 4:8 * k + 8, :]
            own = l1[8 * k:8 * k + 8, :]
            hi_rows = h_right[8 * k:8 * k + 4, :]
        own = own * go
        g1[EXT * k:EXT * k + HALO, :] = lo_rows * gl[4:8]
        g1[EXT * k + HALO:EXT * k + HALO + X, :] = own
        g1[EXT * k + HALO + X:EXT * (k + 1), :] = hi_rows * gr[0:4]
        _, ylo, yhi, zlo, zhi = yz_shifts(own)
        for j, val in enumerate((ylo, yhi, zlo, zhi)):
            rhs[64 * j + 8 * k:64 * j + 8 * k + 8, :] = cat(val)
    send_g1 = pltpu.make_async_copy(g1, g1_out, sem_out.at[0])
    send_g1.start()

    def squares(l, sm):
        acc = jnp.zeros((8, CELLS), F32)
        for i in range(9):
            d = l[64 + 8 * i:72 + 8 * i, :]
            acc = acc + d * d
        for k in range(4):
            d = u[sm, k, 8 + HALO:8 + HALO + X, :] - l[136 + 8 * k:144 + 8 * k, :]
            acc = acc + d * d
        parts = tiles(acc)
        out = parts[0]
        for i in range(1, LT):
            out = out + parts[i]
        return out

    nsend[0] = squares(l1, last)

    add[...] = (
        jnp.dot(nc[:, 0:128], g1[...], precision=HIGHEST, preferred_element_type=F32)
        + jnp.dot(nc[:, 128:384], rhs[...], precision=HIGHEST, preferred_element_type=F32)
    )
    all_totals(1)
    m2 = fbuf[1, 0:104, :] + add[...]
    b2out[...] = jnp.dot(kx[0:32, :], m2, precision=HIGHEST, preferred_element_type=F32)
    halo3 = swap(6, b2out, b2l, b2out, b2r)
    l2[...] = jnp.dot(kx[32:208, :], m2, precision=HIGHEST, preferred_element_type=F32)

    for c in edge_rows:
        settle(c)
    for i in range(2):
        aa[2 + i] += aleft[i]
    aa[X] += aright[0]
    aa[X + 1] += aright[1]
    send_a = pltpu.make_async_copy(aa.at[pl.ds(2, X)], a_out, sem_out.at[1])
    send_a.start()

    settle(halo3)
    for k in range(4):
        fill(k, b2l[8 * k + 4:8 * k + 8, :], b2out[8 * k:8 * k + 8, :], b2r[8 * k:8 * k + 4, :])
    last = smooth()
    acc = jnp.zeros((8, CELLS), F32)
    for i in range(9):
        d = l2[32 + 8 * i:40 + 8 * i, :]
        acc = acc + d * d
    for k in range(4):
        d = u[last, k, 8 + HALO:8 + HALO + X, :] - l2[104 + 8 * k:112 + 8 * k, :]
        acc = acc + d * d
    parts = tiles(acc)
    out = parts[0]
    for i in range(1, LT):
        out = out + parts[i]
    nsend[1] = out
    notes = []
    for j in (1, 2, 3):
        c = pltpu.make_async_remote_copy(nsend, nrecv.at[j - 1], s_nm.at[j - 1], r_nm.at[j - 1],
                                         device_id=(v, lax.rem(s + j, 4)), device_id_type=MESH)
        c.start()
        notes.append(c)

    beta, both = gammas(rw[0:X, :], rw[X:2 * X, :])
    for k in range(8):
        f = u[last, k, 8 + HALO:8 + HALO + X, :] if k < 4 else l2[8 * k - 32:8 * k - 24, :]
        g2_out[8 * k:8 * k + 8, :] = f * (both if k in (3, 4) else beta)

    tile = pl.ds(pl.multiple_of(128 * (v // 4), 128), 128)
    turn = lax.rem(128 - 32 * lax.rem(v, 4), 128)
    for r in range(MOM):
        if 1 <= r <= 4:
            f = u[last, r - 1, 8 + HALO:8 + HALO + X, tile]
        elif r == 0:
            f = l2[0:8, tile]
        elif r >= 10:
            f = l2[8 + 8 * (r - 10):16 + 8 * (r - 10), tile]
        else:
            f = l2[136 + 8 * (r - 5):144 + 8 * (r - 5), tile]
        mac_out[r] = pltpu.roll(f, turn, 1)[:, 0:32]

    settle(notes)
    for i in range(2):
        norm_out[i] = (nsend[i] + nrecv[0, i]) + (nrecv[1, i] + nrecv[2, i])
    send_g1.wait()
    send_a.wait()
    for m in range(2):
        all_sent(m)


def stencil_edge(q_ref, p):
    def rows(o):
        return tiles(q_ref[p, 16 * o:16 * o + 16, :])

    ylo, _ = y_shifts(rows(3))
    _, yhi = y_shifts(rows(4))
    zlo, _ = z_shifts(rows(5))
    _, zhi = z_shifts(rows(6))
    here = rows(0)
    return cat([here[i] + (ylo[i] + yhi[i]) + (zlo[i] + zhi[i]) for i in range(LT)])


PAIRS = 4


def renew(a_hbm, g1_ref, g2_ref, relax_ref, wall_ref, vel_ref, mac_ref, sum_ref, out_hbm, mac_out, norm_out,
          abuf, obuf, stage, rhs, lt, lrows, sem_in, sem_out):
    fetch = [
        pltpu.make_async_copy(a_hbm.at[:, :, pl.ds(256 * i, 256)], abuf.at[i], sem_in.at[i]) for i in range(PAIRS)
    ]
    for c in fetch:
        c.start()
    mac_out[...] = mac_ref[...]
    for i in range(2):
        norm_out[i] = jnp.sqrt(jnp.sum(sum_ref[i]))
    alpha = alpha_of(relax_ref[...], wall_ref[...])

    vel = speed_range * (2.0 * vel_ref[...].astype(F32) + 1.0 - NVX) / NVX
    _, target, stencil = functions_of(vel[0:1], vel[1:2], vel[2:3])
    for k in range(8):
        for o in range(7):
            lrows[8 * o + k:8 * o + k + 1, :] = stencil[o] * target[k]
        lrows[56 + k:57 + k, :] = target[k]
    hi, lo = split(lrows[...])
    hi, lo = hi.astype(F32), lo.astype(F32)
    lt[:, 0:128] = jnp.transpose(jnp.concatenate([hi, hi], 0)).astype(BF16)
    lt[:, 128:256] = jnp.transpose(jnp.concatenate([lo, lo], 0)).astype(BF16)

    for k in range(8):
        at = EXT * k + HALO
        here, ylo, yhi, zlo, zhi = yz_shifts(g1_ref[at:at + 8, :])
        before = g1_ref[at - 1:at + 7, :]
        after = g1_ref[at + 1:at + 9, :]
        for t in range(LT):
            cols = slice(128 * t, 128 * (t + 1))
            vals = (here[t], before[:, cols], after[:, cols], ylo[t], yhi[t], zlo[t], zhi[t])
            for o, val in enumerate(vals):
                stage[t, 64 * o + 8 * k:64 * o + 8 * k + 8, :] = val * alpha[:, cols]
            stage[t, 448 + 8 * k:456 + 8 * k, :] = g2_ref[8 * k:8 * k + 8, cols]

    def spread(x, c):
        for t in range(LT):
            hi, lo = split(stage[t, pl.ds(x, 64, stride=X), :])
            cols = slice(128 * t, 128 * (t + 1))
            rhs[x, 0:64, cols] = hi
            rhs[x, 64:128, cols] = lo
            rhs[x, 128:192, cols] = hi
            rhs[x, 192:256, cols] = lo
        return c

    lax.fori_loop(0, X, spread, 0)

    puts = []
    for i in range(PAIRS):
        fetch[i].wait()

        def plane(x, c):
            al = alpha_of(relax_ref[pl.ds(x, 1), 256 * i:256 * (i + 1)], wall_ref[pl.ds(x, 1), 256 * i:256 * (i + 1)])
            val = jnp.dot(lt[...], rhs[x, :, 256 * i:256 * (i + 1)], preferred_element_type=F32) + al * abuf[i, x]
            obuf[2 * i, pl.ds(x, LV, stride=X), :] = val[:, 0:128]
            obuf[2 * i + 1, pl.ds(x, LV, stride=X), :] = val[:, 128:256]
            return c

        lax.fori_loop(0, X, plane, 0)
        for t in (2 * i, 2 * i + 1):
            c = pltpu.make_async_copy(obuf.at[t], out_hbm.at[:, pl.ds(128 * t, 128)], sem_out.at[t])
            c.start()
            puts.append(c)
    for c in puts:
        c.wait()


def shards(consts, dist, vel_index, relax, wall_mask, macro_inverse):
    vmem = pl.BlockSpec(memory_space=pltpu.VMEM)
    hbm = pl.BlockSpec(memory_space=pl.ANY)
    smem = pl.BlockSpec(memory_space=pltpu.SMEM)
    dma = pltpu.SemaphoreType.DMA
    sds = jax.ShapeDtypeStruct
    a, g1, g2, mac, norm = pl.pallas_call(
        exchange,
        out_shape=(
            sds((X, LV, CELLS), F32), sds((8 * EXT, CELLS), F32), sds((64, CELLS), F32),
            sds((MOM, X, 32), F32), sds((2, 8, 128), F32),
        ),
        in_specs=[hbm] + [vmem] * 9,
        out_specs=(hbm, hbm, vmem, vmem, vmem),
        scratch_shapes=[
            pltpu.VMEM((LT, LV * X, 128), F32),
            pltpu.VMEM((X + 2, LV, CELLS), F32),
            pltpu.VMEM((X + 4, LV, CELLS), F32),
            pltpu.VMEM((X + 4, LV, CELLS), F32),
            pltpu.VMEM((X, 2 * LV, CELLS), BF16),
            pltpu.VMEM((X + 2, 2 * LV, CELLS), BF16),
            pltpu.VMEM((X + 2, 112, CELLS), F32),
            pltpu.VMEM((X + 2, 112, CELLS), F32),
            pltpu.VMEM((2, X, 16, CELLS), F32),
            pltpu.VMEM((2, 48, CELLS), F32),
            pltpu.VMEM((48, CELLS), F32),
            pltpu.VMEM((48, CELLS), F32),
            pltpu.VMEM((2 * X, CELLS), F32),
            pltpu.VMEM((2 * X, CELLS), F32),
            pltpu.VMEM((2 * X, CELLS), F32),
            pltpu.VMEM((16, LV), F32),
            pltpu.VMEM((224, 2 * LV), BF16),
            pltpu.VMEM((4, LV, LV), F32),
            pltpu.VMEM((2 * LV, 2 * LV), BF16),
            pltpu.VMEM((26 * X, X * MOM), F32),
            pltpu.VMEM((2, 2 * CH, CELLS), F32),
            pltpu.VMEM((2, PEERS, CH, 128), F32),
            pltpu.VMEM((2, CH, 128), F32),
            pltpu.VMEM((2, CH, 128), F32),
            pltpu.VMEM((2, CH, 128), F32),
            pltpu.VMEM((2, 2 * CH, CELLS), F32),
            pltpu.VMEM((26 * X, CELLS), F32),
            pltpu.VMEM((64, CELLS), F32),
            pltpu.VMEM((64, CELLS), F32),
            pltpu.VMEM((32, CELLS), F32),
            pltpu.VMEM((32, CELLS), F32),
            pltpu.VMEM((32, CELLS), F32),
            pltpu.VMEM((2, 4, 32, CELLS), F32),
            pltpu.VMEM((4, EXT, CELLS), F32),
            pltpu.VMEM((8 * EXT, CELLS), F32),
            pltpu.VMEM((256, CELLS), F32),
            pltpu.VMEM((X * MOM, CELLS), F32),
            pltpu.VMEM((22 * X, CELLS), F32),
            pltpu.VMEM((2, 8, 128), F32),
            pltpu.VMEM((3, 2, 8, 128), F32),
            pltpu.VMEM((2, LV, CELLS), F32),
            pltpu.VMEM((2, LV, CELLS), F32),
            dma((LT,)), dma((14,)), dma((14,)), dma((2,)), dma((2,)), dma((2,)), dma((2,)), dma((2,)), dma((2,)),
            dma((3,)), dma((3,)), dma((2,)),
        ],
        compiler_params=pltpu.CompilerParams(collective_id=0, has_side_effects=True, vmem_limit_bytes=60 * 2 ** 20),
        name="exchange",
    )(dist.reshape(LV * X, CELLS), relax, wall_mask, vel_index, macro_inverse, *consts)

    out, mac, norm = pl.pallas_call(
        renew,
        out_shape=(sds((LV * X, CELLS), F32), sds((MOM, X, 32), F32), sds((2,), F32)),
        in_specs=[hbm] + [vmem] * 7,
        out_specs=(hbm, vmem, smem),
        scratch_shapes=[
            pltpu.VMEM((PAIRS, X, LV, 256), F32),
            pltpu.VMEM((LT, LV * X, 128), F32),
            pltpu.VMEM((LT, 512, 128), F32),
            pltpu.VMEM((X, 256, CELLS), BF16),
            pltpu.VMEM((LV, 256), BF16),
            pltpu.VMEM((64, LV), F32),
            dma((PAIRS,)), dma((LT,)),
        ],
        compiler_params=pltpu.CompilerParams(vmem_limit_bytes=60 * 2 ** 20),
        name="renew",
    )(a, g1, g2, relax, wall_mask, vel_index, mac, norm)
    return (out.reshape(LV, X, CELLS), mac, norm)


def solution(mesh):
    consts = selection() + [coupling_table()]
    return jax.shard_map(
        lambda *args: shards([jnp.asarray(c) for c in consts], *args),
        mesh=mesh,
        in_specs=(P("vel", "space", None), P(None, "vel"), P("space", None), P("space", None), P()),
        out_specs=(P("vel", "space", None), P(None, "space", "vel"), P()),
        check_vma=False,
    )
```

```python
import functools
import math

import jax
import jax.numpy as jnp
import numpy as np
from jax import lax
from jax.experimental import pallas as pl
from jax.experimental.pallas import tpu as pltpu
from jax.sharding import PartitionSpec as P

NVX = 16
NZ = 16
MOM = 13
SWEEPS = 3
speed_range = 4.0
time_step = 0.08
coupling = 0.5

MESH = pl.DeviceIdType.MESH
F32 = jnp.float32
BF16 = jnp.bfloat16
X = 8
CELLS = 1024
LT = CELLS // 128
RING = 4
PEERS = RING * RING
LV = 128
CH = 56
HALO = 4
EXT = X + 2 * HALO
FIELD_ROWS = (1, 2, 3, 4, 0, 10, 11, 12)
OTHER_ROWS = (0, 5, 6, 7, 8, 9, 10, 11, 12)
HIGHEST = lax.Precision.HIGHEST


def functions_of(cx, cy, cz, xp=jnp):
    square = cx * cx + cy * cy + cz * cz
    weights = (2.0 * speed_range / NVX) ** 3 * math.pi ** (-1.5) * xp.exp(-square)
    heat = square - 2.5
    one = xp.ones_like(cx)
    rows = [
        one, cx, cy, cz, 2.0 * square / 3.0 - 1.0,
        2.0 * cx * cy, 2.0 * cx * cz, 2.0 * cy * cz,
        cx * cx - cy * cy, cy * cy - cz * cz,
        cx * heat, cy * heat, cz * heat,
    ]
    factor = 4.0 / 15.0
    target = [2.0 * cx, 2.0 * cy, 2.0 * cz, square - 1.5, one, factor * cx * heat, factor * cy * heat, factor * cz * heat]
    stencil = [1.0 - time_step * (xp.abs(cx) + xp.abs(cy) + xp.abs(cz))]
    for c in (cx, cy, cz):
        stencil += [time_step * xp.maximum(c, 0.0), time_step * xp.maximum(-c, 0.0)]
    return [r * weights for r in rows], target, stencil


def selection():
    sel = np.zeros((26, MOM))
    own = np.zeros((26, MOM))
    for j in range(26):
        if j < 8:
            sel[j, FIELD_ROWS[j]] = 1
        elif j < 17:
            sel[j, OTHER_ROWS[j - 8]] = 1
            own[j, OTHER_ROWS[j - 8]] = -1
        elif j < 21:
            own[j, j - 16] = 1
        else:
            sel[j, j - 16] = 1
    eye = np.eye(X)
    sel = np.repeat(sel, X, 0)
    spread = np.tile(np.eye(MOM), (1, X))
    mask = np.repeat(np.tile(eye, (26, 1)), MOM, 1)
    fixed = np.einsum("jr,xp->jxpr", own, eye).reshape(26 * X, X * MOM)
    return [a.astype(np.float32) for a in (sel, spread, mask, fixed)]


def coupling_table():
    line = speed_range * (2.0 * np.arange(NVX) + 1.0 - NVX) / NVX
    cx, cy, cz = (a.reshape(-1) for a in np.meshgrid(line, line, line, indexing="ij"))
    rows, target, stencil = functions_of(cx, cy, cz, np)
    n = np.einsum("rv,ov,kv->ork", rows, stencil, target)
    near = np.zeros((X, MOM, 8, EXT))
    side = np.zeros((X, MOM, 4, 8, X))
    for x in range(X):
        near[x, :, :, x + HALO] += n[0]
        near[x, :, :, x + HALO - 1] += n[1]
        near[x, :, :, x + HALO + 1] += n[2]
        for j in range(4):
            side[x, :, j, :, x] += n[3 + j]
    table = np.concatenate([near.reshape(X * MOM, 8 * EXT), side.reshape(X * MOM, 32 * X)], 1)
    return table.astype(np.float32)


def split(a):
    hi = a.astype(BF16)
    return hi, (a - hi.astype(F32)).astype(BF16)


def cat(parts):
    return jnp.concatenate(parts, axis=1)


def tiles(x):
    return [x[:, 128 * i:128 * (i + 1)] for i in range(LT)]


def y_shifts(t):
    lane = lax.broadcasted_iota(jnp.int32, t[0].shape, 1)
    up = [pltpu.roll(a, 16, 1) for a in t]
    down = [pltpu.roll(a, 112, 1) for a in t]
    ylo = [jnp.where(lane < 16, up[i - 1], up[i]) for i in range(LT)]
    yhi = [jnp.where(lane >= 112, down[(i + 1) % LT], down[i]) for i in range(LT)]
    return ylo, yhi


def z_shifts(t):
    z = lax.broadcasted_iota(jnp.int32, t[0].shape, 1) % NZ
    zlo = [jnp.where(z == 0, pltpu.roll(a, 113, 1), pltpu.roll(a, 1, 1)) for a in t]
    zhi = [jnp.where(z == NZ - 1, pltpu.roll(a, 15, 1), pltpu.roll(a, 127, 1)) for a in t]
    return zlo, zhi


def yz_shifts(x):
    t = tiles(x)
    return (t,) + y_shifts(t) + z_shifts(t)


def stencil_moments(q_ref, p):
    def rows(o, at=p):
        return tiles(q_ref[at, 16 * o:16 * o + 16, :])

    ylo, _ = y_shifts(rows(3))
    _, yhi = y_shifts(rows(4))
    zlo, _ = z_shifts(rows(5))
    _, zhi = z_shifts(rows(6))
    here, before, after = rows(0), rows(1, p - 1), rows(2, p + 1)
    return cat([(here[i] + before[i] + after[i]) + (ylo[i] + yhi[i]) + (zlo[i] + zhi[i]) for i in range(LT)])


def alpha_of(relax, wall):
    return jnp.where(wall > 0, 0.0, 1.0 - relax)


def stream_plane(src, halves, p, h, ct, zmat, zsel, put, scale=None):
    pz = ct[3] > 0
    for i in range(LT):
        c = slice(128 * i, 128 * (i + 1))
        z = jnp.dot(cat([halves[h, 0:LV, c], halves[h, LV:2 * LV, c]]), zmat[...], preferred_element_type=F32)
        zsel[:, c] = jnp.where(pz, z[:, 0:128], z[:, 128:256])

    def group(g, carry):
        at = pl.ds(pl.multiple_of(8 * g, 8), 8)
        lane = lax.broadcasted_iota(jnp.int32, (8, 128), 1)
        k0, cx, cy, cz = (ct[i, at, :] for i in range(4))
        px, py = cx > 0, cy > 0
        kx, ky, kz = jnp.abs(cx), jnp.abs(cy), jnp.abs(cz)
        t = [src[p, at, 128 * i:128 * (i + 1)] for i in range(LT)]
        up = [pltpu.roll(a, 16, 1) for a in t]
        down = [pltpu.roll(a, 112, 1) for a in t]
        for i in range(LT):
            c = slice(128 * i, 128 * (i + 1))
            in_x = jnp.where(px, src[p - 1, at, c], src[p + 1, at, c])
            in_y = jnp.where(
                py,
                jnp.where(lane < 16, up[i - 1], up[i]),
                jnp.where(lane >= 112, down[(i + 1) % LT], down[i]),
            )
            val = (k0 * t[i] + kx * in_x) + (ky * in_y + kz * zsel[at, c])
            put(at, c, val if scale is None else val * scale[:, c])
        return carry

    lax.fori_loop(0, LV // 8, group, 0, unroll=4)


def exchange(dist_hbm, relax_ref, wall_ref, vel_ref, inv_ref, sel_ref, spread_ref, mask_ref, fixed_ref, nc,
             aa, g1, g2_out, mac_out, norm_out,
             dbuf, dt, at_, zsel, dhl, ahl, q1, q2, mine, edges, from_left, from_right, rw, rwl, rwr,
             mrows, lm, ct, zmat, kx, pbuf, rsbuf, ssum, xbuf, total, fbuf, l1, h_left, h_right, b2out, b2l, b2r,
             u, b, rhs, add, l2, nsend, nrecv, cin, cout, cfar, cboth, cnear,
             sem_ld, s_nb, r_nb, s_rs, r_rs, s_ag, r_ag, s_x, r_x, s_nm, r_nm, s_e, r_e):
    v = lax.axis_index("vel")
    s = lax.axis_index("space")
    left = (v, lax.rem(s + 3, 4))
    right = (v, lax.rem(s + 1, 4))
    far = v // PEERS
    place = lax.rem(v, PEERS)
    partner = ((1 - far) * PEERS + place, s)

    def peer(o):
        return (far * PEERS + o, s)

    loads = [pltpu.make_async_copy(dist_hbm.at[:, pl.ds(128 * t, 128)], dbuf.at[t], sem_ld.at[t]) for t in range(LT)]
    for c in loads:
        c.start()

    barrier = pltpu.get_barrier_semaphore()

    def greet(j, c):
        pl.semaphore_signal(barrier, inc=1, device_id=peer(lax.rem(place + j, PEERS)), device_id_type=MESH)
        return c

    lax.fori_loop(1, PEERS, greet, 0)
    pl.semaphore_signal(barrier, inc=1, device_id=partner, device_id_type=MESH)
    for j in (1, 2, 3):
        pl.semaphore_signal(barrier, inc=1, device_id=(v, lax.rem(s + j, 4)), device_id_type=MESH)

    rw[0:X, :] = relax_ref[...]
    rw[X:2 * X, :] = wall_ref[...].astype(F32)
    vel = speed_range * (2.0 * vel_ref[...].astype(F32) + 1.0 - NVX) / NVX
    cx, cy, cz = vel[0:1], vel[1:2], vel[2:3]
    rows, _, stencil = functions_of(cx, cy, cz)
    mrows[...] = jnp.zeros_like(mrows)
    for r in range(MOM):
        mrows[r:r + 1, :] = rows[r]
    for o in range(7):
        hi, lo = split(mrows[...] * stencil[o])
        lm[16 * o:16 * o + 16, 0:LV] = hi
        lm[16 * o:16 * o + 16, LV:2 * LV] = hi
        lm[112 + 16 * o:128 + 16 * o, 0:LV] = lo
        lm[112 + 16 * o:128 + 16 * o, LV:2 * LV] = jnp.zeros_like(lo)
    for i, row in enumerate((stencil[0], time_step * cx, time_step * cy, time_step * cz)):
        ct[i] = jnp.transpose(jnp.broadcast_to(row, (LV, LV)))
    src_lane = lax.broadcasted_iota(jnp.int32, (LV, LV), 0)
    dst_lane = lax.broadcasted_iota(jnp.int32, (LV, LV), 1)
    dst_z = dst_lane % NZ
    lower = jnp.where(src_lane == jnp.where(dst_z == 0, dst_lane + NZ - 1, dst_lane - 1), 1.0, 0.0).astype(BF16)
    upper = jnp.where(src_lane == jnp.where(dst_z == NZ - 1, dst_lane - NZ + 1, dst_lane + 1), 1.0, 0.0).astype(BF16)
    for i in range(2):
        zmat[LV * i:LV * (i + 1), 0:LV] = lower
        zmat[LV * i:LV * (i + 1), LV:2 * LV] = upper
    part = jnp.dot(sel_ref[...], inv_ref[...], precision=HIGHEST, preferred_element_type=F32)
    part = jnp.dot(part, spread_ref[...], precision=HIGHEST, preferred_element_type=F32)
    kx[...] = part * mask_ref[...] + fixed_ref[...]
    zero_plane = jnp.zeros((LV, CELLS), F32)
    for p in (0, 9):
        dt[p] = zero_plane
        q1[p, 16:48, :] = jnp.zeros((32, CELLS), F32)
    for p in (0, 11):
        at_[p] = zero_plane
    for m in range(2):
        pbuf[m, 104:112, :] = jnp.zeros((8, CELLS), F32)

    def swap(i, to_right, right_dst, to_left, left_dst):
        a = pltpu.make_async_remote_copy(to_right, right_dst, s_nb.at[2 * i], r_nb.at[2 * i],
                                         device_id=right, device_id_type=MESH)
        c = pltpu.make_async_remote_copy(to_left, left_dst, s_nb.at[2 * i + 1], r_nb.at[2 * i + 1],
                                         device_id=left, device_id_type=MESH)
        a.start()
        c.start()
        return a, c

    def settle(copies):
        for c in copies:
            c.wait()

    settle(loads)

    def first(x, c):
        val = cat([dbuf[t, pl.ds(x, LV, stride=X), :] for t in range(LT)])
        dt[x + 1] = val
        hi, lo = split(val)
        dhl[x, 0:LV, :] = hi
        dhl[x, LV:2 * LV, :] = lo
        q = jnp.dot(lm[...], dhl[x], preferred_element_type=F32)
        q1[x + 1] = q[0:112] + q[112:224]
        return c

    lax.fori_loop(0, X, first, 0)
    pl.semaphore_wait(barrier, PEERS - 1 + 1 + 3)
    halo = swap(0, rw, rwl, rw, rwr)
    edges[0, 0:16, :] = q1[1, 32:48, :]
    edges[1, 0:16, :] = q1[X, 16:32, :]
    outer1 = swap(1, edges.at[1, pl.ds(0, 16)], from_left.at[pl.ds(0, 16)],
                  edges.at[0, pl.ds(0, 16)], from_right.at[pl.ds(0, 16)])

    def sum_first(x, c):
        mine[0, x] = stencil_moments(q1, x + 1)
        return c

    lax.fori_loop(0, X, sum_first, 0)

    def alpha_row(ref, x):
        return alpha_of(ref[pl.ds(x, 1), :], ref[pl.ds(x + X, 1), :])

    def products(i):
        hi, lo = split(at_[i + 1])
        ahl[i, 0:LV, :] = hi
        ahl[i, LV:2 * LV, :] = lo
        q = jnp.dot(lm[...], ahl[i], preferred_element_type=F32)
        q2[i] = q[0:112] + q[112:224]

    def second(j, c):
        x = lax.rem(X - j, X)

        def put(at, c, val):
            at_[x + 2, at, c] = val

        stream_plane(dt, dhl, x + 1, x, ct, zmat, zsel, put, alpha_row(rw, x))
        products(x + 1)
        return c

    def third(i):
        def put(at, c, val):
            aa[i + 1, at, c] = val

        stream_plane(at_, ahl, i + 1, i, ct, zmat, zsel, put)

    lax.fori_loop(0, 2, second, 0)
    settle(outer1)
    mine[0, 0] += from_left[0:16, :]
    mine[0, X - 1] += from_right[0:16, :]

    def pack(m):
        for x in range(X):
            pbuf[m, 13 * x:13 * x + 13, :] = mine[m, x, 0:13, :]

    def chunk_of(o):
        return (pl.ds(pl.multiple_of(CH * (o // LT), 8), CH), pl.ds(pl.multiple_of(128 * lax.rem(o, LT), 128), 128))

    def send_parts(m):
        def send(j, c):
            o = lax.rem(place + j, PEERS)
            r, k = chunk_of(o)
            pltpu.make_async_remote_copy(pbuf.at[m, r, k], rsbuf.at[m, j], s_rs.at[m], r_rs.at[m],
                                         device_id=peer(o), device_id_type=MESH).start()
            return c

        lax.fori_loop(1, PEERS, send, 0)

    def all_parts(m):
        return rsbuf.at[m, pl.ds(1, PEERS - 1)]

    def across(m):
        return pltpu.make_async_remote_copy(ssum.at[m], xbuf.at[m], s_x.at[m], r_x.at[m],
                                            device_id=partner, device_id_type=MESH)

    def own_sum(m):
        pltpu.make_async_copy(all_parts(m), all_parts(m), r_rs.at[m]).wait()
        r, k = chunk_of(place)
        acc = pbuf[m, r, k]
        for j in range(1, PEERS):
            acc = acc + rsbuf[m, j]
        ssum[m] = acc
        across(m).start()

    def send_total(m):
        across(m).wait()
        val = ssum[m] + xbuf[m]
        total[m] = val
        r, k = chunk_of(place)
        fbuf[m, r, k] = val

        def send(j, c):
            pltpu.make_async_remote_copy(total.at[m], fbuf.at[m, r, k], s_ag.at[m], r_ag.at[m],
                                         device_id=peer(lax.rem(place + j, PEERS)), device_id_type=MESH).start()
            return c

        lax.fori_loop(1, PEERS, send, 0)

    def all_totals(m):
        pltpu.make_async_copy(all_parts(m), all_parts(m), r_ag.at[m]).wait()

    def all_sent(m):
        pltpu.make_async_copy(all_parts(m), all_parts(m), s_rs.at[m]).wait()
        pltpu.make_async_copy(all_parts(m), all_parts(m), s_ag.at[m]).wait()

    pack(0)
    send_parts(0)
    lax.fori_loop(2, 7, second, 0)
    own_sum(0)
    lax.fori_loop(7, X, second, 0)

    settle(halo)
    speed = ct[1]
    to_lower = jnp.where(speed > 0, 0.0, -speed)
    to_upper = jnp.where(speed > 0, speed, 0.0)
    al_l, al_r = alpha_row(rwl, X - 1), alpha_row(rwr, 0)
    for i in range(LT):
        c = slice(128 * i, 128 * (i + 1))
        at_[1, :, c] = to_lower * dt[1, :, c] * al_l[:, c]
        at_[X + 2, :, c] = to_upper * dt[X, :, c] * al_r[:, c]

    def ends(j, c):
        products((X + 1) * j)
        return c

    lax.fori_loop(0, 2, ends, 0)

    edges[0, 16:32, :] = stencil_edge(q2, 0) + q2[1, 32:48, :]
    edges[0, 32:48, :] = q2[0, 32:48, :]
    edges[1, 16:32, :] = stencil_edge(q2, X + 1) + q2[X, 16:32, :]
    edges[1, 32:48, :] = q2[X + 1, 16:32, :]
    outer2 = swap(2, edges.at[1, pl.ds(16, 32)], from_left.at[pl.ds(16, 32)],
                  edges.at[0, pl.ds(16, 32)], from_right.at[pl.ds(16, 32)])

    def sum_second(x, c):
        mine[1, x] = stencil_moments(q2, x + 1)
        return c

    lax.fori_loop(0, X, sum_second, 0)
    send_total(0)

    def edge_third(j, c):
        third((X + 1) * j)
        return c

    lax.fori_loop(0, 2, edge_third, 0)
    for i in range(LT):
        c = slice(128 * i, 128 * (i + 1))
        aa[0, :, c] = to_lower * at_[1, :, c]
        aa[X + 3, :, c] = to_upper * at_[X + 2, :, c]
    settle(outer2)
    mine[1, 0] += from_left[16:32, :]
    mine[1, 1] += from_left[32:48, :]
    mine[1, X - 1] += from_right[16:32, :]
    mine[1, X - 2] += from_right[32:48, :]
    pack(1)
    send_parts(1)

    core = lax.rem(s, 2)
    mate = (v, s + 1 - 2 * core)
    over = (v, lax.rem(s + 2, 4))
    half = LV // 2
    mine_v = pl.ds(pl.multiple_of(half * core, 8), half)
    mate_v = pl.ds(pl.multiple_of(half * (1 - core), 8), half)
    out_end = pl.ds((X + 2) * core, 2)
    in_end = pl.ds((X + 2) * (1 - core), 2)

    def hand(i, src, dst, to):
        c = pltpu.make_async_remote_copy(src, dst, s_e.at[i], r_e.at[i], device_id=to, device_id_type=MESH)
        c.start()
        return c

    give = hand(0, aa.at[out_end, mate_v], cin, mate)
    near = hand(1, aa.at[in_end], cnear, mate)

    def inner_third(i, c):
        third(i)
        return c

    lax.fori_loop(1, 3, inner_third, 0)
    give.wait()
    cout[...] = aa[out_end, mine_v, :] + cin[...]
    across_x = hand(2, cout, cfar, over)
    lax.fori_loop(3, X + 1, inner_third, 0)
    own_sum(1)

    all_totals(0)
    l1[...] = jnp.dot(kx[...], fbuf[0, 0:104, :], precision=HIGHEST, preferred_element_type=F32)
    halo2 = swap(3, l1.at[pl.ds(0, 64)], h_left, l1.at[pl.ds(0, 64)], h_right)
    send_total(1)
    across_x.wait()
    share = hand(3, cfar, cboth, mate)
    settle(halo2)

    zero8 = jnp.zeros((8, CELLS), F32)

    def clear_ends(k, c):
        for i in range(2):
            u[i, k, 0:8, :] = zero8
            u[i, k, 24:32, :] = zero8
        return c

    lax.fori_loop(0, 4, clear_ends, 0)

    def fill(k, lo_rows, own, hi_rows):
        b[k, 0:HALO, :] = lo_rows
        b[k, HALO:HALO + X, :] = own
        b[k, HALO + X:EXT, :] = hi_rows

    def smooth():
        def start(k, c):
            u[0, k, 8:24, :] = b[k]
            return c

        lax.fori_loop(0, 4, start, 0)
        for sweep in range(SWEEPS):
            src, dst = sweep % 2, 1 - sweep % 2

            def row(k, c):
                for blk in range(2):
                    lo = 8 + 8 * blk
                    here, ylo, yhi, zlo, zhi = yz_shifts(u[src, k, lo:lo + 8, :])
                    near = u[src, k, lo - 1:lo + 7, :] + u[src, k, lo + 1:lo + 9, :]
                    side = cat([(ylo[i] + yhi[i]) + (zlo[i] + zhi[i]) for i in range(LT)])
                    u[dst, k, lo:lo + 8, :] = (b[k, 8 * blk:8 * blk + 8, :] + coupling * (near + side)) * (1.0 / (1.0 + 6.0 * coupling))
                return c

            lax.fori_loop(0, 4, row, 0)
        return SWEEPS % 2

    for k in range(4):
        fill(k, h_left[8 * k + 4:8 * k + 8, :], l1[8 * k:8 * k + 8, :], h_right[8 * k:8 * k + 4, :])
    last = smooth()

    def gammas(relax, wall):
        return jnp.where(wall > 0, 0.0, relax), jnp.where(wall > 0, 1.0, relax)

    factors = [gammas(ref[0:X, :], ref[X:2 * X, :]) for ref in (rwl, rw, rwr)]
    for k in range(8):
        gl, go, gr = (f[1 if k in (3, 4) else 0] for f in factors)
        if k < 4:
            lo_rows = u[last, k, 8:8 + HALO, :]
            own = u[last, k, 8 + HALO:8 + HALO + X, :]
            hi_rows = u[last, k, 8 + HALO + X:8 + EXT, :]
        else:
            lo_rows = h_left[8 * k + 4:8 * k + 8, :]
            own = l1[8 * k:8 * k + 8, :]
            hi_rows = h_right[8 * k:8 * k + 4, :]
        own = own * go
        g1[EXT * k:EXT * k + HALO, :] = lo_rows * gl[4:8]
        g1[EXT * k + HALO:EXT * k + HALO + X, :] = own
        g1[EXT * k + HALO + X:EXT * (k + 1), :] = hi_rows * gr[0:4]
        _, ylo, yhi, zlo, zhi = yz_shifts(own)
        for j, val in enumerate((ylo, yhi, zlo, zhi)):
            rhs[64 * j + 8 * k:64 * j + 8 * k + 8, :] = cat(val)

    def squares(l, sm):
        acc = jnp.zeros((8, CELLS), F32)
        for i in range(9):
            d = l[64 + 8 * i:72 + 8 * i, :]
            acc = acc + d * d
        for k in range(4):
            d = u[sm, k, 8 + HALO:8 + HALO + X, :] - l[136 + 8 * k:144 + 8 * k, :]
            acc = acc + d * d
        parts = tiles(acc)
        out = parts[0]
        for i in range(1, LT):
            out = out + parts[i]
        return out

    nsend[0] = squares(l1, last)

    add[...] = (
        jnp.dot(nc[:, 0:128], g1[...], precision=HIGHEST, preferred_element_type=F32)
        + jnp.dot(nc[:, 128:384], rhs[...], precision=HIGHEST, preferred_element_type=F32)
    )
    all_totals(1)
    m2 = fbuf[1, 0:104, :] + add[...]
    b2out[...] = jnp.dot(kx[0:32, :], m2, precision=HIGHEST, preferred_element_type=F32)
    halo3 = swap(6, b2out, b2l, b2out, b2r)
    l2[...] = jnp.dot(kx[32:208, :], m2, precision=HIGHEST, preferred_element_type=F32)

    near.wait()
    share.wait()
    is_upper = (core == 0).astype(F32)
    from_far = 2 + (X - 2) * core
    from_near = 2 + (X - 2) * (1 - core)

    def add_ends(i, carry):
        for t in range(LT):
            c = slice(128 * t, 128 * (t + 1))
            aa[from_near + i, :, c] += cnear[i, :, c]
            aa[from_far + i, mine_v, c] += jnp.where(wanted_of(mine_v) > 0, cfar[i, :, c], 0.0)
            aa[from_far + i, mate_v, c] += jnp.where(wanted_of(mate_v) > 0, cboth[i, :, c], 0.0)
        return carry

    def wanted_of(rows):
        towards = ct[1, rows, :]
        return jnp.where(towards > 0, is_upper, 1.0 - is_upper)

    lax.fori_loop(0, 2, add_ends, 0)

    settle(halo3)
    for k in range(4):
        fill(k, b2l[8 * k + 4:8 * k + 8, :], b2out[8 * k:8 * k + 8, :], b2r[8 * k:8 * k + 4, :])
    last = smooth()
    acc = jnp.zeros((8, CELLS), F32)
    for i in range(9):
        d = l2[32 + 8 * i:40 + 8 * i, :]
        acc = acc + d * d
    for k in range(4):
        d = u[last, k, 8 + HALO:8 + HALO + X, :] - l2[104 + 8 * k:112 + 8 * k, :]
        acc = acc + d * d
    parts = tiles(acc)
    out = parts[0]
    for i in range(1, LT):
        out = out + parts[i]
    nsend[1] = out
    notes = []
    for j in (1, 2, 3):
        c = pltpu.make_async_remote_copy(nsend, nrecv.at[j - 1], s_nm.at[j - 1], r_nm.at[j - 1],
                                         device_id=(v, lax.rem(s + j, 4)), device_id_type=MESH)
        c.start()
        notes.append(c)

    beta, both = gammas(rw[0:X, :], rw[X:2 * X, :])
    for k in range(8):
        f = u[last, k, 8 + HALO:8 + HALO + X, :] if k < 4 else l2[8 * k - 32:8 * k - 24, :]
        g2_out[8 * k:8 * k + 8, :] = f * (both if k in (3, 4) else beta)

    tile = pl.ds(pl.multiple_of(128 * (v // 4), 128), 128)
    turn = lax.rem(128 - 32 * lax.rem(v, 4), 128)
    for r in range(MOM):
        if 1 <= r <= 4:
            f = u[last, r - 1, 8 + HALO:8 + HALO + X, tile]
        elif r == 0:
            f = l2[0:8, tile]
        elif r >= 10:
            f = l2[8 + 8 * (r - 10):16 + 8 * (r - 10), tile]
        else:
            f = l2[136 + 8 * (r - 5):144 + 8 * (r - 5), tile]
        mac_out[r] = pltpu.roll(f, turn, 1)[:, 0:32]

    settle(notes)
    for i in range(2):
        norm_out[i] = (nsend[i] + nrecv[0, i]) + (nrecv[1, i] + nrecv[2, i])
    for m in range(2):
        all_sent(m)


def stencil_edge(q_ref, p):
    def rows(o):
        return tiles(q_ref[p, 16 * o:16 * o + 16, :])

    ylo, _ = y_shifts(rows(3))
    _, yhi = y_shifts(rows(4))
    zlo, _ = z_shifts(rows(5))
    _, zhi = z_shifts(rows(6))
    here = rows(0)
    return cat([here[i] + (ylo[i] + yhi[i]) + (zlo[i] + zhi[i]) for i in range(LT)])


PAIRS = 4


def renew(a_ref, g1_ref, g2_ref, relax_ref, wall_ref, vel_ref, mac_ref, sum_ref, out_hbm, mac_out, norm_out,
          obuf, stage, rhs, lt, lrows, sem_out):
    mac_out[...] = mac_ref[...]
    for i in range(2):
        norm_out[i] = jnp.sqrt(jnp.sum(sum_ref[i]))
    alpha = alpha_of(relax_ref[...], wall_ref[...])

    vel = speed_range * (2.0 * vel_ref[...].astype(F32) + 1.0 - NVX) / NVX
    _, target, stencil = functions_of(vel[0:1], vel[1:2], vel[2:3])
    for k in range(8):
        for o in range(7):
            lrows[8 * o + k:8 * o + k + 1, :] = stencil[o] * target[k]
        lrows[56 + k:57 + k, :] = target[k]
    hi, lo = split(lrows[...])
    hi, lo = hi.astype(F32), lo.astype(F32)
    lt[:, 0:128] = jnp.transpose(jnp.concatenate([hi, hi], 0)).astype(BF16)
    lt[:, 128:256] = jnp.transpose(jnp.concatenate([lo, lo], 0)).astype(BF16)

    for k in range(8):
        at = EXT * k + HALO
        here, ylo, yhi, zlo, zhi = yz_shifts(g1_ref[at:at + 8, :])
        before = g1_ref[at - 1:at + 7, :]
        after = g1_ref[at + 1:at + 9, :]
        for t in range(LT):
            cols = slice(128 * t, 128 * (t + 1))
            vals = (here[t], before[:, cols], after[:, cols], ylo[t], yhi[t], zlo[t], zhi[t])
            for o, val in enumerate(vals):
                stage[t, 64 * o + 8 * k:64 * o + 8 * k + 8, :] = val * alpha[:, cols]
            stage[t, 448 + 8 * k:456 + 8 * k, :] = g2_ref[8 * k:8 * k + 8, cols]

    def spread(x, c):
        for t in range(LT):
            hi, lo = split(stage[t, pl.ds(x, 64, stride=X), :])
            cols = slice(128 * t, 128 * (t + 1))
            rhs[x, 0:64, cols] = hi
            rhs[x, 64:128, cols] = lo
            rhs[x, 128:192, cols] = hi
            rhs[x, 192:256, cols] = lo
        return c

    lax.fori_loop(0, X, spread, 0)

    puts = []
    for i in range(PAIRS):
        def plane(x, c):
            al = alpha_of(relax_ref[pl.ds(x, 1), 256 * i:256 * (i + 1)], wall_ref[pl.ds(x, 1), 256 * i:256 * (i + 1)])
            val = jnp.dot(lt[...], rhs[x, :, 256 * i:256 * (i + 1)], preferred_element_type=F32) + al * a_ref[x + 2, :, 256 * i:256 * (i + 1)]
            obuf[2 * i, pl.ds(x, LV, stride=X), :] = val[:, 0:128]
            obuf[2 * i + 1, pl.ds(x, LV, stride=X), :] = val[:, 128:256]
            return c

        lax.fori_loop(0, X, plane, 0)
        for t in (2 * i, 2 * i + 1):
            c = pltpu.make_async_copy(obuf.at[t], out_hbm.at[:, pl.ds(128 * t, 128)], sem_out.at[t])
            c.start()
            puts.append(c)
    for c in puts:
        c.wait()


def shards(consts, dist, vel_index, relax, wall_mask, macro_inverse):
    vmem = pl.BlockSpec(memory_space=pltpu.VMEM)
    hbm = pl.BlockSpec(memory_space=pl.ANY)
    smem = pl.BlockSpec(memory_space=pltpu.SMEM)
    dma = pltpu.SemaphoreType.DMA
    sds = jax.ShapeDtypeStruct
    a, g1, g2, mac, norm = pl.pallas_call(
        exchange,
        out_shape=(
            pltpu.VMEM((X + 4, LV, CELLS), F32), pltpu.VMEM((8 * EXT, CELLS), F32), pltpu.VMEM((64, CELLS), F32),
            pltpu.VMEM((MOM, X, 32), F32), pltpu.VMEM((2, 8, 128), F32),
        ),
        in_specs=[hbm] + [vmem] * 9,
        out_specs=(vmem,) * 5,
        scratch_shapes=[
            pltpu.VMEM((LT, LV * X, 128), F32),
            pltpu.VMEM((X + 2, LV, CELLS), F32),
            pltpu.VMEM((X + 4, LV, CELLS), F32),
            pltpu.VMEM((LV, CELLS), F32),
            pltpu.VMEM((X, 2 * LV, CELLS), BF16),
            pltpu.VMEM((X + 2, 2 * LV, CELLS), BF16),
            pltpu.VMEM((X + 2, 112, CELLS), F32),
            pltpu.VMEM((X + 2, 112, CELLS), F32),
            pltpu.VMEM((2, X, 16, CELLS), F32),
            pltpu.VMEM((2, 48, CELLS), F32),
            pltpu.VMEM((48, CELLS), F32),
            pltpu.VMEM((48, CELLS), F32),
            pltpu.VMEM((2 * X, CELLS), F32),
            pltpu.VMEM((2 * X, CELLS), F32),
            pltpu.VMEM((2 * X, CELLS), F32),
            pltpu.VMEM((16, LV), F32),
            pltpu.VMEM((224, 2 * LV), BF16),
            pltpu.VMEM((4, LV, LV), F32),
            pltpu.VMEM((2 * LV, 2 * LV), BF16),
            pltpu.VMEM((26 * X, X * MOM), F32),
            pltpu.VMEM((2, 2 * CH, CELLS), F32),
            pltpu.VMEM((2, PEERS, CH, 128), F32),
            pltpu.VMEM((2, CH, 128), F32),
            pltpu.VMEM((2, CH, 128), F32),
            pltpu.VMEM((2, CH, 128), F32),
            pltpu.VMEM((2, 2 * CH, CELLS), F32),
            pltpu.VMEM((26 * X, CELLS), F32),
            pltpu.VMEM((64, CELLS), F32),
            pltpu.VMEM((64, CELLS), F32),
            pltpu.VMEM((32, CELLS), F32),
            pltpu.VMEM((32, CELLS), F32),
            pltpu.VMEM((32, CELLS), F32),
            pltpu.VMEM((2, 4, 32, CELLS), F32),
            pltpu.VMEM((4, EXT, CELLS), F32),
            pltpu.VMEM((256, CELLS), F32),
            pltpu.VMEM((X * MOM, CELLS), F32),
            pltpu.VMEM((22 * X, CELLS), F32),
            pltpu.VMEM((2, 8, 128), F32),
            pltpu.VMEM((3, 2, 8, 128), F32),
            pltpu.VMEM((2, LV // 2, CELLS), F32),
            pltpu.VMEM((2, LV // 2, CELLS), F32),
            pltpu.VMEM((2, LV // 2, CELLS), F32),
            pltpu.VMEM((2, LV // 2, CELLS), F32),
            pltpu.VMEM((2, LV, CELLS), F32),
            dma((LT,)), dma((14,)), dma((14,)), dma((2,)), dma((2,)), dma((2,)), dma((2,)), dma((2,)), dma((2,)),
            dma((3,)), dma((3,)), dma((4,)), dma((4,)),
        ],
        compiler_params=pltpu.CompilerParams(collective_id=0, has_side_effects=True, vmem_limit_bytes=54 * 2 ** 20),
        name="exchange",
    )(dist.reshape(LV * X, CELLS), relax, wall_mask, vel_index, macro_inverse, *consts)

    out, mac, norm = pl.pallas_call(
        renew,
        out_shape=(sds((LV * X, CELLS), F32), sds((MOM, X, 32), F32), sds((2,), F32)),
        in_specs=[vmem] * 8,
        out_specs=(hbm, vmem, smem),
        scratch_shapes=[
            pltpu.VMEM((LT, LV * X, 128), F32),
            pltpu.VMEM((LT, 512, 128), F32),
            pltpu.VMEM((X, 256, CELLS), BF16),
            pltpu.VMEM((LV, 256), BF16),
            pltpu.VMEM((64, LV), F32),
            dma((LT,)),
        ],
        compiler_params=pltpu.CompilerParams(vmem_limit_bytes=32 * 2 ** 20),
        name="renew",
    )(a, g1, g2, relax, wall_mask, vel_index, mac, norm)
    return (out.reshape(LV, X, CELLS), mac, norm)


def solution(mesh):
    consts = selection() + [coupling_table()]
    return jax.shard_map(
        lambda *args: shards([jnp.asarray(c) for c in consts], *args),
        mesh=mesh,
        in_specs=(P("vel", "space", None), P(None, "vel"), P("space", None), P("space", None), P()),
        out_specs=(P("vel", "space", None), P(None, "space", "vel"), P()),
        check_vma=False,
    )
```

```python
import functools
import math

import jax
import jax.numpy as jnp
import numpy as np
from jax import lax
from jax.experimental import pallas as pl
from jax.experimental.pallas import tpu as pltpu
from jax.sharding import PartitionSpec as P

NVX = 16
NZ = 16
MOM = 13
SWEEPS = 3
speed_range = 4.0
time_step = 0.08
coupling = 0.5

MESH = pl.DeviceIdType.MESH
F32 = jnp.float32
BF16 = jnp.bfloat16
X = 8
CELLS = 1024
LT = CELLS // 128
RING = 4
PEERS = RING * RING
LV = 128
CH = 56
HALO = 4
EXT = X + 2 * HALO
FIELD_ROWS = (1, 2, 3, 4, 0, 10, 11, 12)
OTHER_ROWS = (0, 5, 6, 7, 8, 9, 10, 11, 12)
HIGHEST = lax.Precision.HIGHEST


def functions_of(cx, cy, cz, xp=jnp):
    square = cx * cx + cy * cy + cz * cz
    weights = (2.0 * speed_range / NVX) ** 3 * math.pi ** (-1.5) * xp.exp(-square)
    heat = square - 2.5
    one = xp.ones_like(cx)
    rows = [
        one, cx, cy, cz, 2.0 * square / 3.0 - 1.0,
        2.0 * cx * cy, 2.0 * cx * cz, 2.0 * cy * cz,
        cx * cx - cy * cy, cy * cy - cz * cz,
        cx * heat, cy * heat, cz * heat,
    ]
    factor = 4.0 / 15.0
    target = [2.0 * cx, 2.0 * cy, 2.0 * cz, square - 1.5, one, factor * cx * heat, factor * cy * heat, factor * cz * heat]
    stencil = [1.0 - time_step * (xp.abs(cx) + xp.abs(cy) + xp.abs(cz))]
    for c in (cx, cy, cz):
        stencil += [time_step * xp.maximum(c, 0.0), time_step * xp.maximum(-c, 0.0)]
    return [r * weights for r in rows], target, stencil


def selection():
    sel = np.zeros((26, MOM))
    own = np.zeros((26, MOM))
    for j in range(26):
        if j < 8:
            sel[j, FIELD_ROWS[j]] = 1
        elif j < 17:
            sel[j, OTHER_ROWS[j - 8]] = 1
            own[j, OTHER_ROWS[j - 8]] = -1
        elif j < 21:
            own[j, j - 16] = 1
        else:
            sel[j, j - 16] = 1
    eye = np.eye(X)
    sel = np.repeat(sel, X, 0)
    spread = np.tile(np.eye(MOM), (1, X))
    mask = np.repeat(np.tile(eye, (26, 1)), MOM, 1)
    fixed = np.einsum("jr,xp->jxpr", own, eye).reshape(26 * X, X * MOM)
    return [a.astype(np.float32) for a in (sel, spread, mask, fixed)]


def coupling_table():
    line = speed_range * (2.0 * np.arange(NVX) + 1.0 - NVX) / NVX
    cx, cy, cz = (a.reshape(-1) for a in np.meshgrid(line, line, line, indexing="ij"))
    rows, target, stencil = functions_of(cx, cy, cz, np)
    n = np.einsum("rv,ov,kv->ork", rows, stencil, target)
    near = np.zeros((X, MOM, 8, EXT))
    side = np.zeros((X, MOM, 4, 8, X))
    for x in range(X):
        near[x, :, :, x + HALO] += n[0]
        near[x, :, :, x + HALO - 1] += n[1]
        near[x, :, :, x + HALO + 1] += n[2]
        for j in range(4):
            side[x, :, j, :, x] += n[3 + j]
    table = np.concatenate([near.reshape(X * MOM, 8 * EXT), side.reshape(X * MOM, 32 * X)], 1)
    return table.astype(np.float32)


def split(a):
    hi = a.astype(BF16)
    return hi, (a - hi.astype(F32)).astype(BF16)


def cat(parts):
    return jnp.concatenate(parts, axis=1)


def tiles(x):
    return [x[:, 128 * i:128 * (i + 1)] for i in range(LT)]


def y_shifts(t):
    lane = lax.broadcasted_iota(jnp.int32, t[0].shape, 1)
    up = [pltpu.roll(a, 16, 1) for a in t]
    down = [pltpu.roll(a, 112, 1) for a in t]
    ylo = [jnp.where(lane < 16, up[i - 1], up[i]) for i in range(LT)]
    yhi = [jnp.where(lane >= 112, down[(i + 1) % LT], down[i]) for i in range(LT)]
    return ylo, yhi


def z_shifts(t):
    z = lax.broadcasted_iota(jnp.int32, t[0].shape, 1) % NZ
    zlo = [jnp.where(z == 0, pltpu.roll(a, 113, 1), pltpu.roll(a, 1, 1)) for a in t]
    zhi = [jnp.where(z == NZ - 1, pltpu.roll(a, 15, 1), pltpu.roll(a, 127, 1)) for a in t]
    return zlo, zhi


def yz_shifts(x):
    t = tiles(x)
    return (t,) + y_shifts(t) + z_shifts(t)


def stencil_moments(q_ref, p):
    def rows(o, at=p):
        return tiles(q_ref[at, 16 * o:16 * o + 16, :])

    ylo, _ = y_shifts(rows(3))
    _, yhi = y_shifts(rows(4))
    zlo, _ = z_shifts(rows(5))
    _, zhi = z_shifts(rows(6))
    here, before, after = rows(0), rows(1, p - 1), rows(2, p + 1)
    return cat([(here[i] + before[i] + after[i]) + (ylo[i] + yhi[i]) + (zlo[i] + zhi[i]) for i in range(LT)])


def alpha_of(relax, wall):
    return jnp.where(wall > 0, 0.0, 1.0 - relax)


def stream_plane(src, halves, p, h, ct, zmat, scale=None):
    lane = lax.broadcasted_iota(jnp.int32, (LV, 128), 1)
    k0, cx, cy, cz = (ct[i] for i in range(4))
    px, py, pz = cx > 0, cy > 0, cz > 0
    kx, ky, kz = jnp.abs(cx), jnp.abs(cy), jnp.abs(cz)
    t = [src[p, :, 128 * i:128 * (i + 1)] for i in range(LT)]
    z = [
        jnp.dot(
            cat([halves[h, 0:LV, 128 * i:128 * (i + 1)], halves[h, LV:2 * LV, 128 * i:128 * (i + 1)]]),
            zmat[...],
            preferred_element_type=F32,
        )
        for i in range(LT)
    ]
    up = [pltpu.roll(a, 16, 1) for a in t]
    down = [pltpu.roll(a, 112, 1) for a in t]
    out = []
    for i in range(LT):
        s = slice(128 * i, 128 * (i + 1))
        in_x = jnp.where(px, src[p - 1, :, s], src[p + 1, :, s])
        in_y = jnp.where(
            py,
            jnp.where(lane < 16, up[i - 1], up[i]),
            jnp.where(lane >= 112, down[(i + 1) % LT], down[i]),
        )
        in_z = jnp.where(pz, z[i][:, 0:128], z[i][:, 128:256])
        val = (k0 * t[i] + kx * in_x) + (ky * in_y + kz * in_z)
        out.append(val if scale is None else val * scale[:, s])
    return out


def exchange(dist_hbm, relax_ref, wall_ref, vel_ref, inv_ref, sel_ref, spread_ref, mask_ref, fixed_ref, nc,
             aa, g1, g2_out, mac_out, norm_out,
             dbuf, dt, at_, dhl, ahl, q1, q2, mine, edges, from_left, from_right, rw, rwl, rwr,
             mrows, lm, ct, zmat, kx, pbuf, rsbuf, ssum, xbuf, total, fbuf, l1, h_left, h_right, b2out, b2l, b2r,
             u, b, rhs, add, l2, nsend, nrecv, cin, cout, cfar, cboth, cnear,
             sem_ld, s_nb, r_nb, s_rs, r_rs, s_ag, r_ag, s_x, r_x, s_nm, r_nm, s_e, r_e):
    v = lax.axis_index("vel")
    s = lax.axis_index("space")
    left = (v, lax.rem(s + 3, 4))
    right = (v, lax.rem(s + 1, 4))
    far = v // PEERS
    place = lax.rem(v, PEERS)
    partner = ((1 - far) * PEERS + place, s)

    def peer(o):
        return (far * PEERS + o, s)

    loads = [pltpu.make_async_copy(dist_hbm.at[:, pl.ds(128 * t, 128)], dbuf.at[t], sem_ld.at[t]) for t in range(LT)]
    for c in loads:
        c.start()

    barrier = pltpu.get_barrier_semaphore()

    def greet(j, c):
        pl.semaphore_signal(barrier, inc=1, device_id=peer(lax.rem(place + j, PEERS)), device_id_type=MESH)
        return c

    lax.fori_loop(1, PEERS, greet, 0)
    pl.semaphore_signal(barrier, inc=1, device_id=partner, device_id_type=MESH)
    for j in (1, 2, 3):
        pl.semaphore_signal(barrier, inc=1, device_id=(v, lax.rem(s + j, 4)), device_id_type=MESH)

    rw[0:X, :] = relax_ref[...]
    rw[X:2 * X, :] = wall_ref[...].astype(F32)
    vel = speed_range * (2.0 * vel_ref[...].astype(F32) + 1.0 - NVX) / NVX
    cx, cy, cz = vel[0:1], vel[1:2], vel[2:3]
    rows, _, stencil = functions_of(cx, cy, cz)
    mrows[...] = jnp.zeros_like(mrows)
    for r in range(MOM):
        mrows[r:r + 1, :] = rows[r]
    for o in range(7):
        hi, lo = split(mrows[...] * stencil[o])
        lm[16 * o:16 * o + 16, 0:LV] = hi
        lm[16 * o:16 * o + 16, LV:2 * LV] = hi
        lm[112 + 16 * o:128 + 16 * o, 0:LV] = lo
        lm[112 + 16 * o:128 + 16 * o, LV:2 * LV] = jnp.zeros_like(lo)
    for i, row in enumerate((stencil[0], time_step * cx, time_step * cy, time_step * cz)):
        ct[i] = jnp.transpose(jnp.broadcast_to(row, (LV, LV)))
    src_lane = lax.broadcasted_iota(jnp.int32, (LV, LV), 0)
    dst_lane = lax.broadcasted_iota(jnp.int32, (LV, LV), 1)
    dst_z = dst_lane % NZ
    lower = jnp.where(src_lane == jnp.where(dst_z == 0, dst_lane + NZ - 1, dst_lane - 1), 1.0, 0.0).astype(BF16)
    upper = jnp.where(src_lane == jnp.where(dst_z == NZ - 1, dst_lane - NZ + 1, dst_lane + 1), 1.0, 0.0).astype(BF16)
    for i in range(2):
        zmat[LV * i:LV * (i + 1), 0:LV] = lower
        zmat[LV * i:LV * (i + 1), LV:2 * LV] = upper
    part = jnp.dot(sel_ref[...], inv_ref[...], precision=HIGHEST, preferred_element_type=F32)
    part = jnp.dot(part, spread_ref[...], precision=HIGHEST, preferred_element_type=F32)
    kx[...] = part * mask_ref[...] + fixed_ref[...]
    zero_plane = jnp.zeros((LV, CELLS), F32)
    for p in (0, 9):
        dt[p] = zero_plane
        q1[p, 16:48, :] = jnp.zeros((32, CELLS), F32)
    for p in (0, 11):
        at_[p] = zero_plane
    for m in range(2):
        pbuf[m, 104:112, :] = jnp.zeros((8, CELLS), F32)

    def swap(i, to_right, right_dst, to_left, left_dst):
        a = pltpu.make_async_remote_copy(to_right, right_dst, s_nb.at[2 * i], r_nb.at[2 * i],
                                         device_id=right, device_id_type=MESH)
        c = pltpu.make_async_remote_copy(to_left, left_dst, s_nb.at[2 * i + 1], r_nb.at[2 * i + 1],
                                         device_id=left, device_id_type=MESH)
        a.start()
        c.start()
        return a, c

    def settle(copies):
        for c in copies:
            c.wait()

    settle(loads)

    def first(x, c):
        val = cat([dbuf[t, pl.ds(x, LV, stride=X), :] for t in range(LT)])
        dt[x + 1] = val
        hi, lo = split(val)
        dhl[x, 0:LV, :] = hi
        dhl[x, LV:2 * LV, :] = lo
        q = jnp.dot(lm[...], dhl[x], preferred_element_type=F32)
        q1[x + 1] = q[0:112] + q[112:224]
        return c

    lax.fori_loop(0, X, first, 0)
    pl.semaphore_wait(barrier, PEERS - 1 + 1 + 3)
    halo = swap(0, rw, rwl, rw, rwr)
    edges[0, 0:16, :] = q1[1, 32:48, :]
    edges[1, 0:16, :] = q1[X, 16:32, :]
    outer1 = swap(1, edges.at[1, pl.ds(0, 16)], from_left.at[pl.ds(0, 16)],
                  edges.at[0, pl.ds(0, 16)], from_right.at[pl.ds(0, 16)])

    def sum_first(x, c):
        mine[0, x] = stencil_moments(q1, x + 1)
        return c

    lax.fori_loop(0, X, sum_first, 0)

    def alpha_row(ref, x):
        return alpha_of(ref[pl.ds(x, 1), :], ref[pl.ds(x + X, 1), :])

    def products(i):
        hi, lo = split(at_[i + 1])
        ahl[i, 0:LV, :] = hi
        ahl[i, LV:2 * LV, :] = lo
        q = jnp.dot(lm[...], ahl[i], preferred_element_type=F32)
        q2[i] = q[0:112] + q[112:224]

    def second(j, c):
        x = lax.rem(X - j, X)

        val = stream_plane(dt, dhl, x + 1, x, ct, zmat, alpha_row(rw, x))
        for i in range(LT):
            at_[x + 2, :, 128 * i:128 * (i + 1)] = val[i]
        products(x + 1)
        return c

    def third(i):
        val = stream_plane(at_, ahl, i + 1, i, ct, zmat)
        for t in range(LT):
            aa[i + 1, :, 128 * t:128 * (t + 1)] = val[t]

    lax.fori_loop(0, 2, second, 0)
    settle(outer1)
    mine[0, 0] += from_left[0:16, :]
    mine[0, X - 1] += from_right[0:16, :]

    def pack(m):
        for x in range(X):
            pbuf[m, 13 * x:13 * x + 13, :] = mine[m, x, 0:13, :]

    def chunk_of(o):
        return (pl.ds(pl.multiple_of(CH * (o // LT), 8), CH), pl.ds(pl.multiple_of(128 * lax.rem(o, LT), 128), 128))

    def send_parts(m):
        def send(j, c):
            o = lax.rem(place + j, PEERS)
            r, k = chunk_of(o)
            pltpu.make_async_remote_copy(pbuf.at[m, r, k], rsbuf.at[m, j], s_rs.at[m], r_rs.at[m],
                                         device_id=peer(o), device_id_type=MESH).start()
            return c

        lax.fori_loop(1, PEERS, send, 0)

    def all_parts(m):
        return rsbuf.at[m, pl.ds(1, PEERS - 1)]

    def across(m):
        return pltpu.make_async_remote_copy(ssum.at[m], xbuf.at[m], s_x.at[m], r_x.at[m],
                                            device_id=partner, device_id_type=MESH)

    def own_sum(m):
        pltpu.make_async_copy(all_parts(m), all_parts(m), r_rs.at[m]).wait()
        r, k = chunk_of(place)
        acc = pbuf[m, r, k]
        for j in range(1, PEERS):
            acc = acc + rsbuf[m, j]
        ssum[m] = acc
        across(m).start()

    def send_total(m):
        across(m).wait()
        val = ssum[m] + xbuf[m]
        total[m] = val
        r, k = chunk_of(place)
        fbuf[m, r, k] = val

        def send(j, c):
            pltpu.make_async_remote_copy(total.at[m], fbuf.at[m, r, k], s_ag.at[m], r_ag.at[m],
                                         device_id=peer(lax.rem(place + j, PEERS)), device_id_type=MESH).start()
            return c

        lax.fori_loop(1, PEERS, send, 0)

    def all_totals(m):
        pltpu.make_async_copy(all_parts(m), all_parts(m), r_ag.at[m]).wait()

    def all_sent(m):
        pltpu.make_async_copy(all_parts(m), all_parts(m), s_rs.at[m]).wait()
        pltpu.make_async_copy(all_parts(m), all_parts(m), s_ag.at[m]).wait()

    pack(0)
    send_parts(0)
    lax.fori_loop(2, 7, second, 0)
    own_sum(0)
    lax.fori_loop(7, X, second, 0)

    settle(halo)
    speed = ct[1]
    to_lower = jnp.where(speed > 0, 0.0, -speed)
    to_upper = jnp.where(speed > 0, speed, 0.0)
    al_l, al_r = alpha_row(rwl, X - 1), alpha_row(rwr, 0)
    for i in range(LT):
        c = slice(128 * i, 128 * (i + 1))
        at_[1, :, c] = to_lower * dt[1, :, c] * al_l[:, c]
        at_[X + 2, :, c] = to_upper * dt[X, :, c] * al_r[:, c]

    def ends(j, c):
        products((X + 1) * j)
        return c

    lax.fori_loop(0, 2, ends, 0)

    edges[0, 16:32, :] = stencil_edge(q2, 0) + q2[1, 32:48, :]
    edges[0, 32:48, :] = q2[0, 32:48, :]
    edges[1, 16:32, :] = stencil_edge(q2, X + 1) + q2[X, 16:32, :]
    edges[1, 32:48, :] = q2[X + 1, 16:32, :]
    outer2 = swap(2, edges.at[1, pl.ds(16, 32)], from_left.at[pl.ds(16, 32)],
                  edges.at[0, pl.ds(16, 32)], from_right.at[pl.ds(16, 32)])

    def sum_second(x, c):
        mine[1, x] = stencil_moments(q2, x + 1)
        return c

    lax.fori_loop(0, X, sum_second, 0)
    send_total(0)

    def edge_third(j, c):
        third((X + 1) * j)
        return c

    lax.fori_loop(0, 2, edge_third, 0)
    for i in range(LT):
        c = slice(128 * i, 128 * (i + 1))
        aa[0, :, c] = to_lower * at_[1, :, c]
        aa[X + 3, :, c] = to_upper * at_[X + 2, :, c]
    settle(outer2)
    mine[1, 0] += from_left[16:32, :]
    mine[1, 1] += from_left[32:48, :]
    mine[1, X - 1] += from_right[16:32, :]
    mine[1, X - 2] += from_right[32:48, :]
    pack(1)
    send_parts(1)

    core = lax.rem(s, 2)
    mate = (v, s + 1 - 2 * core)
    over = (v, lax.rem(s + 2, 4))
    half = LV // 2
    mine_v = pl.ds(pl.multiple_of(half * core, 8), half)
    mate_v = pl.ds(pl.multiple_of(half * (1 - core), 8), half)
    out_end = pl.ds((X + 2) * core, 2)
    in_end = pl.ds((X + 2) * (1 - core), 2)

    def hand(i, src, dst, to):
        c = pltpu.make_async_remote_copy(src, dst, s_e.at[i], r_e.at[i], device_id=to, device_id_type=MESH)
        c.start()
        return c

    give = hand(0, aa.at[out_end, mate_v], cin, mate)
    near = hand(1, aa.at[in_end], cnear, mate)

    def inner_third(i, c):
        third(i)
        return c

    lax.fori_loop(1, 3, inner_third, 0)
    give.wait()
    cout[...] = aa[out_end, mine_v, :] + cin[...]
    across_x = hand(2, cout, cfar, over)
    lax.fori_loop(3, X + 1, inner_third, 0)
    own_sum(1)

    all_totals(0)
    l1[...] = jnp.dot(kx[...], fbuf[0, 0:104, :], precision=HIGHEST, preferred_element_type=F32)
    halo2 = swap(3, l1.at[pl.ds(0, 64)], h_left, l1.at[pl.ds(0, 64)], h_right)
    send_total(1)
    settle(halo2)

    zero8 = jnp.zeros((8, CELLS), F32)

    def clear_ends(k, c):
        for i in range(2):
            u[i, k, 0:8, :] = zero8
            u[i, k, 24:32, :] = zero8
        return c

    lax.fori_loop(0, 4, clear_ends, 0)

    def fill(k, lo_rows, own, hi_rows):
        b[k, 0:HALO, :] = lo_rows
        b[k, HALO:HALO + X, :] = own
        b[k, HALO + X:EXT, :] = hi_rows

    def smooth():
        def start(k, c):
            u[0, k, 8:24, :] = b[k]
            return c

        lax.fori_loop(0, 4, start, 0)
        for sweep in range(SWEEPS):
            src, dst = sweep % 2, 1 - sweep % 2

            def row(k, c):
                for blk in range(2):
                    lo = 8 + 8 * blk
                    here, ylo, yhi, zlo, zhi = yz_shifts(u[src, k, lo:lo + 8, :])
                    near = u[src, k, lo - 1:lo + 7, :] + u[src, k, lo + 1:lo + 9, :]
                    side = cat([(ylo[i] + yhi[i]) + (zlo[i] + zhi[i]) for i in range(LT)])
                    u[dst, k, lo:lo + 8, :] = (b[k, 8 * blk:8 * blk + 8, :] + coupling * (near + side)) * (1.0 / (1.0 + 6.0 * coupling))
                return c

            lax.fori_loop(0, 4, row, 0)
        return SWEEPS % 2

    for k in range(4):
        fill(k, h_left[8 * k + 4:8 * k + 8, :], l1[8 * k:8 * k + 8, :], h_right[8 * k:8 * k + 4, :])
    last = smooth()

    def gammas(relax, wall):
        return jnp.where(wall > 0, 0.0, relax), jnp.where(wall > 0, 1.0, relax)

    factors = [gammas(ref[0:X, :], ref[X:2 * X, :]) for ref in (rwl, rw, rwr)]
    for k in range(8):
        gl, go, gr = (f[1 if k in (3, 4) else 0] for f in factors)
        if k < 4:
            lo_rows = u[last, k, 8:8 + HALO, :]
            own = u[last, k, 8 + HALO:8 + HALO + X, :]
            hi_rows = u[last, k, 8 + HALO + X:8 + EXT, :]
        else:
            lo_rows = h_left[8 * k + 4:8 * k + 8, :]
            own = l1[8 * k:8 * k + 8, :]
            hi_rows = h_right[8 * k:8 * k + 4, :]
        own = own * go
        g1[EXT * k:EXT * k + HALO, :] = lo_rows * gl[4:8]
        g1[EXT * k + HALO:EXT * k + HALO + X, :] = own
        g1[EXT * k + HALO + X:EXT * (k + 1), :] = hi_rows * gr[0:4]
        _, ylo, yhi, zlo, zhi = yz_shifts(own)
        for j, val in enumerate((ylo, yhi, zlo, zhi)):
            rhs[64 * j + 8 * k:64 * j + 8 * k + 8, :] = cat(val)

    def squares(l, sm):
        acc = jnp.zeros((8, CELLS), F32)
        for i in range(9):
            d = l[64 + 8 * i:72 + 8 * i, :]
            acc = acc + d * d
        for k in range(4):
            d = u[sm, k, 8 + HALO:8 + HALO + X, :] - l[136 + 8 * k:144 + 8 * k, :]
            acc = acc + d * d
        parts = tiles(acc)
        out = parts[0]
        for i in range(1, LT):
            out = out + parts[i]
        return out

    nsend[0] = squares(l1, last)

    add[...] = (
        jnp.dot(nc[:, 0:128], g1[...], precision=HIGHEST, preferred_element_type=F32)
        + jnp.dot(nc[:, 128:384], rhs[...], precision=HIGHEST, preferred_element_type=F32)
    )
    across_x.wait()
    share = hand(3, cfar, cboth, mate)
    all_totals(1)
    m2 = fbuf[1, 0:104, :] + add[...]
    b2out[...] = jnp.dot(kx[0:32, :], m2, precision=HIGHEST, preferred_element_type=F32)
    halo3 = swap(6, b2out, b2l, b2out, b2r)
    l2[...] = jnp.dot(kx[32:208, :], m2, precision=HIGHEST, preferred_element_type=F32)

    near.wait()
    share.wait()
    is_upper = (core == 0).astype(F32)
    from_far = 2 + (X - 2) * core
    from_near = 2 + (X - 2) * (1 - core)

    def add_ends(i, carry):
        for t in range(LT):
            c = slice(128 * t, 128 * (t + 1))
            aa[from_near + i, :, c] += cnear[i, :, c]
            aa[from_far + i, mine_v, c] += jnp.where(wanted_of(mine_v) > 0, cfar[i, :, c], 0.0)
            aa[from_far + i, mate_v, c] += jnp.where(wanted_of(mate_v) > 0, cboth[i, :, c], 0.0)
        return carry

    def wanted_of(rows):
        towards = ct[1, rows, :]
        return jnp.where(towards > 0, is_upper, 1.0 - is_upper)

    lax.fori_loop(0, 2, add_ends, 0)

    settle(halo3)
    for k in range(4):
        fill(k, b2l[8 * k + 4:8 * k + 8, :], b2out[8 * k:8 * k + 8, :], b2r[8 * k:8 * k + 4, :])
    last = smooth()
    acc = jnp.zeros((8, CELLS), F32)
    for i in range(9):
        d = l2[32 + 8 * i:40 + 8 * i, :]
        acc = acc + d * d
    for k in range(4):
        d = u[last, k, 8 + HALO:8 + HALO + X, :] - l2[104 + 8 * k:112 + 8 * k, :]
        acc = acc + d * d
    parts = tiles(acc)
    out = parts[0]
    for i in range(1, LT):
        out = out + parts[i]
    nsend[1] = out
    notes = []
    for j in (1, 2, 3):
        c = pltpu.make_async_remote_copy(nsend, nrecv.at[j - 1], s_nm.at[j - 1], r_nm.at[j - 1],
                                         device_id=(v, lax.rem(s + j, 4)), device_id_type=MESH)
        c.start()
        notes.append(c)

    beta, both = gammas(rw[0:X, :], rw[X:2 * X, :])
    for k in range(8):
        f = u[last, k, 8 + HALO:8 + HALO + X, :] if k < 4 else l2[8 * k - 32:8 * k - 24, :]
        g2_out[8 * k:8 * k + 8, :] = f * (both if k in (3, 4) else beta)

    tile = pl.ds(pl.multiple_of(128 * (v // 4), 128), 128)
    turn = lax.rem(128 - 32 * lax.rem(v, 4), 128)
    for r in range(MOM):
        if 1 <= r <= 4:
            f = u[last, r - 1, 8 + HALO:8 + HALO + X, tile]
        elif r == 0:
            f = l2[0:8, tile]
        elif r >= 10:
            f = l2[8 + 8 * (r - 10):16 + 8 * (r - 10), tile]
        else:
            f = l2[136 + 8 * (r - 5):144 + 8 * (r - 5), tile]
        mac_out[r] = pltpu.roll(f, turn, 1)[:, 0:32]

    settle(notes)
    for i in range(2):
        norm_out[i] = (nsend[i] + nrecv[0, i]) + (nrecv[1, i] + nrecv[2, i])
    for m in range(2):
        all_sent(m)


def stencil_edge(q_ref, p):
    def rows(o):
        return tiles(q_ref[p, 16 * o:16 * o + 16, :])

    ylo, _ = y_shifts(rows(3))
    _, yhi = y_shifts(rows(4))
    zlo, _ = z_shifts(rows(5))
    _, zhi = z_shifts(rows(6))
    here = rows(0)
    return cat([here[i] + (ylo[i] + yhi[i]) + (zlo[i] + zhi[i]) for i in range(LT)])


PAIRS = 4


def renew(a_ref, g1_ref, g2_ref, relax_ref, wall_ref, vel_ref, mac_ref, sum_ref, out_hbm, mac_out, norm_out,
          obuf, stage, rhs, lt, lrows, sem_out):
    mac_out[...] = mac_ref[...]
    for i in range(2):
        norm_out[i] = jnp.sqrt(jnp.sum(sum_ref[i]))
    alpha = alpha_of(relax_ref[...], wall_ref[...])

    vel = speed_range * (2.0 * vel_ref[...].astype(F32) + 1.0 - NVX) / NVX
    _, target, stencil = functions_of(vel[0:1], vel[1:2], vel[2:3])
    for k in range(8):
        for o in range(7):
            lrows[8 * o + k:8 * o + k + 1, :] = stencil[o] * target[k]
        lrows[56 + k:57 + k, :] = target[k]
    hi, lo = split(lrows[...])
    hi, lo = hi.astype(F32), lo.astype(F32)
    lt[:, 0:128] = jnp.transpose(jnp.concatenate([hi, hi], 0)).astype(BF16)
    lt[:, 128:256] = jnp.transpose(jnp.concatenate([lo, lo], 0)).astype(BF16)

    for k in range(8):
        at = EXT * k + HALO
        here, ylo, yhi, zlo, zhi = yz_shifts(g1_ref[at:at + 8, :])
        before = g1_ref[at - 1:at + 7, :]
        after = g1_ref[at + 1:at + 9, :]
        for t in range(LT):
            cols = slice(128 * t, 128 * (t + 1))
            vals = (here[t], before[:, cols], after[:, cols], ylo[t], yhi[t], zlo[t], zhi[t])
            for o, val in enumerate(vals):
                stage[t, 64 * o + 8 * k:64 * o + 8 * k + 8, :] = val * alpha[:, cols]
            stage[t, 448 + 8 * k:456 + 8 * k, :] = g2_ref[8 * k:8 * k + 8, cols]

    def spread(x, c):
        for t in range(LT):
            hi, lo = split(stage[t, pl.ds(x, 64, stride=X), :])
            cols = slice(128 * t, 128 * (t + 1))
            rhs[x, 0:64, cols] = hi
            rhs[x, 64:128, cols] = lo
            rhs[x, 128:192, cols] = hi
            rhs[x, 192:256, cols] = lo
        return c

    lax.fori_loop(0, X, spread, 0)

    puts = []
    for i in range(PAIRS):
        def plane(x, c):
            al = alpha_of(relax_ref[pl.ds(x, 1), 256 * i:256 * (i + 1)], wall_ref[pl.ds(x, 1), 256 * i:256 * (i + 1)])
            val = jnp.dot(lt[...], rhs[x, :, 256 * i:256 * (i + 1)], preferred_element_type=F32) + al * a_ref[x + 2, :, 256 * i:256 * (i + 1)]
            obuf[2 * i, pl.ds(x, LV, stride=X), :] = val[:, 0:128]
            obuf[2 * i + 1, pl.ds(x, LV, stride=X), :] = val[:, 128:256]
            return c

        lax.fori_loop(0, X, plane, 0)
        for t in (2 * i, 2 * i + 1):
            c = pltpu.make_async_copy(obuf.at[t], out_hbm.at[:, pl.ds(128 * t, 128)], sem_out.at[t])
            c.start()
            puts.append(c)
    for c in puts:
        c.wait()


def shards(consts, dist, vel_index, relax, wall_mask, macro_inverse):
    vmem = pl.BlockSpec(memory_space=pltpu.VMEM)
    hbm = pl.BlockSpec(memory_space=pl.ANY)
    smem = pl.BlockSpec(memory_space=pltpu.SMEM)
    dma = pltpu.SemaphoreType.DMA
    sds = jax.ShapeDtypeStruct
    a, g1, g2, mac, norm = pl.pallas_call(
        exchange,
        out_shape=(
            pltpu.VMEM((X + 4, LV, CELLS), F32), pltpu.VMEM((8 * EXT, CELLS), F32), pltpu.VMEM((64, CELLS), F32),
            pltpu.VMEM((MOM, X, 32), F32), pltpu.VMEM((2, 8, 128), F32),
        ),
        in_specs=[hbm] + [vmem] * 9,
        out_specs=(vmem,) * 5,
        scratch_shapes=[
            pltpu.VMEM((LT, LV * X, 128), F32),
            pltpu.VMEM((X + 2, LV, CELLS), F32),
            pltpu.VMEM((X + 4, LV, CELLS), F32),
            pltpu.VMEM((X, 2 * LV, CELLS), BF16),
            pltpu.VMEM((X + 2, 2 * LV, CELLS), BF16),
            pltpu.VMEM((X + 2, 112, CELLS), F32),
            pltpu.VMEM((X + 2, 112, CELLS), F32),
            pltpu.VMEM((2, X, 16, CELLS), F32),
            pltpu.VMEM((2, 48, CELLS), F32),
            pltpu.VMEM((48, CELLS), F32),
            pltpu.VMEM((48, CELLS), F32),
            pltpu.VMEM((2 * X, CELLS), F32),
            pltpu.VMEM((2 * X, CELLS), F32),
            pltpu.VMEM((2 * X, CELLS), F32),
            pltpu.VMEM((16, LV), F32),
            pltpu.VMEM((224, 2 * LV), BF16),
            pltpu.VMEM((4, LV, LV), F32),
            pltpu.VMEM((2 * LV, 2 * LV), BF16),
            pltpu.VMEM((26 * X, X * MOM), F32),
            pltpu.VMEM((2, 2 * CH, CELLS), F32),
            pltpu.VMEM((2, PEERS, CH, 128), F32),
            pltpu.VMEM((2, CH, 128), F32),
            pltpu.VMEM((2, CH, 128), F32),
            pltpu.VMEM((2, CH, 128), F32),
            pltpu.VMEM((2, 2 * CH, CELLS), F32),
            pltpu.VMEM((26 * X, CELLS), F32),
            pltpu.VMEM((64, CELLS), F32),
            pltpu.VMEM((64, CELLS), F32),
            pltpu.VMEM((32, CELLS), F32),
            pltpu.VMEM((32, CELLS), F32),
            pltpu.VMEM((32, CELLS), F32),
            pltpu.VMEM((2, 4, 32, CELLS), F32),
            pltpu.VMEM((4, EXT, CELLS), F32),
            pltpu.VMEM((256, CELLS), F32),
            pltpu.VMEM((X * MOM, CELLS), F32),
            pltpu.VMEM((22 * X, CELLS), F32),
            pltpu.VMEM((2, 8, 128), F32),
            pltpu.VMEM((3, 2, 8, 128), F32),
            pltpu.VMEM((2, LV // 2, CELLS), F32),
            pltpu.VMEM((2, LV // 2, CELLS), F32),
            pltpu.VMEM((2, LV // 2, CELLS), F32),
            pltpu.VMEM((2, LV // 2, CELLS), F32),
            pltpu.VMEM((2, LV, CELLS), F32),
            dma((LT,)), dma((14,)), dma((14,)), dma((2,)), dma((2,)), dma((2,)), dma((2,)), dma((2,)), dma((2,)),
            dma((3,)), dma((3,)), dma((4,)), dma((4,)),
        ],
        compiler_params=pltpu.CompilerParams(collective_id=0, has_side_effects=True, vmem_limit_bytes=54 * 2 ** 20),
        name="exchange",
    )(dist.reshape(LV * X, CELLS), relax, wall_mask, vel_index, macro_inverse, *consts)

    out, mac, norm = pl.pallas_call(
        renew,
        out_shape=(sds((LV * X, CELLS), F32), sds((MOM, X, 32), F32), sds((2,), F32)),
        in_specs=[vmem] * 8,
        out_specs=(hbm, vmem, smem),
        scratch_shapes=[
            pltpu.VMEM((LT, LV * X, 128), F32),
            pltpu.VMEM((LT, 512, 128), F32),
            pltpu.VMEM((X, 256, CELLS), BF16),
            pltpu.VMEM((LV, 256), BF16),
            pltpu.VMEM((64, LV), F32),
            dma((LT,)),
        ],
        compiler_params=pltpu.CompilerParams(vmem_limit_bytes=32 * 2 ** 20),
        name="renew",
    )(a, g1, g2, relax, wall_mask, vel_index, mac, norm)
    return (out.reshape(LV, X, CELLS), mac, norm)


def solution(mesh):
    consts = selection() + [coupling_table()]
    return jax.shard_map(
        lambda *args: shards([jnp.asarray(c) for c in consts], *args),
        mesh=mesh,
        in_specs=(P("vel", "space", None), P(None, "vel"), P("space", None), P("space", None), P()),
        out_specs=(P("vel", "space", None), P(None, "space", "vel"), P()),
        check_vma=False,
    )
```

```python
import functools
import math

import jax
import jax.numpy as jnp
import numpy as np
from jax import lax
from jax.experimental import pallas as pl
from jax.experimental.pallas import tpu as pltpu
from jax.sharding import PartitionSpec as P

NVX = 16
NZ = 16
MOM = 13
SWEEPS = 3
speed_range = 4.0
time_step = 0.08
coupling = 0.5

MESH = pl.DeviceIdType.MESH
F32 = jnp.float32
BF16 = jnp.bfloat16
X = 8
CELLS = 1024
LT = CELLS // 128
RING = 4
PEERS = RING * RING
LV = 128
CH = 56
HALO = 4
EXT = X + 2 * HALO
FIELD_ROWS = (1, 2, 3, 4, 0, 10, 11, 12)
OTHER_ROWS = (0, 5, 6, 7, 8, 9, 10, 11, 12)
HIGHEST = lax.Precision.HIGHEST


def functions_of(cx, cy, cz, xp=jnp):
    square = cx * cx + cy * cy + cz * cz
    weights = (2.0 * speed_range / NVX) ** 3 * math.pi ** (-1.5) * xp.exp(-square)
    heat = square - 2.5
    one = xp.ones_like(cx)
    rows = [
        one, cx, cy, cz, 2.0 * square / 3.0 - 1.0,
        2.0 * cx * cy, 2.0 * cx * cz, 2.0 * cy * cz,
        cx * cx - cy * cy, cy * cy - cz * cz,
        cx * heat, cy * heat, cz * heat,
    ]
    factor = 4.0 / 15.0
    target = [2.0 * cx, 2.0 * cy, 2.0 * cz, square - 1.5, one, factor * cx * heat, factor * cy * heat, factor * cz * heat]
    stencil = [1.0 - time_step * (xp.abs(cx) + xp.abs(cy) + xp.abs(cz))]
    for c in (cx, cy, cz):
        stencil += [time_step * xp.maximum(c, 0.0), time_step * xp.maximum(-c, 0.0)]
    return [r * weights for r in rows], target, stencil


def selection():
    sel = np.zeros((26, MOM))
    own = np.zeros((26, MOM))
    for j in range(26):
        if j < 8:
            sel[j, FIELD_ROWS[j]] = 1
        elif j < 17:
            sel[j, OTHER_ROWS[j - 8]] = 1
            own[j, OTHER_ROWS[j - 8]] = -1
        elif j < 21:
            own[j, j - 16] = 1
        else:
            sel[j, j - 16] = 1
    eye = np.eye(X)
    sel = np.repeat(sel, X, 0)
    spread = np.tile(np.eye(MOM), (1, X))
    mask = np.repeat(np.tile(eye, (26, 1)), MOM, 1)
    fixed = np.einsum("jr,xp->jxpr", own, eye).reshape(26 * X, X * MOM)
    return [a.astype(np.float32) for a in (sel, spread, mask, fixed)]


def coupling_table():
    line = speed_range * (2.0 * np.arange(NVX) + 1.0 - NVX) / NVX
    cx, cy, cz = (a.reshape(-1) for a in np.meshgrid(line, line, line, indexing="ij"))
    rows, target, stencil = functions_of(cx, cy, cz, np)
    n = np.einsum("rv,ov,kv->ork", rows, stencil, target)
    near = np.zeros((X, MOM, 8, EXT))
    side = np.zeros((X, MOM, 4, 8, X))
    for x in range(X):
        near[x, :, :, x + HALO] += n[0]
        near[x, :, :, x + HALO - 1] += n[1]
        near[x, :, :, x + HALO + 1] += n[2]
        for j in range(4):
            side[x, :, j, :, x] += n[3 + j]
    table = np.concatenate([near.reshape(X * MOM, 8 * EXT), side.reshape(X * MOM, 32 * X)], 1)
    return table.astype(np.float32)


def split(a):
    hi = a.astype(BF16)
    return hi, (a - hi.astype(F32)).astype(BF16)


def cat(parts):
    return jnp.concatenate(parts, axis=1)


def tiles(x):
    return [x[:, 128 * i:128 * (i + 1)] for i in range(LT)]


def y_shifts(t):
    lane = lax.broadcasted_iota(jnp.int32, t[0].shape, 1)
    up = [pltpu.roll(a, 16, 1) for a in t]
    down = [pltpu.roll(a, 112, 1) for a in t]
    ylo = [jnp.where(lane < 16, up[i - 1], up[i]) for i in range(LT)]
    yhi = [jnp.where(lane >= 112, down[(i + 1) % LT], down[i]) for i in range(LT)]
    return ylo, yhi


def z_shifts(t):
    z = lax.broadcasted_iota(jnp.int32, t[0].shape, 1) % NZ
    zlo = [jnp.where(z == 0, pltpu.roll(a, 113, 1), pltpu.roll(a, 1, 1)) for a in t]
    zhi = [jnp.where(z == NZ - 1, pltpu.roll(a, 15, 1), pltpu.roll(a, 127, 1)) for a in t]
    return zlo, zhi


def yz_shifts(x):
    t = tiles(x)
    return (t,) + y_shifts(t) + z_shifts(t)


def stencil_moments(q_ref, p):
    def rows(o, at=p):
        return tiles(q_ref[at, 16 * o:16 * o + 16, :])

    ylo, _ = y_shifts(rows(3))
    _, yhi = y_shifts(rows(4))
    zlo, _ = z_shifts(rows(5))
    _, zhi = z_shifts(rows(6))
    here, before, after = rows(0), rows(1, p - 1), rows(2, p + 1)
    return cat([(here[i] + before[i] + after[i]) + (ylo[i] + yhi[i]) + (zlo[i] + zhi[i]) for i in range(LT)])


def alpha_of(relax, wall):
    return jnp.where(wall > 0, 0.0, 1.0 - relax)


def stream_plane(src, halves, p, h, ct, zmat, scale=None):
    lane = lax.broadcasted_iota(jnp.int32, (LV, 128), 1)
    k0, cx, cy, cz = (ct[i] for i in range(4))
    px, py, pz = cx > 0, cy > 0, cz > 0
    kx, ky, kz = jnp.abs(cx), jnp.abs(cy), jnp.abs(cz)
    t = [src[p, :, 128 * i:128 * (i + 1)] for i in range(LT)]
    z = [
        jnp.dot(
            cat([halves[h, 0:LV, 128 * i:128 * (i + 1)], halves[h, LV:2 * LV, 128 * i:128 * (i + 1)]]),
            zmat[...],
            preferred_element_type=F32,
        )
        for i in range(LT)
    ]
    up = [pltpu.roll(a, 16, 1) for a in t]
    down = [pltpu.roll(a, 112, 1) for a in t]
    out = []
    for i in range(LT):
        s = slice(128 * i, 128 * (i + 1))
        in_x = jnp.where(px, src[p - 1, :, s], src[p + 1, :, s])
        in_y = jnp.where(
            py,
            jnp.where(lane < 16, up[i - 1], up[i]),
            jnp.where(lane >= 112, down[(i + 1) % LT], down[i]),
        )
        in_z = jnp.where(pz, z[i][:, 0:128], z[i][:, 128:256])
        val = (k0 * t[i] + kx * in_x) + (ky * in_y + kz * in_z)
        out.append(val if scale is None else val * scale[:, s])
    return out


def exchange(dist_hbm, relax_ref, wall_ref, vel_ref, inv_ref, sel_ref, spread_ref, mask_ref, fixed_ref, nc,
             aa, g2_out, mac_out, norm_out,
             dbuf, dt, at_, dhl, ahl, q1, q2, mine, edges, from_left, from_right, rw, rwl, rwr,
             mrows, lm, ct, zmat, kx, pbuf, rsbuf, ssum, xbuf, total, fbuf, l1, h_out, h_left, h_right, b2out, b2_out, b2l, b2r,
             u, b, g1, rhs, lrows, lt, add, l2, nsend, nrecv, cin, cout, cfar, cboth, cnear,
             sem_ld, s_nb, r_nb, s_rs, r_rs, s_ag, r_ag, s_x, r_x, s_nm, r_nm, s_e, r_e):
    v = lax.axis_index("vel")
    s = lax.axis_index("space")
    left = (v, lax.rem(s + 3, 4))
    right = (v, lax.rem(s + 1, 4))
    far = v // PEERS
    place = lax.rem(v, PEERS)
    partner = ((1 - far) * PEERS + place, s)

    def peer(o):
        return (far * PEERS + o, s)

    loads = [pltpu.make_async_copy(dist_hbm.at[:, pl.ds(128 * t, 128)], dbuf.at[t], sem_ld.at[t]) for t in range(LT)]
    for c in loads:
        c.start()

    barrier = pltpu.get_barrier_semaphore()

    def greet(j, c):
        pl.semaphore_signal(barrier, inc=1, device_id=peer(lax.rem(place + j, PEERS)), device_id_type=MESH)
        return c

    lax.fori_loop(1, PEERS, greet, 0)
    pl.semaphore_signal(barrier, inc=1, device_id=partner, device_id_type=MESH)
    for j in (1, 2, 3):
        pl.semaphore_signal(barrier, inc=1, device_id=(v, lax.rem(s + j, 4)), device_id_type=MESH)

    rw[0:X, :] = relax_ref[...]
    rw[X:2 * X, :] = wall_ref[...].astype(F32)
    vel = speed_range * (2.0 * vel_ref[...].astype(F32) + 1.0 - NVX) / NVX
    cx, cy, cz = vel[0:1], vel[1:2], vel[2:3]
    rows, target, stencil = functions_of(cx, cy, cz)
    mrows[...] = jnp.zeros_like(mrows)
    for r in range(MOM):
        mrows[r:r + 1, :] = rows[r]
    for o in range(7):
        hi, lo = split(mrows[...] * stencil[o])
        lm[16 * o:16 * o + 16, 0:LV] = hi
        lm[16 * o:16 * o + 16, LV:2 * LV] = hi
        lm[112 + 16 * o:128 + 16 * o, 0:LV] = lo
        lm[112 + 16 * o:128 + 16 * o, LV:2 * LV] = jnp.zeros_like(lo)
    for i, row in enumerate((stencil[0], time_step * cx, time_step * cy, time_step * cz)):
        ct[i] = jnp.transpose(jnp.broadcast_to(row, (LV, LV)))
    for k in range(8):
        for o in range(7):
            lrows[8 * o + k:8 * o + k + 1, :] = stencil[o] * target[k]
    hi, lo = split(lrows[...])
    hi, lo = hi.astype(F32), lo.astype(F32)
    quad = jnp.concatenate([hi, hi, lo, lo, jnp.zeros((32, LV), F32)], 0)
    lt[:, 0:128] = jnp.transpose(quad[0:128]).astype(BF16)
    lt[:, 128:224] = jnp.transpose(quad[128:256])[:, 0:96].astype(BF16)
    src_lane = lax.broadcasted_iota(jnp.int32, (LV, LV), 0)
    dst_lane = lax.broadcasted_iota(jnp.int32, (LV, LV), 1)
    dst_z = dst_lane % NZ
    lower = jnp.where(src_lane == jnp.where(dst_z == 0, dst_lane + NZ - 1, dst_lane - 1), 1.0, 0.0).astype(BF16)
    upper = jnp.where(src_lane == jnp.where(dst_z == NZ - 1, dst_lane - NZ + 1, dst_lane + 1), 1.0, 0.0).astype(BF16)
    for i in range(2):
        zmat[LV * i:LV * (i + 1), 0:LV] = lower
        zmat[LV * i:LV * (i + 1), LV:2 * LV] = upper
    part = jnp.dot(sel_ref[...], inv_ref[...], precision=HIGHEST, preferred_element_type=F32)
    part = jnp.dot(part, spread_ref[...], precision=HIGHEST, preferred_element_type=F32)
    kx[...] = part * mask_ref[...] + fixed_ref[...]
    zero_plane = jnp.zeros((LV, CELLS), F32)
    for p in (0, 9):
        dt[p] = zero_plane
        q1[p, 16:48, :] = jnp.zeros((32, CELLS), F32)
    for p in (0, 11):
        at_[p] = zero_plane
    for m in range(2):
        pbuf[m, 104:112, :] = jnp.zeros((8, CELLS), F32)

    def swap(i, to_right, right_dst, to_left, left_dst):
        a = pltpu.make_async_remote_copy(to_right, right_dst, s_nb.at[2 * i], r_nb.at[2 * i],
                                         device_id=right, device_id_type=MESH)
        c = pltpu.make_async_remote_copy(to_left, left_dst, s_nb.at[2 * i + 1], r_nb.at[2 * i + 1],
                                         device_id=left, device_id_type=MESH)
        a.start()
        c.start()
        return a, c

    def settle(copies):
        for c in copies:
            c.wait()

    settle(loads)

    def first(x, c):
        val = cat([dbuf[t, pl.ds(x, LV, stride=X), :] for t in range(LT)])
        dt[x + 1] = val
        hi, lo = split(val)
        dhl[x, 0:LV, :] = hi
        dhl[x, LV:2 * LV, :] = lo
        q = jnp.dot(lm[...], dhl[x], preferred_element_type=F32)
        q1[x + 1] = q[0:112] + q[112:224]
        return c

    lax.fori_loop(0, X, first, 0)
    pl.semaphore_wait(barrier, PEERS - 1 + 1 + 3)
    halo = swap(0, rw, rwl, rw, rwr)
    edges[0, 0:16, :] = q1[1, 32:48, :]
    edges[1, 0:16, :] = q1[X, 16:32, :]
    outer1 = swap(1, edges.at[1, pl.ds(0, 16)], from_left.at[pl.ds(0, 16)],
                  edges.at[0, pl.ds(0, 16)], from_right.at[pl.ds(0, 16)])

    def sum_first(x, c):
        mine[0, x] = stencil_moments(q1, x + 1)
        return c

    lax.fori_loop(0, X, sum_first, 0)

    def alpha_row(ref, x):
        return alpha_of(ref[pl.ds(x, 1), :], ref[pl.ds(x + X, 1), :])

    def products(i):
        hi, lo = split(at_[i + 1])
        ahl[i, 0:LV, :] = hi
        ahl[i, LV:2 * LV, :] = lo
        q = jnp.dot(lm[...], ahl[i], preferred_element_type=F32)
        q2[i] = q[0:112] + q[112:224]

    def second(j, c):
        x = lax.rem(X - j, X)

        val = stream_plane(dt, dhl, x + 1, x, ct, zmat, alpha_row(rw, x))
        for i in range(LT):
            at_[x + 2, :, 128 * i:128 * (i + 1)] = val[i]
        products(x + 1)
        return c

    def third(i):
        val = stream_plane(at_, ahl, i + 1, i, ct, zmat)
        for t in range(LT):
            aa[i + 1, :, 128 * t:128 * (t + 1)] = val[t]

    lax.fori_loop(0, 2, second, 0)
    settle(outer1)
    mine[0, 0] += from_left[0:16, :]
    mine[0, X - 1] += from_right[0:16, :]

    def pack(m):
        for x in range(X):
            pbuf[m, 13 * x:13 * x + 13, :] = mine[m, x, 0:13, :]

    def chunk_of(o):
        return (pl.ds(pl.multiple_of(CH * (o // LT), 8), CH), pl.ds(pl.multiple_of(128 * lax.rem(o, LT), 128), 128))

    def send_parts(m):
        def send(j, c):
            o = lax.rem(place + j, PEERS)
            r, k = chunk_of(o)
            pltpu.make_async_remote_copy(pbuf.at[m, r, k], rsbuf.at[m, j], s_rs.at[m], r_rs.at[m],
                                         device_id=peer(o), device_id_type=MESH).start()
            return c

        lax.fori_loop(1, PEERS, send, 0)

    def all_parts(m):
        return rsbuf.at[m, pl.ds(1, PEERS - 1)]

    def across(m):
        return pltpu.make_async_remote_copy(ssum.at[m], xbuf.at[m], s_x.at[m], r_x.at[m],
                                            device_id=partner, device_id_type=MESH)

    def own_sum(m):
        pltpu.make_async_copy(all_parts(m), all_parts(m), r_rs.at[m]).wait()
        r, k = chunk_of(place)
        acc = pbuf[m, r, k]
        for j in range(1, PEERS):
            acc = acc + rsbuf[m, j]
        ssum[m] = acc
        across(m).start()

    def send_total(m):
        across(m).wait()
        val = ssum[m] + xbuf[m]
        total[m] = val
        r, k = chunk_of(place)
        fbuf[m, r, k] = val

        def send(j, c):
            pltpu.make_async_remote_copy(total.at[m], fbuf.at[m, r, k], s_ag.at[m], r_ag.at[m],
                                         device_id=peer(lax.rem(place + j, PEERS)), device_id_type=MESH).start()
            return c

        lax.fori_loop(1, PEERS, send, 0)

    def all_totals(m):
        pltpu.make_async_copy(all_parts(m), all_parts(m), r_ag.at[m]).wait()

    def all_sent(m):
        pltpu.make_async_copy(all_parts(m), all_parts(m), s_rs.at[m]).wait()
        pltpu.make_async_copy(all_parts(m), all_parts(m), s_ag.at[m]).wait()

    pack(0)
    send_parts(0)
    lax.fori_loop(2, X, second, 0)

    settle(halo)
    speed = ct[1]
    to_lower = jnp.where(speed > 0, 0.0, -speed)
    to_upper = jnp.where(speed > 0, speed, 0.0)
    al_l, al_r = alpha_row(rwl, X - 1), alpha_row(rwr, 0)
    for i in range(LT):
        c = slice(128 * i, 128 * (i + 1))
        at_[1, :, c] = to_lower * dt[1, :, c] * al_l[:, c]
        at_[X + 2, :, c] = to_upper * dt[X, :, c] * al_r[:, c]

    def ends(j, c):
        products((X + 1) * j)
        return c

    lax.fori_loop(0, 2, ends, 0)

    edges[0, 16:32, :] = stencil_edge(q2, 0) + q2[1, 32:48, :]
    edges[0, 32:48, :] = q2[0, 32:48, :]
    edges[1, 16:32, :] = stencil_edge(q2, X + 1) + q2[X, 16:32, :]
    edges[1, 32:48, :] = q2[X + 1, 16:32, :]
    outer2 = swap(2, edges.at[1, pl.ds(16, 32)], from_left.at[pl.ds(16, 32)],
                  edges.at[0, pl.ds(16, 32)], from_right.at[pl.ds(16, 32)])
    own_sum(0)

    def sum_second(x, c):
        mine[1, x] = stencil_moments(q2, x + 1)
        return c

    lax.fori_loop(0, X, sum_second, 0)

    def edge_third(j, c):
        third((X + 1) * j)
        return c

    lax.fori_loop(0, 2, edge_third, 0)
    for i in range(LT):
        c = slice(128 * i, 128 * (i + 1))
        aa[0, :, c] = to_lower * at_[1, :, c]
        aa[X + 3, :, c] = to_upper * at_[X + 2, :, c]
    settle(outer2)
    mine[1, 0] += from_left[16:32, :]
    mine[1, 1] += from_left[32:48, :]
    mine[1, X - 1] += from_right[16:32, :]
    mine[1, X - 2] += from_right[32:48, :]
    pack(1)
    send_parts(1)
    send_total(0)

    core = lax.rem(s, 2)
    mate = (v, s + 1 - 2 * core)
    over = (v, lax.rem(s + 2, 4))
    half = LV // 2
    mine_v = pl.ds(pl.multiple_of(half * core, 8), half)
    mate_v = pl.ds(pl.multiple_of(half * (1 - core), 8), half)
    out_end = pl.ds((X + 2) * core, 2)
    in_end = pl.ds((X + 2) * (1 - core), 2)

    def hand(i, src, dst, to):
        c = pltpu.make_async_remote_copy(src, dst, s_e.at[i], r_e.at[i], device_id=to, device_id_type=MESH)
        c.start()
        return c

    give = hand(0, aa.at[out_end, mate_v], cin, mate)
    near = hand(1, aa.at[in_end], cnear, mate)

    def inner_third(i, c):
        third(i)
        return c

    lax.fori_loop(1, 3, inner_third, 0)
    give.wait()
    cout[...] = aa[out_end, mine_v, :] + cin[...]
    over_0 = hand(2, cout.at[0], cfar.at[0], over)
    lax.fori_loop(3, 6, inner_third, 0)

    all_totals(0)
    l1[...] = jnp.dot(kx[...], fbuf[0, 0:104, :], precision=HIGHEST, preferred_element_type=F32)
    for k in range(8):
        h_out[0, HALO * k:HALO * (k + 1), :] = l1[8 * k:8 * k + HALO, :]
        h_out[1, HALO * k:HALO * (k + 1), :] = l1[8 * k + X - HALO:8 * k + X, :]
    halo2 = swap(3, h_out.at[1], h_left, h_out.at[0], h_right)
    own_sum(1)
    lax.fori_loop(6, X + 1, inner_third, 0)
    send_total(1)
    over_1 = hand(3, cout.at[1], cfar.at[1], over)
    settle(halo2)

    zero8 = jnp.zeros((8, CELLS), F32)

    def clear_ends(k, c):
        for i in range(2):
            u[i, k, 0:8, :] = zero8
            u[i, k, 24:32, :] = zero8
        return c

    lax.fori_loop(0, 4, clear_ends, 0)

    def fill(k, lo_rows, own, hi_rows):
        b[k, 0:HALO, :] = lo_rows
        b[k, HALO:HALO + X, :] = own
        b[k, HALO + X:EXT, :] = hi_rows

    def smooth():
        def start(k, c):
            u[0, k, 8:24, :] = b[k]
            return c

        lax.fori_loop(0, 4, start, 0)
        for sweep in range(SWEEPS):
            src, dst = sweep % 2, 1 - sweep % 2

            def row(k, c):
                for blk in range(2):
                    lo = 8 + 8 * blk
                    here, ylo, yhi, zlo, zhi = yz_shifts(u[src, k, lo:lo + 8, :])
                    near = u[src, k, lo - 1:lo + 7, :] + u[src, k, lo + 1:lo + 9, :]
                    side = cat([(ylo[i] + yhi[i]) + (zlo[i] + zhi[i]) for i in range(LT)])
                    u[dst, k, lo:lo + 8, :] = (b[k, 8 * blk:8 * blk + 8, :] + coupling * (near + side)) * (1.0 / (1.0 + 6.0 * coupling))
                return c

            lax.fori_loop(0, 4, row, 0)
        return SWEEPS % 2

    for k in range(4):
        fill(k, h_left[4 * k:4 * k + 4, :], l1[8 * k:8 * k + 8, :], h_right[4 * k:4 * k + 4, :])
    last = smooth()

    def gammas(relax, wall):
        return jnp.where(wall > 0, 0.0, relax), jnp.where(wall > 0, 1.0, relax)

    own_alpha = alpha_of(rw[0:X, :], rw[X:2 * X, :])
    factors = [gammas(ref[0:X, :], ref[X:2 * X, :]) for ref in (rwl, rw, rwr)]
    for k in range(8):
        gl, go, gr = (f[1 if k in (3, 4) else 0] for f in factors)
        if k < 4:
            lo_rows = u[last, k, 8:8 + HALO, :]
            own = u[last, k, 8 + HALO:8 + HALO + X, :]
            hi_rows = u[last, k, 8 + HALO + X:8 + EXT, :]
        else:
            lo_rows = h_left[4 * k:4 * k + 4, :]
            own = l1[8 * k:8 * k + 8, :]
            hi_rows = h_right[4 * k:4 * k + 4, :]
        own = own * go
        g1[EXT * k:EXT * k + HALO, :] = lo_rows * gl[4:8]
        g1[EXT * k + HALO:EXT * k + HALO + X, :] = own
        g1[EXT * k + HALO + X:EXT * (k + 1), :] = hi_rows * gr[0:4]
        here, ylo, yhi, zlo, zhi = yz_shifts(own)
        for j, val in enumerate((ylo, yhi, zlo, zhi)):
            rhs[64 * j + 8 * k:64 * j + 8 * k + 8, :] = cat(val)
        at = EXT * k + HALO
        before = tiles(g1[at - 1:at + 7, :])
        after = tiles(g1[at + 1:at + 9, :])
        for t in range(LT):
            al = own_alpha[:, 128 * t:128 * (t + 1)]
            for o, val in enumerate((here, before, after, ylo, yhi, zlo, zhi)):
                dbuf[t, 64 * o + 8 * k:64 * o + 8 * k + 8, :] = val[t] * al

    def squares(l, sm):
        acc = jnp.zeros((8, CELLS), F32)
        for i in range(9):
            d = l[64 + 8 * i:72 + 8 * i, :]
            acc = acc + d * d
        for k in range(4):
            d = u[sm, k, 8 + HALO:8 + HALO + X, :] - l[136 + 8 * k:144 + 8 * k, :]
            acc = acc + d * d
        parts = tiles(acc)
        out = parts[0]
        for i in range(1, LT):
            out = out + parts[i]
        return out

    nsend[0] = squares(l1, last)

    add[...] = (
        jnp.dot(nc[:, 0:128], g1[...], precision=HIGHEST, preferred_element_type=F32)
        + jnp.dot(nc[:, 128:384], rhs[...], precision=HIGHEST, preferred_element_type=F32)
    )

    def spread(x, c):
        for t in range(LT):
            hi, lo = split(dbuf[t, pl.ds(x, 56, stride=X), :])
            both_parts = jnp.concatenate([hi.astype(F32), lo.astype(F32)], 0).astype(BF16)
            cols = slice(128 * t, 128 * (t + 1))
            dhl[x, 0:112, cols] = both_parts
            dhl[x, 112:224, cols] = both_parts
        return c

    lax.fori_loop(0, X, spread, 0)
    over_0.wait()
    over_1.wait()
    share = hand(4, cfar, cboth, mate)
    all_totals(1)
    m2 = fbuf[1, 0:104, :] + add[...]
    b2out[...] = jnp.dot(kx[0:32, :], m2, precision=HIGHEST, preferred_element_type=F32)
    for k in range(4):
        b2_out[0, HALO * k:HALO * (k + 1), :] = b2out[8 * k:8 * k + HALO, :]
        b2_out[1, HALO * k:HALO * (k + 1), :] = b2out[8 * k + X - HALO:8 * k + X, :]
    halo3 = swap(6, b2_out.at[1], b2l, b2_out.at[0], b2r)
    l2[...] = jnp.dot(kx[32:208, :], m2, precision=HIGHEST, preferred_element_type=F32)

    def combine(x):
        aa[x + 2] = jnp.dot(lt[...], dhl[x, 0:224, :], preferred_element_type=F32) + alpha_row(rw, x) * aa[x + 2]

    def middle(x, c):
        combine(x)
        return c

    lax.fori_loop(2, X - 2, middle, 0)
    settle(halo3)
    for k in range(4):
        fill(k, b2l[4 * k:4 * k + 4, :], b2out[8 * k:8 * k + 8, :], b2r[4 * k:4 * k + 4, :])
    last = smooth()
    acc = jnp.zeros((8, CELLS), F32)
    for i in range(9):
        d = l2[32 + 8 * i:40 + 8 * i, :]
        acc = acc + d * d
    for k in range(4):
        d = u[last, k, 8 + HALO:8 + HALO + X, :] - l2[104 + 8 * k:112 + 8 * k, :]
        acc = acc + d * d
    parts = tiles(acc)
    out = parts[0]
    for i in range(1, LT):
        out = out + parts[i]
    nsend[1] = out
    notes = []
    for j in (1, 2, 3):
        c = pltpu.make_async_remote_copy(nsend, nrecv.at[j - 1], s_nm.at[j - 1], r_nm.at[j - 1],
                                         device_id=(v, lax.rem(s + j, 4)), device_id_type=MESH)
        c.start()
        notes.append(c)

    beta, both = gammas(rw[0:X, :], rw[X:2 * X, :])
    for k in range(8):
        f = u[last, k, 8 + HALO:8 + HALO + X, :] if k < 4 else l2[8 * k - 32:8 * k - 24, :]
        g2_out[8 * k:8 * k + 8, :] = f * (both if k in (3, 4) else beta)

    tile = pl.ds(pl.multiple_of(128 * (v // 4), 128), 128)
    turn = lax.rem(128 - 32 * lax.rem(v, 4), 128)
    for r in range(MOM):
        if 1 <= r <= 4:
            f = u[last, r - 1, 8 + HALO:8 + HALO + X, tile]
        elif r == 0:
            f = l2[0:8, tile]
        elif r >= 10:
            f = l2[8 + 8 * (r - 10):16 + 8 * (r - 10), tile]
        else:
            f = l2[136 + 8 * (r - 5):144 + 8 * (r - 5), tile]
        mac_out[r] = pltpu.roll(f, turn, 1)[:, 0:32]

    near.wait()
    share.wait()
    is_upper = (core == 0).astype(F32)
    from_far = 2 + (X - 2) * core
    from_near = 2 + (X - 2) * (1 - core)

    def add_ends(i, carry):
        for t in range(LT):
            c = slice(128 * t, 128 * (t + 1))
            aa[from_near + i, :, c] += cnear[i, :, c]
            aa[from_far + i, mine_v, c] += jnp.where(wanted_of(mine_v) > 0, cfar[i, :, c], 0.0)
            aa[from_far + i, mate_v, c] += jnp.where(wanted_of(mate_v) > 0, cboth[i, :, c], 0.0)
        return carry

    def wanted_of(rows):
        towards = ct[1, rows, :]
        return jnp.where(towards > 0, is_upper, 1.0 - is_upper)

    lax.fori_loop(0, 2, add_ends, 0)

    def outside(j, c):
        combine(lax.rem(j + X - 2, X))
        return c

    lax.fori_loop(0, 4, outside, 0)

    settle(notes)
    for i in range(2):
        norm_out[i] = (nsend[i] + nrecv[0, i]) + (nrecv[1, i] + nrecv[2, i])
    for m in range(2):
        all_sent(m)


def stencil_edge(q_ref, p):
    def rows(o):
        return tiles(q_ref[p, 16 * o:16 * o + 16, :])

    ylo, _ = y_shifts(rows(3))
    _, yhi = y_shifts(rows(4))
    zlo, _ = z_shifts(rows(5))
    _, zhi = z_shifts(rows(6))
    here = rows(0)
    return cat([here[i] + (ylo[i] + yhi[i]) + (zlo[i] + zhi[i]) for i in range(LT)])


PAIRS = 4


def renew(a_ref, g2_ref, vel_ref, mac_ref, sum_ref, out_hbm, mac_out, norm_out, obuf, stage, rhs, lt, sem_out):
    mac_out[...] = mac_ref[...]
    for i in range(2):
        norm_out[i] = jnp.sqrt(jnp.sum(sum_ref[i]))

    vel = speed_range * (2.0 * vel_ref[...].astype(F32) + 1.0 - NVX) / NVX
    _, target, _ = functions_of(vel[0:1], vel[1:2], vel[2:3])
    for k in range(8):
        stage[0, k:k + 1, :] = target[k]
    hi, lo = split(stage[0, 0:8, :])
    hi, lo = hi.astype(F32), lo.astype(F32)
    quad = jnp.concatenate([hi, hi, lo, lo, jnp.zeros((96, LV), F32)], 0)
    lt[...] = jnp.transpose(quad)[:, 0:32].astype(BF16)

    for t in range(LT):
        stage[t] = g2_ref[:, 128 * t:128 * (t + 1)]

    def spread(x, c):
        for t in range(LT):
            hi, lo = split(stage[t, pl.ds(x, 8, stride=X), :])
            both_parts = jnp.concatenate([hi.astype(F32), lo.astype(F32)], 0).astype(BF16)
            cols = slice(128 * t, 128 * (t + 1))
            rhs[x, 0:16, cols] = both_parts
            rhs[x, 16:32, cols] = both_parts
        return c

    lax.fori_loop(0, X, spread, 0)

    puts = []
    for i in range(PAIRS):
        pair = slice(256 * i, 256 * (i + 1))

        def plane(x, c):
            val = jnp.dot(lt[...], rhs[x, :, pair], preferred_element_type=F32) + a_ref[x + 2, :, pair]
            obuf[2 * i, pl.ds(x, LV, stride=X), :] = val[:, 0:128]
            obuf[2 * i + 1, pl.ds(x, LV, stride=X), :] = val[:, 128:256]
            return c

        lax.fori_loop(0, X, plane, 0)
        for t in (2 * i, 2 * i + 1):
            c = pltpu.make_async_copy(obuf.at[t], out_hbm.at[:, pl.ds(128 * t, 128)], sem_out.at[t])
            c.start()
            puts.append(c)
    for c in puts:
        c.wait()


def shards(consts, dist, vel_index, relax, wall_mask, macro_inverse):
    vmem = pl.BlockSpec(memory_space=pltpu.VMEM)
    hbm = pl.BlockSpec(memory_space=pl.ANY)
    smem = pl.BlockSpec(memory_space=pltpu.SMEM)
    dma = pltpu.SemaphoreType.DMA
    sds = jax.ShapeDtypeStruct
    a, g2, mac, norm = pl.pallas_call(
        exchange,
        out_shape=(
            pltpu.VMEM((X + 4, LV, CELLS), F32), pltpu.VMEM((64, CELLS), F32),
            pltpu.VMEM((MOM, X, 32), F32), pltpu.VMEM((2, 8, 128), F32),
        ),
        in_specs=[hbm] + [vmem] * 9,
        out_specs=(vmem,) * 4,
        scratch_shapes=[
            pltpu.VMEM((LT, LV * X, 128), F32),
            pltpu.VMEM((X + 2, LV, CELLS), F32),
            pltpu.VMEM((X + 4, LV, CELLS), F32),
            pltpu.VMEM((X, 2 * LV, CELLS), BF16),
            pltpu.VMEM((X + 2, 2 * LV, CELLS), BF16),
            pltpu.VMEM((X + 2, 112, CELLS), F32),
            pltpu.VMEM((X + 2, 112, CELLS), F32),
            pltpu.VMEM((2, X, 16, CELLS), F32),
            pltpu.VMEM((2, 48, CELLS), F32),
            pltpu.VMEM((48, CELLS), F32),
            pltpu.VMEM((48, CELLS), F32),
            pltpu.VMEM((2 * X, CELLS), F32),
            pltpu.VMEM((2 * X, CELLS), F32),
            pltpu.VMEM((2 * X, CELLS), F32),
            pltpu.VMEM((16, LV), F32),
            pltpu.VMEM((224, 2 * LV), BF16),
            pltpu.VMEM((4, LV, LV), F32),
            pltpu.VMEM((2 * LV, 2 * LV), BF16),
            pltpu.VMEM((26 * X, X * MOM), F32),
            pltpu.VMEM((2, 2 * CH, CELLS), F32),
            pltpu.VMEM((2, PEERS, CH, 128), F32),
            pltpu.VMEM((2, CH, 128), F32),
            pltpu.VMEM((2, CH, 128), F32),
            pltpu.VMEM((2, CH, 128), F32),
            pltpu.VMEM((2, 2 * CH, CELLS), F32),
            pltpu.VMEM((26 * X, CELLS), F32),
            pltpu.VMEM((2, 32, CELLS), F32),
            pltpu.VMEM((32, CELLS), F32),
            pltpu.VMEM((32, CELLS), F32),
            pltpu.VMEM((32, CELLS), F32),
            pltpu.VMEM((2, 16, CELLS), F32),
            pltpu.VMEM((16, CELLS), F32),
            pltpu.VMEM((16, CELLS), F32),
            pltpu.VMEM((2, 4, 32, CELLS), F32),
            pltpu.VMEM((4, EXT, CELLS), F32),
            pltpu.VMEM((8 * EXT, CELLS), F32),
            pltpu.VMEM((256, CELLS), F32),
            pltpu.VMEM((56, LV), F32),
            pltpu.VMEM((LV, 224), BF16),
            pltpu.VMEM((X * MOM, CELLS), F32),
            pltpu.VMEM((22 * X, CELLS), F32),
            pltpu.VMEM((2, 8, 128), F32),
            pltpu.VMEM((3, 2, 8, 128), F32),
            pltpu.VMEM((2, LV // 2, CELLS), F32),
            pltpu.VMEM((2, LV // 2, CELLS), F32),
            pltpu.VMEM((2, LV // 2, CELLS), F32),
            pltpu.VMEM((2, LV // 2, CELLS), F32),
            pltpu.VMEM((2, LV, CELLS), F32),
            dma((LT,)), dma((14,)), dma((14,)), dma((2,)), dma((2,)), dma((2,)), dma((2,)), dma((2,)), dma((2,)),
            dma((3,)), dma((3,)), dma((5,)), dma((5,)),
        ],
        compiler_params=pltpu.CompilerParams(collective_id=0, has_side_effects=True, vmem_limit_bytes=54 * 2 ** 20),
        name="exchange",
    )(dist.reshape(LV * X, CELLS), relax, wall_mask, vel_index, macro_inverse, *consts)

    out, mac, norm = pl.pallas_call(
        renew,
        out_shape=(sds((LV * X, CELLS), F32), sds((MOM, X, 32), F32), sds((2,), F32)),
        in_specs=[vmem] * 5,
        out_specs=(hbm, vmem, smem),
        scratch_shapes=[
            pltpu.VMEM((LT, LV * X, 128), F32),
            pltpu.VMEM((LT, 64, 128), F32),
            pltpu.VMEM((X, 32, CELLS), BF16),
            pltpu.VMEM((LV, 32), BF16),
            dma((LT,)),
        ],
        compiler_params=pltpu.CompilerParams(vmem_limit_bytes=32 * 2 ** 20),
        name="renew",
    )(a, g2, vel_index, mac, norm)
    return (out.reshape(LV, X, CELLS), mac, norm)


def solution(mesh):
    consts = selection() + [coupling_table()]
    return jax.shard_map(
        lambda *args: shards([jnp.asarray(c) for c in consts], *args),
        mesh=mesh,
        in_specs=(P("vel", "space", None), P(None, "vel"), P("space", None), P("space", None), P()),
        out_specs=(P("vel", "space", None), P(None, "space", "vel"), P()),
        check_vma=False,
    )
```

```python
import functools
import math

import jax
import jax.numpy as jnp
import numpy as np
from jax import lax
from jax.experimental import pallas as pl
from jax.experimental.pallas import tpu as pltpu
from jax.sharding import PartitionSpec as P

NVX = 16
NZ = 16
MOM = 13
SWEEPS = 3
speed_range = 4.0
time_step = 0.08
coupling = 0.5

MESH = pl.DeviceIdType.MESH
F32 = jnp.float32
BF16 = jnp.bfloat16
X = 8
CELLS = 1024
LT = CELLS // 128
RING = 4
PEERS = RING * RING
LV = 128
CH = 56
HALO = 4
EXT = X + 2 * HALO
FIELD_ROWS = (1, 2, 3, 4, 0, 10, 11, 12)
OTHER_ROWS = (0, 5, 6, 7, 8, 9, 10, 11, 12)
HIGHEST = lax.Precision.HIGHEST


def functions_of(cx, cy, cz, xp=jnp):
    square = cx * cx + cy * cy + cz * cz
    weights = (2.0 * speed_range / NVX) ** 3 * math.pi ** (-1.5) * xp.exp(-square)
    heat = square - 2.5
    one = xp.ones_like(cx)
    rows = [
        one, cx, cy, cz, 2.0 * square / 3.0 - 1.0,
        2.0 * cx * cy, 2.0 * cx * cz, 2.0 * cy * cz,
        cx * cx - cy * cy, cy * cy - cz * cz,
        cx * heat, cy * heat, cz * heat,
    ]
    factor = 4.0 / 15.0
    target = [2.0 * cx, 2.0 * cy, 2.0 * cz, square - 1.5, one, factor * cx * heat, factor * cy * heat, factor * cz * heat]
    stencil = [1.0 - time_step * (xp.abs(cx) + xp.abs(cy) + xp.abs(cz))]
    for c in (cx, cy, cz):
        stencil += [time_step * xp.maximum(c, 0.0), time_step * xp.maximum(-c, 0.0)]
    return [r * weights for r in rows], target, stencil


def selection():
    sel = np.zeros((26, MOM))
    own = np.zeros((26, MOM))
    for j in range(26):
        if j < 8:
            sel[j, FIELD_ROWS[j]] = 1
        elif j < 17:
            sel[j, OTHER_ROWS[j - 8]] = 1
            own[j, OTHER_ROWS[j - 8]] = -1
        elif j < 21:
            own[j, j - 16] = 1
        else:
            sel[j, j - 16] = 1
    eye = np.eye(X)
    sel = np.repeat(sel, X, 0)
    spread = np.tile(np.eye(MOM), (1, X))
    mask = np.repeat(np.tile(eye, (26, 1)), MOM, 1)
    fixed = np.einsum("jr,xp->jxpr", own, eye).reshape(26 * X, X * MOM)
    return [a.astype(np.float32) for a in (sel, spread, mask, fixed)]


def coupling_table():
    line = speed_range * (2.0 * np.arange(NVX) + 1.0 - NVX) / NVX
    cx, cy, cz = (a.reshape(-1) for a in np.meshgrid(line, line, line, indexing="ij"))
    rows, target, stencil = functions_of(cx, cy, cz, np)
    n = np.einsum("rv,ov,kv->ork", rows, stencil, target)
    near = np.zeros((X, MOM, 8, EXT))
    side = np.zeros((X, MOM, 4, 8, X))
    for x in range(X):
        near[x, :, :, x + HALO] += n[0]
        near[x, :, :, x + HALO - 1] += n[1]
        near[x, :, :, x + HALO + 1] += n[2]
        for j in range(4):
            side[x, :, j, :, x] += n[3 + j]
    table = np.concatenate([near.reshape(X * MOM, 8 * EXT), side.reshape(X * MOM, 32 * X)], 1)
    return table.astype(np.float32)


def split(a):
    hi = a.astype(BF16)
    return hi, (a - hi.astype(F32)).astype(BF16)


def cat(parts):
    return jnp.concatenate(parts, axis=1)


def tiles(x):
    return [x[:, 128 * i:128 * (i + 1)] for i in range(LT)]


def y_shifts(t):
    lane = lax.broadcasted_iota(jnp.int32, t[0].shape, 1)
    up = [pltpu.roll(a, 16, 1) for a in t]
    down = [pltpu.roll(a, 112, 1) for a in t]
    ylo = [jnp.where(lane < 16, up[i - 1], up[i]) for i in range(LT)]
    yhi = [jnp.where(lane >= 112, down[(i + 1) % LT], down[i]) for i in range(LT)]
    return ylo, yhi


def z_shifts(t):
    z = lax.broadcasted_iota(jnp.int32, t[0].shape, 1) % NZ
    zlo = [jnp.where(z == 0, pltpu.roll(a, 113, 1), pltpu.roll(a, 1, 1)) for a in t]
    zhi = [jnp.where(z == NZ - 1, pltpu.roll(a, 15, 1), pltpu.roll(a, 127, 1)) for a in t]
    return zlo, zhi


def yz_shifts(x):
    t = tiles(x)
    return (t,) + y_shifts(t) + z_shifts(t)


def stencil_moments(q_ref, p):
    def rows(o, at=p):
        return tiles(q_ref[at, 16 * o:16 * o + 16, :])

    ylo, _ = y_shifts(rows(3))
    _, yhi = y_shifts(rows(4))
    zlo, _ = z_shifts(rows(5))
    _, zhi = z_shifts(rows(6))
    here, before, after = rows(0), rows(1, p - 1), rows(2, p + 1)
    return cat([(here[i] + before[i] + after[i]) + (ylo[i] + yhi[i]) + (zlo[i] + zhi[i]) for i in range(LT)])


def alpha_of(relax, wall):
    return jnp.where(wall > 0, 0.0, 1.0 - relax)


def stream_plane(src, halves, p, h, ct, zmat, scale=None):
    lane = lax.broadcasted_iota(jnp.int32, (LV, 128), 1)
    k0, cx, cy, cz = (ct[i] for i in range(4))
    px, py, pz = cx > 0, cy > 0, cz > 0
    kx, ky, kz = jnp.abs(cx), jnp.abs(cy), jnp.abs(cz)
    t = [src[p, :, 128 * i:128 * (i + 1)] for i in range(LT)]
    z = [
        jnp.dot(
            cat([halves[h, 0:LV, 128 * i:128 * (i + 1)], halves[h, LV:2 * LV, 128 * i:128 * (i + 1)]]),
            zmat[...],
            preferred_element_type=F32,
        )
        for i in range(LT)
    ]
    up = [pltpu.roll(a, 16, 1) for a in t]
    down = [pltpu.roll(a, 112, 1) for a in t]
    out = []
    for i in range(LT):
        s = slice(128 * i, 128 * (i + 1))
        in_x = jnp.where(px, src[p - 1, :, s], src[p + 1, :, s])
        in_y = jnp.where(
            py,
            jnp.where(lane < 16, up[i - 1], up[i]),
            jnp.where(lane >= 112, down[(i + 1) % LT], down[i]),
        )
        in_z = jnp.where(pz, z[i][:, 0:128], z[i][:, 128:256])
        val = (k0 * t[i] + kx * in_x) + (ky * in_y + kz * in_z)
        out.append(val if scale is None else val * scale[:, s])
    return out


def exchange(dist_hbm, relax_ref, wall_ref, vel_ref, inv_ref, sel_ref, spread_ref, mask_ref, fixed_ref, nc,
             aa, g2_out, mac_out, norm_out,
             dbuf, dt, at_, dhl, ahl, q1, q2, mine, edges, from_left, from_right, rw, rwl, rwr,
             mrows, lm, ct, zmat, kx, pbuf, rsbuf, ssum, xbuf, total, fbuf, l1, h_out, h_left, h_right, b2out, b2_out, b2l, b2r,
             u, b, g1, rhs, lrows, lt, add, l2, nsend, nrecv, cin, cout, cfar, cboth, cnear,
             sem_ld, s_nb, r_nb, s_rs, r_rs, s_ag, r_ag, s_x, r_x, s_nm, r_nm, s_e, r_e):
    v = lax.axis_index("vel")
    s = lax.axis_index("space")
    left = (v, lax.rem(s + 3, 4))
    right = (v, lax.rem(s + 1, 4))
    far = v // PEERS
    place = lax.rem(v, PEERS)
    partner = ((1 - far) * PEERS + place, s)

    def peer(o):
        return (far * PEERS + o, s)

    loads = [pltpu.make_async_copy(dist_hbm.at[:, pl.ds(128 * t, 128)], dbuf.at[t], sem_ld.at[t]) for t in range(LT)]
    for c in loads:
        c.start()

    barrier = pltpu.get_barrier_semaphore()

    def greet(j, c):
        pl.semaphore_signal(barrier, inc=1, device_id=peer(lax.rem(place + j, PEERS)), device_id_type=MESH)
        return c

    lax.fori_loop(1, PEERS, greet, 0)
    pl.semaphore_signal(barrier, inc=1, device_id=partner, device_id_type=MESH)
    for j in (1, 2, 3):
        pl.semaphore_signal(barrier, inc=1, device_id=(v, lax.rem(s + j, 4)), device_id_type=MESH)

    rw[0:X, :] = relax_ref[...]
    rw[X:2 * X, :] = wall_ref[...].astype(F32)
    vel = speed_range * (2.0 * vel_ref[...].astype(F32) + 1.0 - NVX) / NVX
    cx, cy, cz = vel[0:1], vel[1:2], vel[2:3]
    rows, target, stencil = functions_of(cx, cy, cz)
    mrows[...] = jnp.zeros_like(mrows)
    for r in range(MOM):
        mrows[r:r + 1, :] = rows[r]
    for o in range(7):
        hi, lo = split(mrows[...] * stencil[o])
        lm[16 * o:16 * o + 16, 0:LV] = hi
        lm[16 * o:16 * o + 16, LV:2 * LV] = hi
        lm[112 + 16 * o:128 + 16 * o, 0:LV] = lo
        lm[112 + 16 * o:128 + 16 * o, LV:2 * LV] = jnp.zeros_like(lo)
    for i, row in enumerate((stencil[0], time_step * cx, time_step * cy, time_step * cz)):
        ct[i] = jnp.transpose(jnp.broadcast_to(row, (LV, LV)))
    for k in range(8):
        for o in range(7):
            lrows[8 * o + k:8 * o + k + 1, :] = stencil[o] * target[k]
    hi, lo = split(lrows[...])
    hi, lo = hi.astype(F32), lo.astype(F32)
    quad = jnp.concatenate([hi, hi, lo, lo, jnp.zeros((32, LV), F32)], 0)
    lt[:, 0:128] = jnp.transpose(quad[0:128]).astype(BF16)
    lt[:, 128:224] = jnp.transpose(quad[128:256])[:, 0:96].astype(BF16)
    src_lane = lax.broadcasted_iota(jnp.int32, (LV, LV), 0)
    dst_lane = lax.broadcasted_iota(jnp.int32, (LV, LV), 1)
    dst_z = dst_lane % NZ
    lower = jnp.where(src_lane == jnp.where(dst_z == 0, dst_lane + NZ - 1, dst_lane - 1), 1.0, 0.0).astype(BF16)
    upper = jnp.where(src_lane == jnp.where(dst_z == NZ - 1, dst_lane - NZ + 1, dst_lane + 1), 1.0, 0.0).astype(BF16)
    for i in range(2):
        zmat[LV * i:LV * (i + 1), 0:LV] = lower
        zmat[LV * i:LV * (i + 1), LV:2 * LV] = upper
    part = jnp.dot(sel_ref[...], inv_ref[...], precision=HIGHEST, preferred_element_type=F32)
    part = jnp.dot(part, spread_ref[...], precision=HIGHEST, preferred_element_type=F32)
    kx[...] = part * mask_ref[...] + fixed_ref[...]
    zero_plane = jnp.zeros((LV, CELLS), F32)
    for p in (0, 9):
        dt[p] = zero_plane
        q1[p, 16:48, :] = jnp.zeros((32, CELLS), F32)
    for p in (0, 11):
        at_[p] = zero_plane
    for m in range(2):
        pbuf[m, 104:112, :] = jnp.zeros((8, CELLS), F32)

    def swap(i, to_right, right_dst, to_left, left_dst):
        a = pltpu.make_async_remote_copy(to_right, right_dst, s_nb.at[2 * i], r_nb.at[2 * i],
                                         device_id=right, device_id_type=MESH)
        c = pltpu.make_async_remote_copy(to_left, left_dst, s_nb.at[2 * i + 1], r_nb.at[2 * i + 1],
                                         device_id=left, device_id_type=MESH)
        a.start()
        c.start()
        return a, c

    def settle(copies):
        for c in copies:
            c.wait()

    settle(loads)

    def first(x, c):
        val = cat([dbuf[t, pl.ds(x, LV, stride=X), :] for t in range(LT)])
        dt[x + 1] = val
        hi, lo = split(val)
        dhl[x, 0:LV, :] = hi
        dhl[x, LV:2 * LV, :] = lo
        q = jnp.dot(lm[...], dhl[x], preferred_element_type=F32)
        q1[x + 1] = q[0:112] + q[112:224]
        return c

    lax.fori_loop(0, X, first, 0)
    pl.semaphore_wait(barrier, PEERS - 1 + 1 + 3)
    halo = swap(0, rw, rwl, rw, rwr)
    edges[0, 0:16, :] = q1[1, 32:48, :]
    edges[1, 0:16, :] = q1[X, 16:32, :]
    outer1 = swap(1, edges.at[1, pl.ds(0, 16)], from_left.at[pl.ds(0, 16)],
                  edges.at[0, pl.ds(0, 16)], from_right.at[pl.ds(0, 16)])

    def sum_first(x, c):
        mine[0, x] = stencil_moments(q1, x + 1)
        return c

    lax.fori_loop(0, X, sum_first, 0)

    def alpha_row(ref, x):
        return alpha_of(ref[pl.ds(x, 1), :], ref[pl.ds(x + X, 1), :])

    def products(i):
        hi, lo = split(at_[i + 1])
        ahl[i, 0:LV, :] = hi
        ahl[i, LV:2 * LV, :] = lo
        q = jnp.dot(lm[...], ahl[i], preferred_element_type=F32)
        q2[i] = q[0:112] + q[112:224]

    def second(j, c):
        x = lax.rem(X - j, X)

        val = stream_plane(dt, dhl, x + 1, x, ct, zmat, alpha_row(rw, x))
        for i in range(LT):
            at_[x + 2, :, 128 * i:128 * (i + 1)] = val[i]
        products(x + 1)
        return c

    def third(i):
        val = stream_plane(at_, ahl, i + 1, i, ct, zmat)
        for t in range(LT):
            aa[i + 1, :, 128 * t:128 * (t + 1)] = val[t]

    lax.fori_loop(0, 2, second, 0)
    settle(outer1)
    mine[0, 0] += from_left[0:16, :]
    mine[0, X - 1] += from_right[0:16, :]

    def pack(m):
        for x in range(X):
            pbuf[m, 13 * x:13 * x + 13, :] = mine[m, x, 0:13, :]

    def chunk_of(o):
        return (pl.ds(pl.multiple_of(CH * (o // LT), 8), CH), pl.ds(pl.multiple_of(128 * lax.rem(o, LT), 128), 128))

    def send_parts(m):
        def send(j, c):
            o = lax.rem(place + j, PEERS)
            r, k = chunk_of(o)
            pltpu.make_async_remote_copy(pbuf.at[m, r, k], rsbuf.at[m, j], s_rs.at[m], r_rs.at[m],
                                         device_id=peer(o), device_id_type=MESH).start()
            return c

        lax.fori_loop(1, PEERS, send, 0)

    def all_parts(m):
        return rsbuf.at[m, pl.ds(1, PEERS - 1)]

    def across(m):
        return pltpu.make_async_remote_copy(ssum.at[m], xbuf.at[m], s_x.at[m], r_x.at[m],
                                            device_id=partner, device_id_type=MESH)

    def own_sum(m):
        pltpu.make_async_copy(all_parts(m), all_parts(m), r_rs.at[m]).wait()
        r, k = chunk_of(place)
        acc = pbuf[m, r, k]
        for j in range(1, PEERS):
            acc = acc + rsbuf[m, j]
        ssum[m] = acc
        across(m).start()

    def send_total(m):
        across(m).wait()
        val = ssum[m] + xbuf[m]
        total[m] = val
        r, k = chunk_of(place)
        fbuf[m, r, k] = val

        def send(j, c):
            pltpu.make_async_remote_copy(total.at[m], fbuf.at[m, r, k], s_ag.at[m], r_ag.at[m],
                                         device_id=peer(lax.rem(place + j, PEERS)), device_id_type=MESH).start()
            return c

        lax.fori_loop(1, PEERS, send, 0)

    def all_totals(m):
        pltpu.make_async_copy(all_parts(m), all_parts(m), r_ag.at[m]).wait()

    def all_sent(m):
        pltpu.make_async_copy(all_parts(m), all_parts(m), s_rs.at[m]).wait()
        pltpu.make_async_copy(all_parts(m), all_parts(m), s_ag.at[m]).wait()

    pack(0)
    send_parts(0)
    lax.fori_loop(2, X, second, 0)

    settle(halo)
    speed = ct[1]
    to_lower = jnp.where(speed > 0, 0.0, -speed)
    to_upper = jnp.where(speed > 0, speed, 0.0)
    al_l, al_r = alpha_row(rwl, X - 1), alpha_row(rwr, 0)
    for i in range(LT):
        c = slice(128 * i, 128 * (i + 1))
        at_[1, :, c] = to_lower * dt[1, :, c] * al_l[:, c]
        at_[X + 2, :, c] = to_upper * dt[X, :, c] * al_r[:, c]

    def ends(j, c):
        products((X + 1) * j)
        return c

    lax.fori_loop(0, 2, ends, 0)

    edges[0, 16:32, :] = stencil_edge(q2, 0) + q2[1, 32:48, :]
    edges[0, 32:48, :] = q2[0, 32:48, :]
    edges[1, 16:32, :] = stencil_edge(q2, X + 1) + q2[X, 16:32, :]
    edges[1, 32:48, :] = q2[X + 1, 16:32, :]
    outer2 = swap(2, edges.at[1, pl.ds(16, 32)], from_left.at[pl.ds(16, 32)],
                  edges.at[0, pl.ds(16, 32)], from_right.at[pl.ds(16, 32)])
    own_sum(0)

    def sum_second(x, c):
        mine[1, x] = stencil_moments(q2, x + 1)
        return c

    lax.fori_loop(0, X, sum_second, 0)

    def edge_third(j, c):
        third((X + 1) * j)
        return c

    lax.fori_loop(0, 2, edge_third, 0)
    for i in range(LT):
        c = slice(128 * i, 128 * (i + 1))
        aa[0, :, c] = to_lower * at_[1, :, c]
        aa[X + 3, :, c] = to_upper * at_[X + 2, :, c]
    send_total(0)
    settle(outer2)
    mine[1, 0] += from_left[16:32, :]
    mine[1, 1] += from_left[32:48, :]
    mine[1, X - 1] += from_right[16:32, :]
    mine[1, X - 2] += from_right[32:48, :]
    pack(1)
    send_parts(1)

    core = lax.rem(s, 2)
    mate = (v, s + 1 - 2 * core)
    over = (v, lax.rem(s + 2, 4))
    half = LV // 2
    mine_v = pl.ds(pl.multiple_of(half * core, 8), half)
    mate_v = pl.ds(pl.multiple_of(half * (1 - core), 8), half)
    out_end = pl.ds((X + 2) * core, 2)
    in_end = pl.ds((X + 2) * (1 - core), 2)

    def hand(i, src, dst, to):
        c = pltpu.make_async_remote_copy(src, dst, s_e.at[i], r_e.at[i], device_id=to, device_id_type=MESH)
        c.start()
        return c

    give = hand(0, aa.at[out_end, mate_v], cin, mate)
    near = hand(1, aa.at[in_end], cnear, mate)

    def inner_third(i, c):
        third(i)
        return c

    lax.fori_loop(1, 3, inner_third, 0)
    give.wait()
    cout[...] = aa[out_end, mine_v, :] + cin[...]
    over_0 = hand(2, cout.at[0], cfar.at[0], over)
    lax.fori_loop(3, 7, inner_third, 0)

    all_totals(0)
    l1[...] = jnp.dot(kx[...], fbuf[0, 0:104, :], precision=HIGHEST, preferred_element_type=F32)
    for k in range(8):
        h_out[0, HALO * k:HALO * (k + 1), :] = l1[8 * k:8 * k + HALO, :]
        h_out[1, HALO * k:HALO * (k + 1), :] = l1[8 * k + X - HALO:8 * k + X, :]
    halo2 = swap(3, h_out.at[1], h_left, h_out.at[0], h_right)
    own_sum(1)
    lax.fori_loop(7, X + 1, inner_third, 0)
    send_total(1)
    over_1 = hand(3, cout.at[1], cfar.at[1], over)
    settle(halo2)

    zero8 = jnp.zeros((8, CELLS), F32)

    def clear_ends(k, c):
        for i in range(2):
            u[i, k, 0:8, :] = zero8
            u[i, k, 24:32, :] = zero8
        return c

    lax.fori_loop(0, 4, clear_ends, 0)

    def fill(k, lo_rows, own, hi_rows):
        b[k, 0:HALO, :] = lo_rows
        b[k, HALO:HALO + X, :] = own
        b[k, HALO + X:EXT, :] = hi_rows

    def smooth():
        def start(k, c):
            u[0, k, 8:24, :] = b[k]
            return c

        lax.fori_loop(0, 4, start, 0)
        for sweep in range(SWEEPS):
            src, dst = sweep % 2, 1 - sweep % 2

            def row(k, c):
                for blk in range(2):
                    lo = 8 + 8 * blk
                    here, ylo, yhi, zlo, zhi = yz_shifts(u[src, k, lo:lo + 8, :])
                    near = u[src, k, lo - 1:lo + 7, :] + u[src, k, lo + 1:lo + 9, :]
                    side = cat([(ylo[i] + yhi[i]) + (zlo[i] + zhi[i]) for i in range(LT)])
                    u[dst, k, lo:lo + 8, :] = (b[k, 8 * blk:8 * blk + 8, :] + coupling * (near + side)) * (1.0 / (1.0 + 6.0 * coupling))
                return c

            lax.fori_loop(0, 4, row, 0)
        return SWEEPS % 2

    for k in range(4):
        fill(k, h_left[4 * k:4 * k + 4, :], l1[8 * k:8 * k + 8, :], h_right[4 * k:4 * k + 4, :])
    last = smooth()

    def gammas(relax, wall):
        return jnp.where(wall > 0, 0.0, relax), jnp.where(wall > 0, 1.0, relax)

    own_alpha = alpha_of(rw[0:X, :], rw[X:2 * X, :])
    factors = [gammas(ref[0:X, :], ref[X:2 * X, :]) for ref in (rwl, rw, rwr)]
    for k in range(8):
        gl, go, gr = (f[1 if k in (3, 4) else 0] for f in factors)
        if k < 4:
            lo_rows = u[last, k, 8:8 + HALO, :]
            own = u[last, k, 8 + HALO:8 + HALO + X, :]
            hi_rows = u[last, k, 8 + HALO + X:8 + EXT, :]
        else:
            lo_rows = h_left[4 * k:4 * k + 4, :]
            own = l1[8 * k:8 * k + 8, :]
            hi_rows = h_right[4 * k:4 * k + 4, :]
        own = own * go
        g1[EXT * k:EXT * k + HALO, :] = lo_rows * gl[4:8]
        g1[EXT * k + HALO:EXT * k + HALO + X, :] = own
        g1[EXT * k + HALO + X:EXT * (k + 1), :] = hi_rows * gr[0:4]
        here, ylo, yhi, zlo, zhi = yz_shifts(own)
        for j, val in enumerate((ylo, yhi, zlo, zhi)):
            rhs[64 * j + 8 * k:64 * j + 8 * k + 8, :] = cat(val)
        at = EXT * k + HALO
        before = tiles(g1[at - 1:at + 7, :])
        after = tiles(g1[at + 1:at + 9, :])
        for t in range(LT):
            al = own_alpha[:, 128 * t:128 * (t + 1)]
            for o, val in enumerate((here, before, after, ylo, yhi, zlo, zhi)):
                dbuf[t, 64 * o + 8 * k:64 * o + 8 * k + 8, :] = val[t] * al

    def squares(l, sm):
        acc = jnp.zeros((8, CELLS), F32)
        for i in range(9):
            d = l[64 + 8 * i:72 + 8 * i, :]
            acc = acc + d * d
        for k in range(4):
            d = u[sm, k, 8 + HALO:8 + HALO + X, :] - l[136 + 8 * k:144 + 8 * k, :]
            acc = acc + d * d
        parts = tiles(acc)
        out = parts[0]
        for i in range(1, LT):
            out = out + parts[i]
        return out

    nsend[0] = squares(l1, last)

    add[...] = (
        jnp.dot(nc[:, 0:128], g1[...], precision=HIGHEST, preferred_element_type=F32)
        + jnp.dot(nc[:, 128:384], rhs[...], precision=HIGHEST, preferred_element_type=F32)
    )

    def spread(x, c):
        for t in range(LT):
            hi, lo = split(dbuf[t, pl.ds(x, 56, stride=X), :])
            both_parts = jnp.concatenate([hi.astype(F32), lo.astype(F32)], 0).astype(BF16)
            cols = slice(128 * t, 128 * (t + 1))
            dhl[x, 0:112, cols] = both_parts
            dhl[x, 112:224, cols] = both_parts
        return c

    lax.fori_loop(0, X, spread, 0)
    over_0.wait()
    over_1.wait()
    share = hand(4, cfar, cboth, mate)
    all_totals(1)
    m2 = fbuf[1, 0:104, :] + add[...]
    b2out[...] = jnp.dot(kx[0:32, :], m2, precision=HIGHEST, preferred_element_type=F32)
    for k in range(4):
        b2_out[0, HALO * k:HALO * (k + 1), :] = b2out[8 * k:8 * k + HALO, :]
        b2_out[1, HALO * k:HALO * (k + 1), :] = b2out[8 * k + X - HALO:8 * k + X, :]
    halo3 = swap(6, b2_out.at[1], b2l, b2_out.at[0], b2r)
    l2[...] = jnp.dot(kx[32:208, :], m2, precision=HIGHEST, preferred_element_type=F32)

    def combine(x):
        aa[x + 2] = jnp.dot(lt[...], dhl[x, 0:224, :], preferred_element_type=F32) + alpha_row(rw, x) * aa[x + 2]

    def middle(x, c):
        combine(x)
        return c

    lax.fori_loop(2, X - 2, middle, 0)
    settle(halo3)
    for k in range(4):
        fill(k, b2l[4 * k:4 * k + 4, :], b2out[8 * k:8 * k + 8, :], b2r[4 * k:4 * k + 4, :])
    last = smooth()
    acc = jnp.zeros((8, CELLS), F32)
    for i in range(9):
        d = l2[32 + 8 * i:40 + 8 * i, :]
        acc = acc + d * d
    for k in range(4):
        d = u[last, k, 8 + HALO:8 + HALO + X, :] - l2[104 + 8 * k:112 + 8 * k, :]
        acc = acc + d * d
    parts = tiles(acc)
    out = parts[0]
    for i in range(1, LT):
        out = out + parts[i]
    nsend[1] = out
    notes = []
    for j in (1, 2, 3):
        c = pltpu.make_async_remote_copy(nsend, nrecv.at[j - 1], s_nm.at[j - 1], r_nm.at[j - 1],
                                         device_id=(v, lax.rem(s + j, 4)), device_id_type=MESH)
        c.start()
        notes.append(c)

    beta, both = gammas(rw[0:X, :], rw[X:2 * X, :])
    for k in range(8):
        f = u[last, k, 8 + HALO:8 + HALO + X, :] if k < 4 else l2[8 * k - 32:8 * k - 24, :]
        g2_out[8 * k:8 * k + 8, :] = f * (both if k in (3, 4) else beta)

    tile = pl.ds(pl.multiple_of(128 * (v // 4), 128), 128)
    turn = lax.rem(128 - 32 * lax.rem(v, 4), 128)
    for r in range(MOM):
        if 1 <= r <= 4:
            f = u[last, r - 1, 8 + HALO:8 + HALO + X, tile]
        elif r == 0:
            f = l2[0:8, tile]
        elif r >= 10:
            f = l2[8 + 8 * (r - 10):16 + 8 * (r - 10), tile]
        else:
            f = l2[136 + 8 * (r - 5):144 + 8 * (r - 5), tile]
        mac_out[r] = pltpu.roll(f, turn, 1)[:, 0:32]

    near.wait()
    share.wait()
    is_upper = (core == 0).astype(F32)
    from_far = 2 + (X - 2) * core
    from_near = 2 + (X - 2) * (1 - core)

    def add_ends(i, carry):
        for t in range(LT):
            c = slice(128 * t, 128 * (t + 1))
            aa[from_near + i, :, c] += cnear[i, :, c]
            aa[from_far + i, mine_v, c] += jnp.where(wanted_of(mine_v) > 0, cfar[i, :, c], 0.0)
            aa[from_far + i, mate_v, c] += jnp.where(wanted_of(mate_v) > 0, cboth[i, :, c], 0.0)
        return carry

    def wanted_of(rows):
        towards = ct[1, rows, :]
        return jnp.where(towards > 0, is_upper, 1.0 - is_upper)

    lax.fori_loop(0, 2, add_ends, 0)

    def outside(j, c):
        combine(lax.rem(j + X - 2, X))
        return c

    lax.fori_loop(0, 4, outside, 0)

    settle(notes)
    for i in range(2):
        norm_out[i] = (nsend[i] + nrecv[0, i]) + (nrecv[1, i] + nrecv[2, i])
    for m in range(2):
        all_sent(m)


def stencil_edge(q_ref, p):
    def rows(o):
        return tiles(q_ref[p, 16 * o:16 * o + 16, :])

    ylo, _ = y_shifts(rows(3))
    _, yhi = y_shifts(rows(4))
    zlo, _ = z_shifts(rows(5))
    _, zhi = z_shifts(rows(6))
    here = rows(0)
    return cat([here[i] + (ylo[i] + yhi[i]) + (zlo[i] + zhi[i]) for i in range(LT)])


PAIRS = 4


def renew(a_ref, g2_ref, vel_ref, mac_ref, sum_ref, out_hbm, mac_out, norm_out, obuf, stage, rhs, lt, sem_out):
    mac_out[...] = mac_ref[...]
    for i in range(2):
        norm_out[i] = jnp.sqrt(jnp.sum(sum_ref[i]))

    vel = speed_range * (2.0 * vel_ref[...].astype(F32) + 1.0 - NVX) / NVX
    _, target, _ = functions_of(vel[0:1], vel[1:2], vel[2:3])
    for k in range(8):
        stage[0, k:k + 1, :] = target[k]
    hi, lo = split(stage[0, 0:8, :])
    hi, lo = hi.astype(F32), lo.astype(F32)
    quad = jnp.concatenate([hi, hi, lo, lo, jnp.zeros((96, LV), F32)], 0)
    lt[...] = jnp.transpose(quad)[:, 0:32].astype(BF16)

    for t in range(LT):
        stage[t] = g2_ref[:, 128 * t:128 * (t + 1)]

    def spread(x, c):
        for t in range(LT):
            hi, lo = split(stage[t, pl.ds(x, 8, stride=X), :])
            both_parts = jnp.concatenate([hi.astype(F32), lo.astype(F32)], 0).astype(BF16)
            cols = slice(128 * t, 128 * (t + 1))
            rhs[x, 0:16, cols] = both_parts
            rhs[x, 16:32, cols] = both_parts
        return c

    lax.fori_loop(0, X, spread, 0)

    puts = []
    for i in range(PAIRS):
        pair = slice(256 * i, 256 * (i + 1))

        def plane(x, c):
            val = jnp.dot(lt[...], rhs[x, :, pair], preferred_element_type=F32) + a_ref[x + 2, :, pair]
            obuf[2 * i, pl.ds(x, LV, stride=X), :] = val[:, 0:128]
            obuf[2 * i + 1, pl.ds(x, LV, stride=X), :] = val[:, 128:256]
            return c

        lax.fori_loop(0, X, plane, 0)
        for t in (2 * i, 2 * i + 1):
            c = pltpu.make_async_copy(obuf.at[t], out_hbm.at[:, pl.ds(128 * t, 128)], sem_out.at[t])
            c.start()
            puts.append(c)
    for c in puts:
        c.wait()


def shards(consts, dist, vel_index, relax, wall_mask, macro_inverse):
    vmem = pl.BlockSpec(memory_space=pltpu.VMEM)
    hbm = pl.BlockSpec(memory_space=pl.ANY)
    smem = pl.BlockSpec(memory_space=pltpu.SMEM)
    dma = pltpu.SemaphoreType.DMA
    sds = jax.ShapeDtypeStruct
    a, g2, mac, norm = pl.pallas_call(
        exchange,
        out_shape=(
            pltpu.VMEM((X + 4, LV, CELLS), F32), pltpu.VMEM((64, CELLS), F32),
            pltpu.VMEM((MOM, X, 32), F32), pltpu.VMEM((2, 8, 128), F32),
        ),
        in_specs=[hbm] + [vmem] * 9,
        out_specs=(vmem,) * 4,
        scratch_shapes=[
            pltpu.VMEM((LT, LV * X, 128), F32),
            pltpu.VMEM((X + 2, LV, CELLS), F32),
            pltpu.VMEM((X + 4, LV, CELLS), F32),
            pltpu.VMEM((X, 2 * LV, CELLS), BF16),
            pltpu.VMEM((X + 2, 2 * LV, CELLS), BF16),
            pltpu.VMEM((X + 2, 112, CELLS), F32),
            pltpu.VMEM((X + 2, 112, CELLS), F32),
            pltpu.VMEM((2, X, 16, CELLS), F32),
            pltpu.VMEM((2, 48, CELLS), F32),
            pltpu.VMEM((48, CELLS), F32),
            pltpu.VMEM((48, CELLS), F32),
            pltpu.VMEM((2 * X, CELLS), F32),
            pltpu.VMEM((2 * X, CELLS), F32),
            pltpu.VMEM((2 * X, CELLS), F32),
            pltpu.VMEM((16, LV), F32),
            pltpu.VMEM((224, 2 * LV), BF16),
            pltpu.VMEM((4, LV, LV), F32),
            pltpu.VMEM((2 * LV, 2 * LV), BF16),
            pltpu.VMEM((26 * X, X * MOM), F32),
            pltpu.VMEM((2, 2 * CH, CELLS), F32),
            pltpu.VMEM((2, PEERS, CH, 128), F32),
            pltpu.VMEM((2, CH, 128), F32),
            pltpu.VMEM((2, CH, 128), F32),
            pltpu.VMEM((2, CH, 128), F32),
            pltpu.VMEM((2, 2 * CH, CELLS), F32),
            pltpu.VMEM((26 * X, CELLS), F32),
            pltpu.VMEM((2, 32, CELLS), F32),
            pltpu.VMEM((32, CELLS), F32),
            pltpu.VMEM((32, CELLS), F32),
            pltpu.VMEM((32, CELLS), F32),
            pltpu.VMEM((2, 16, CELLS), F32),
            pltpu.VMEM((16, CELLS), F32),
            pltpu.VMEM((16, CELLS), F32),
            pltpu.VMEM((2, 4, 32, CELLS), F32),
            pltpu.VMEM((4, EXT, CELLS), F32),
            pltpu.VMEM((8 * EXT, CELLS), F32),
            pltpu.VMEM((256, CELLS), F32),
            pltpu.VMEM((56, LV), F32),
            pltpu.VMEM((LV, 224), BF16),
            pltpu.VMEM((X * MOM, CELLS), F32),
            pltpu.VMEM((22 * X, CELLS), F32),
            pltpu.VMEM((2, 8, 128), F32),
            pltpu.VMEM((3, 2, 8, 128), F32),
            pltpu.VMEM((2, LV // 2, CELLS), F32),
            pltpu.VMEM((2, LV // 2, CELLS), F32),
            pltpu.VMEM((2, LV // 2, CELLS), F32),
            pltpu.VMEM((2, LV // 2, CELLS), F32),
            pltpu.VMEM((2, LV, CELLS), F32),
            dma((LT,)), dma((14,)), dma((14,)), dma((2,)), dma((2,)), dma((2,)), dma((2,)), dma((2,)), dma((2,)),
            dma((3,)), dma((3,)), dma((5,)), dma((5,)),
        ],
        compiler_params=pltpu.CompilerParams(collective_id=0, has_side_effects=True, vmem_limit_bytes=54 * 2 ** 20),
        name="exchange",
    )(dist.reshape(LV * X, CELLS), relax, wall_mask, vel_index, macro_inverse, *consts)

    out, mac, norm = pl.pallas_call(
        renew,
        out_shape=(sds((LV * X, CELLS), F32), sds((MOM, X, 32), F32), sds((2,), F32)),
        in_specs=[vmem] * 5,
        out_specs=(hbm, vmem, smem),
        scratch_shapes=[
            pltpu.VMEM((LT, LV * X, 128), F32),
            pltpu.VMEM((LT, 64, 128), F32),
            pltpu.VMEM((X, 32, CELLS), BF16),
            pltpu.VMEM((LV, 32), BF16),
            dma((LT,)),
        ],
        compiler_params=pltpu.CompilerParams(vmem_limit_bytes=32 * 2 ** 20),
        name="renew",
    )(a, g2, vel_index, mac, norm)
    return (out.reshape(LV, X, CELLS), mac, norm)


def solution(mesh):
    consts = selection() + [coupling_table()]
    return jax.shard_map(
        lambda *args: shards([jnp.asarray(c) for c in consts], *args),
        mesh=mesh,
        in_specs=(P("vel", "space", None), P(None, "vel"), P("space", None), P("space", None), P()),
        out_specs=(P("vel", "space", None), P(None, "space", "vel"), P()),
        check_vma=False,
    )
```

```python
import functools
import math

import jax
import jax.numpy as jnp
import numpy as np
from jax import lax
from jax.experimental import pallas as pl
from jax.experimental.pallas import tpu as pltpu
from jax.sharding import PartitionSpec as P

NVX = 16
NZ = 16
MOM = 13
SWEEPS = 3
speed_range = 4.0
time_step = 0.08
coupling = 0.5

MESH = pl.DeviceIdType.MESH
F32 = jnp.float32
BF16 = jnp.bfloat16
X = 8
CELLS = 1024
LT = CELLS // 128
RING = 4
PEERS = RING * RING
LV = 128
CH = 56
HALO = 4
EXT = X + 2 * HALO
FIELD_ROWS = (1, 2, 3, 4, 0, 10, 11, 12)
OTHER_ROWS = (0, 5, 6, 7, 8, 9, 10, 11, 12)
HIGHEST = lax.Precision.HIGHEST


def functions_of(cx, cy, cz, xp=jnp):
    square = cx * cx + cy * cy + cz * cz
    weights = (2.0 * speed_range / NVX) ** 3 * math.pi ** (-1.5) * xp.exp(-square)
    heat = square - 2.5
    one = xp.ones_like(cx)
    rows = [
        one, cx, cy, cz, 2.0 * square / 3.0 - 1.0,
        2.0 * cx * cy, 2.0 * cx * cz, 2.0 * cy * cz,
        cx * cx - cy * cy, cy * cy - cz * cz,
        cx * heat, cy * heat, cz * heat,
    ]
    factor = 4.0 / 15.0
    target = [2.0 * cx, 2.0 * cy, 2.0 * cz, square - 1.5, one, factor * cx * heat, factor * cy * heat, factor * cz * heat]
    stencil = [1.0 - time_step * (xp.abs(cx) + xp.abs(cy) + xp.abs(cz))]
    for c in (cx, cy, cz):
        stencil += [time_step * xp.maximum(c, 0.0), time_step * xp.maximum(-c, 0.0)]
    return [r * weights for r in rows], target, stencil


def selection():
    sel = np.zeros((26, MOM))
    own = np.zeros((26, MOM))
    for j in range(26):
        if j < 8:
            sel[j, FIELD_ROWS[j]] = 1
        elif j < 17:
            sel[j, OTHER_ROWS[j - 8]] = 1
            own[j, OTHER_ROWS[j - 8]] = -1
        elif j < 21:
            own[j, j - 16] = 1
        else:
            sel[j, j - 16] = 1
    eye = np.eye(X)
    sel = np.repeat(sel, X, 0)
    spread = np.tile(np.eye(MOM), (1, X))
    mask = np.repeat(np.tile(eye, (26, 1)), MOM, 1)
    fixed = np.einsum("jr,xp->jxpr", own, eye).reshape(26 * X, X * MOM)
    return [a.astype(np.float32) for a in (sel, spread, mask, fixed)]


def coupling_table():
    line = speed_range * (2.0 * np.arange(NVX) + 1.0 - NVX) / NVX
    cx, cy, cz = (a.reshape(-1) for a in np.meshgrid(line, line, line, indexing="ij"))
    rows, target, stencil = functions_of(cx, cy, cz, np)
    n = np.einsum("rv,ov,kv->ork", rows, stencil, target)
    near = np.zeros((X, MOM, 8, EXT))
    side = np.zeros((X, MOM, 4, 8, X))
    for x in range(X):
        near[x, :, :, x + HALO] += n[0]
        near[x, :, :, x + HALO - 1] += n[1]
        near[x, :, :, x + HALO + 1] += n[2]
        for j in range(4):
            side[x, :, j, :, x] += n[3 + j]
    table = np.concatenate([near.reshape(X * MOM, 8 * EXT), side.reshape(X * MOM, 32 * X)], 1)
    return table.astype(np.float32)


def split(a):
    hi = a.astype(BF16)
    return hi, (a - hi.astype(F32)).astype(BF16)


def cat(parts):
    return jnp.concatenate(parts, axis=1)


def tiles(x):
    return [x[:, 128 * i:128 * (i + 1)] for i in range(LT)]


def y_shifts(t):
    lane = lax.broadcasted_iota(jnp.int32, t[0].shape, 1)
    up = [pltpu.roll(a, 16, 1) for a in t]
    down = [pltpu.roll(a, 112, 1) for a in t]
    ylo = [jnp.where(lane < 16, up[i - 1], up[i]) for i in range(LT)]
    yhi = [jnp.where(lane >= 112, down[(i + 1) % LT], down[i]) for i in range(LT)]
    return ylo, yhi


def z_shifts(t):
    z = lax.broadcasted_iota(jnp.int32, t[0].shape, 1) % NZ
    zlo = [jnp.where(z == 0, pltpu.roll(a, 113, 1), pltpu.roll(a, 1, 1)) for a in t]
    zhi = [jnp.where(z == NZ - 1, pltpu.roll(a, 15, 1), pltpu.roll(a, 127, 1)) for a in t]
    return zlo, zhi


def yz_shifts(x):
    t = tiles(x)
    return (t,) + y_shifts(t) + z_shifts(t)


def stencil_moments(q_ref, p):
    def rows(o, at=p):
        return tiles(q_ref[at, 16 * o:16 * o + 16, :])

    ylo, _ = y_shifts(rows(3))
    _, yhi = y_shifts(rows(4))
    zlo, _ = z_shifts(rows(5))
    _, zhi = z_shifts(rows(6))
    here, before, after = rows(0), rows(1, p - 1), rows(2, p + 1)
    return cat([(here[i] + before[i] + after[i]) + (ylo[i] + yhi[i]) + (zlo[i] + zhi[i]) for i in range(LT)])


def alpha_of(relax, wall):
    return jnp.where(wall > 0, 0.0, 1.0 - relax)


def stream_plane(src, halves, p, h, ct, zmat, scale=None):
    lane = lax.broadcasted_iota(jnp.int32, (LV, 128), 1)
    k0, cx, cy, cz = (ct[i] for i in range(4))
    px, py, pz = cx > 0, cy > 0, cz > 0
    kx, ky, kz = jnp.abs(cx), jnp.abs(cy), jnp.abs(cz)
    t = [src[p, :, 128 * i:128 * (i + 1)] for i in range(LT)]
    z = [
        jnp.dot(
            cat([halves[h, 0:LV, 128 * i:128 * (i + 1)], halves[h, LV:2 * LV, 128 * i:128 * (i + 1)]]),
            zmat[...],
            preferred_element_type=F32,
        )
        for i in range(LT)
    ]
    up = [pltpu.roll(a, 16, 1) for a in t]
    down = [pltpu.roll(a, 112, 1) for a in t]
    out = []
    for i in range(LT):
        s = slice(128 * i, 128 * (i + 1))
        in_x = jnp.where(px, src[p - 1, :, s], src[p + 1, :, s])
        in_y = jnp.where(
            py,
            jnp.where(lane < 16, up[i - 1], up[i]),
            jnp.where(lane >= 112, down[(i + 1) % LT], down[i]),
        )
        in_z = jnp.where(pz, z[i][:, 0:128], z[i][:, 128:256])
        val = (k0 * t[i] + kx * in_x) + (ky * in_y + kz * in_z)
        out.append(val if scale is None else val * scale[:, s])
    return out


def exchange(dist_hbm, relax_ref, wall_ref, vel_ref, inv_ref, sel_ref, spread_ref, mask_ref, fixed_ref, nc,
             aa, g2_out, mac_out, norm_out,
             dbuf, dt, at_, dhl, ahl, q1, q2, mine, edges, from_left, from_right, rw, rwl, rwr,
             mrows, lm, ct, zmat, kx, pbuf, rsbuf, ssum, xbuf, total, fbuf, l1, h_out, h_left, h_right, b2out, b2_out, b2l, b2r,
             u, b, g1, rhs, lrows, lt, add, l2, nsend, nrecv, cin, cout, cfar, cboth, cnear,
             sem_ld, s_nb, r_nb, s_rs, r_rs, s_ag, r_ag, s_x, r_x, s_nm, r_nm, s_e, r_e):
    v = lax.axis_index("vel")
    s = lax.axis_index("space")
    left = (v, lax.rem(s + 3, 4))
    right = (v, lax.rem(s + 1, 4))
    far = v // PEERS
    place = lax.rem(v, PEERS)
    partner = ((1 - far) * PEERS + place, s)

    def peer(o):
        return (far * PEERS + o, s)

    loads = [pltpu.make_async_copy(dist_hbm.at[:, pl.ds(128 * t, 128)], dbuf.at[t], sem_ld.at[t]) for t in range(LT)]
    for c in loads:
        c.start()

    barrier = pltpu.get_barrier_semaphore()

    def greet(j, c):
        pl.semaphore_signal(barrier, inc=1, device_id=peer(lax.rem(place + j, PEERS)), device_id_type=MESH)
        return c

    lax.fori_loop(1, PEERS, greet, 0)
    pl.semaphore_signal(barrier, inc=1, device_id=partner, device_id_type=MESH)
    for j in (1, 2, 3):
        pl.semaphore_signal(barrier, inc=1, device_id=(v, lax.rem(s + j, 4)), device_id_type=MESH)

    rw[0:X, :] = relax_ref[...]
    rw[X:2 * X, :] = wall_ref[...].astype(F32)
    vel = speed_range * (2.0 * vel_ref[...].astype(F32) + 1.0 - NVX) / NVX
    cx, cy, cz = vel[0:1], vel[1:2], vel[2:3]
    rows, target, stencil = functions_of(cx, cy, cz)
    mrows[...] = jnp.zeros_like(mrows)
    for r in range(MOM):
        mrows[r:r + 1, :] = rows[r]
    for o in range(7):
        hi, lo = split(mrows[...] * stencil[o])
        lm[16 * o:16 * o + 16, 0:LV] = hi
        lm[16 * o:16 * o + 16, LV:2 * LV] = hi
        lm[112 + 16 * o:128 + 16 * o, 0:LV] = lo
        lm[112 + 16 * o:128 + 16 * o, LV:2 * LV] = jnp.zeros_like(lo)
    for i, row in enumerate((stencil[0], time_step * cx, time_step * cy, time_step * cz)):
        ct[i] = jnp.transpose(jnp.broadcast_to(row, (LV, LV)))
    for k in range(8):
        for o in range(7):
            lrows[8 * o + k:8 * o + k + 1, :] = stencil[o] * target[k]
    hi, lo = split(lrows[...])
    hi, lo = hi.astype(F32), lo.astype(F32)
    quad = jnp.concatenate([hi, hi, lo, lo, jnp.zeros((32, LV), F32)], 0)
    lt[:, 0:128] = jnp.transpose(quad[0:128]).astype(BF16)
    lt[:, 128:224] = jnp.transpose(quad[128:256])[:, 0:96].astype(BF16)
    src_lane = lax.broadcasted_iota(jnp.int32, (LV, LV), 0)
    dst_lane = lax.broadcasted_iota(jnp.int32, (LV, LV), 1)
    dst_z = dst_lane % NZ
    lower = jnp.where(src_lane == jnp.where(dst_z == 0, dst_lane + NZ - 1, dst_lane - 1), 1.0, 0.0).astype(BF16)
    upper = jnp.where(src_lane == jnp.where(dst_z == NZ - 1, dst_lane - NZ + 1, dst_lane + 1), 1.0, 0.0).astype(BF16)
    for i in range(2):
        zmat[LV * i:LV * (i + 1), 0:LV] = lower
        zmat[LV * i:LV * (i + 1), LV:2 * LV] = upper
    part = jnp.dot(sel_ref[...], inv_ref[...], precision=HIGHEST, preferred_element_type=F32)
    part = jnp.dot(part, spread_ref[...], precision=HIGHEST, preferred_element_type=F32)
    kx[...] = part * mask_ref[...] + fixed_ref[...]
    zero_plane = jnp.zeros((LV, CELLS), F32)
    for p in (0, 9):
        dt[p] = zero_plane
        q1[p, 16:48, :] = jnp.zeros((32, CELLS), F32)
    for p in (0, 11):
        at_[p] = zero_plane
    for m in range(2):
        pbuf[m, 104:112, :] = jnp.zeros((8, CELLS), F32)

    def swap(i, to_right, right_dst, to_left, left_dst):
        a = pltpu.make_async_remote_copy(to_right, right_dst, s_nb.at[2 * i], r_nb.at[2 * i],
                                         device_id=right, device_id_type=MESH)
        c = pltpu.make_async_remote_copy(to_left, left_dst, s_nb.at[2 * i + 1], r_nb.at[2 * i + 1],
                                         device_id=left, device_id_type=MESH)
        a.start()
        c.start()
        return a, c

    def settle(copies):
        for c in copies:
            c.wait()

    settle(loads)

    def first(x, c):
        val = cat([dbuf[t, pl.ds(x, LV, stride=X), :] for t in range(LT)])
        dt[x + 1] = val
        hi, lo = split(val)
        dhl[x, 0:LV, :] = hi
        dhl[x, LV:2 * LV, :] = lo
        q = jnp.dot(lm[...], dhl[x], preferred_element_type=F32)
        q1[x + 1] = q[0:112] + q[112:224]
        return c

    lax.fori_loop(0, X, first, 0)
    pl.semaphore_wait(barrier, PEERS - 1 + 1 + 3)
    halo = swap(0, rw, rwl, rw, rwr)
    edges[0, 0:16, :] = q1[1, 32:48, :]
    edges[1, 0:16, :] = q1[X, 16:32, :]
    outer1 = swap(1, edges.at[1, pl.ds(0, 16)], from_left.at[pl.ds(0, 16)],
                  edges.at[0, pl.ds(0, 16)], from_right.at[pl.ds(0, 16)])

    def sum_first(x, c):
        mine[0, x] = stencil_moments(q1, x + 1)
        return c

    lax.fori_loop(0, X, sum_first, 0)

    def alpha_row(ref, x):
        return alpha_of(ref[pl.ds(x, 1), :], ref[pl.ds(x + X, 1), :])

    def products(i):
        hi, lo = split(at_[i + 1])
        ahl[i, 0:LV, :] = hi
        ahl[i, LV:2 * LV, :] = lo
        q = jnp.dot(lm[...], ahl[i], preferred_element_type=F32)
        q2[i] = q[0:112] + q[112:224]

    def second(j, c):
        x = lax.rem(X - j, X)

        val = stream_plane(dt, dhl, x + 1, x, ct, zmat, alpha_row(rw, x))
        for i in range(LT):
            at_[x + 2, :, 128 * i:128 * (i + 1)] = val[i]
        products(x + 1)
        return c

    def third(i):
        val = stream_plane(at_, ahl, i + 1, i, ct, zmat)
        for t in range(LT):
            aa[i + 1, :, 128 * t:128 * (t + 1)] = val[t]

    lax.fori_loop(0, 2, second, 0)
    settle(outer1)
    mine[0, 0] += from_left[0:16, :]
    mine[0, X - 1] += from_right[0:16, :]

    def pack(m):
        for x in range(X):
            pbuf[m, 13 * x:13 * x + 13, :] = mine[m, x, 0:13, :]

    def chunk_of(o):
        return (pl.ds(pl.multiple_of(CH * (o // LT), 8), CH), pl.ds(pl.multiple_of(128 * lax.rem(o, LT), 128), 128))

    def send_parts(m):
        def send(j, c):
            o = lax.rem(place + j, PEERS)
            r, k = chunk_of(o)
            pltpu.make_async_remote_copy(pbuf.at[m, r, k], rsbuf.at[m, j], s_rs.at[m], r_rs.at[m],
                                         device_id=peer(o), device_id_type=MESH).start()
            return c

        lax.fori_loop(1, PEERS, send, 0)

    def all_parts(m):
        return rsbuf.at[m, pl.ds(1, PEERS - 1)]

    def across(m):
        return pltpu.make_async_remote_copy(ssum.at[m], xbuf.at[m], s_x.at[m], r_x.at[m],
                                            device_id=partner, device_id_type=MESH)

    def own_sum(m):
        pltpu.make_async_copy(all_parts(m), all_parts(m), r_rs.at[m]).wait()
        r, k = chunk_of(place)
        acc = pbuf[m, r, k]
        for j in range(1, PEERS):
            acc = acc + rsbuf[m, j]
        ssum[m] = acc
        across(m).start()

    def send_total(m):
        across(m).wait()
        val = ssum[m] + xbuf[m]
        total[m] = val
        r, k = chunk_of(place)
        fbuf[m, r, k] = val

        def send(j, c):
            pltpu.make_async_remote_copy(total.at[m], fbuf.at[m, r, k], s_ag.at[m], r_ag.at[m],
                                         device_id=peer(lax.rem(place + j, PEERS)), device_id_type=MESH).start()
            return c

        lax.fori_loop(1, PEERS, send, 0)

    def all_totals(m):
        pltpu.make_async_copy(all_parts(m), all_parts(m), r_ag.at[m]).wait()

    def all_sent(m):
        pltpu.make_async_copy(all_parts(m), all_parts(m), s_rs.at[m]).wait()
        pltpu.make_async_copy(all_parts(m), all_parts(m), s_ag.at[m]).wait()

    pack(0)
    send_parts(0)
    lax.fori_loop(2, X, second, 0)

    settle(halo)
    speed = ct[1]
    to_lower = jnp.where(speed > 0, 0.0, -speed)
    to_upper = jnp.where(speed > 0, speed, 0.0)
    al_l, al_r = alpha_row(rwl, X - 1), alpha_row(rwr, 0)
    for i in range(LT):
        c = slice(128 * i, 128 * (i + 1))
        at_[1, :, c] = to_lower * dt[1, :, c] * al_l[:, c]
        at_[X + 2, :, c] = to_upper * dt[X, :, c] * al_r[:, c]

    def ends(j, c):
        products((X + 1) * j)
        return c

    lax.fori_loop(0, 2, ends, 0)

    edges[0, 16:32, :] = stencil_edge(q2, 0) + q2[1, 32:48, :]
    edges[0, 32:48, :] = q2[0, 32:48, :]
    edges[1, 16:32, :] = stencil_edge(q2, X + 1) + q2[X, 16:32, :]
    edges[1, 32:48, :] = q2[X + 1, 16:32, :]
    outer2 = swap(2, edges.at[1, pl.ds(16, 32)], from_left.at[pl.ds(16, 32)],
                  edges.at[0, pl.ds(16, 32)], from_right.at[pl.ds(16, 32)])
    own_sum(0)

    def sum_second(x, c):
        mine[1, x] = stencil_moments(q2, x + 1)
        return c

    lax.fori_loop(0, X, sum_second, 0)

    def edge_third(j, c):
        third((X + 1) * j)
        return c

    lax.fori_loop(0, 2, edge_third, 0)
    for i in range(LT):
        c = slice(128 * i, 128 * (i + 1))
        aa[0, :, c] = to_lower * at_[1, :, c]
        aa[X + 3, :, c] = to_upper * at_[X + 2, :, c]
    send_total(0)
    settle(outer2)
    mine[1, 0] += from_left[16:32, :]
    mine[1, 1] += from_left[32:48, :]
    mine[1, X - 1] += from_right[16:32, :]
    mine[1, X - 2] += from_right[32:48, :]
    pack(1)
    send_parts(1)

    core = lax.rem(s, 2)
    mate = (v, s + 1 - 2 * core)
    over = (v, lax.rem(s + 2, 4))
    half = LV // 2
    mine_v = pl.ds(pl.multiple_of(half * core, 8), half)
    mate_v = pl.ds(pl.multiple_of(half * (1 - core), 8), half)
    out_end = pl.ds((X + 2) * core, 2)
    in_end = pl.ds((X + 2) * (1 - core), 2)

    def hand(i, src, dst, to):
        c = pltpu.make_async_remote_copy(src, dst, s_e.at[i], r_e.at[i], device_id=to, device_id_type=MESH)
        c.start()
        return c

    give = hand(0, aa.at[out_end, mate_v], cin, mate)
    near = hand(1, aa.at[in_end], cnear, mate)

    def inner_third(i, c):
        third(i)
        return c

    lax.fori_loop(1, 3, inner_third, 0)
    give.wait()
    cout[...] = aa[out_end, mine_v, :] + cin[...]
    over_0 = hand(2, cout.at[0], cfar.at[0], over)
    lax.fori_loop(3, 7, inner_third, 0)

    all_totals(0)
    l1[0:64, :] = jnp.dot(kx[0:64, :], fbuf[0, 0:104, :], precision=HIGHEST, preferred_element_type=F32)
    for k in range(8):
        h_out[0, HALO * k:HALO * (k + 1), :] = l1[8 * k:8 * k + HALO, :]
        h_out[1, HALO * k:HALO * (k + 1), :] = l1[8 * k + X - HALO:8 * k + X, :]
    halo2 = swap(3, h_out.at[1], h_left, h_out.at[0], h_right)
    own_sum(1)
    l1[64:168, :] = jnp.dot(kx[64:168, :], fbuf[0, 0:104, :], precision=HIGHEST, preferred_element_type=F32)
    lax.fori_loop(7, X + 1, inner_third, 0)
    send_total(1)
    over_1 = hand(3, cout.at[1], cfar.at[1], over)
    settle(halo2)

    zero8 = jnp.zeros((8, CELLS), F32)

    def clear_ends(k, c):
        for i in range(2):
            u[i, k, 0:8, :] = zero8
            u[i, k, 24:32, :] = zero8
        return c

    lax.fori_loop(0, 4, clear_ends, 0)

    def fill(k, lo_rows, own, hi_rows):
        b[k, 0:HALO, :] = lo_rows
        b[k, HALO:HALO + X, :] = own
        b[k, HALO + X:EXT, :] = hi_rows

    def smooth():
        def start(k, c):
            u[0, k, 8:24, :] = b[k]
            return c

        lax.fori_loop(0, 4, start, 0)
        for sweep in range(SWEEPS):
            src, dst = sweep % 2, 1 - sweep % 2

            def row(k, c):
                for blk in range(2):
                    lo = 8 + 8 * blk
                    here, ylo, yhi, zlo, zhi = yz_shifts(u[src, k, lo:lo + 8, :])
                    near = u[src, k, lo - 1:lo + 7, :] + u[src, k, lo + 1:lo + 9, :]
                    side = cat([(ylo[i] + yhi[i]) + (zlo[i] + zhi[i]) for i in range(LT)])
                    u[dst, k, lo:lo + 8, :] = (b[k, 8 * blk:8 * blk + 8, :] + coupling * (near + side)) * (1.0 / (1.0 + 6.0 * coupling))
                return c

            lax.fori_loop(0, 4, row, 0)
        return SWEEPS % 2

    for k in range(4):
        fill(k, h_left[4 * k:4 * k + 4, :], l1[8 * k:8 * k + 8, :], h_right[4 * k:4 * k + 4, :])
    last = smooth()

    def gammas(relax, wall):
        return jnp.where(wall > 0, 0.0, relax), jnp.where(wall > 0, 1.0, relax)

    own_alpha = alpha_of(rw[0:X, :], rw[X:2 * X, :])
    factors = [gammas(ref[0:X, :], ref[X:2 * X, :]) for ref in (rwl, rw, rwr)]
    for k in range(8):
        gl, go, gr = (f[1 if k in (3, 4) else 0] for f in factors)
        if k < 4:
            lo_rows = u[last, k, 8:8 + HALO, :]
            own = u[last, k, 8 + HALO:8 + HALO + X, :]
            hi_rows = u[last, k, 8 + HALO + X:8 + EXT, :]
        else:
            lo_rows = h_left[4 * k:4 * k + 4, :]
            own = l1[8 * k:8 * k + 8, :]
            hi_rows = h_right[4 * k:4 * k + 4, :]
        own = own * go
        g1[EXT * k:EXT * k + HALO, :] = lo_rows * gl[4:8]
        g1[EXT * k + HALO:EXT * k + HALO + X, :] = own
        g1[EXT * k + HALO + X:EXT * (k + 1), :] = hi_rows * gr[0:4]
        here, ylo, yhi, zlo, zhi = yz_shifts(own)
        for j, val in enumerate((ylo, yhi, zlo, zhi)):
            rhs[64 * j + 8 * k:64 * j + 8 * k + 8, :] = cat(val)
        at = EXT * k + HALO
        before = tiles(g1[at - 1:at + 7, :])
        after = tiles(g1[at + 1:at + 9, :])
        for t in range(LT):
            al = own_alpha[:, 128 * t:128 * (t + 1)]
            for o, val in enumerate((here, before, after, ylo, yhi, zlo, zhi)):
                dbuf[t, 64 * o + 8 * k:64 * o + 8 * k + 8, :] = val[t] * al

    def squares(l, sm):
        acc = jnp.zeros((8, CELLS), F32)
        for i in range(9):
            d = l[64 + 8 * i:72 + 8 * i, :]
            acc = acc + d * d
        for k in range(4):
            d = u[sm, k, 8 + HALO:8 + HALO + X, :] - l[136 + 8 * k:144 + 8 * k, :]
            acc = acc + d * d
        parts = tiles(acc)
        out = parts[0]
        for i in range(1, LT):
            out = out + parts[i]
        return out

    nsend[0] = squares(l1, last)

    add[...] = (
        jnp.dot(nc[:, 0:128], g1[...], precision=HIGHEST, preferred_element_type=F32)
        + jnp.dot(nc[:, 128:384], rhs[...], precision=HIGHEST, preferred_element_type=F32)
    )

    def spread(x, c):
        for t in range(LT):
            hi, lo = split(dbuf[t, pl.ds(x, 56, stride=X), :])
            both_parts = jnp.concatenate([hi.astype(F32), lo.astype(F32)], 0).astype(BF16)
            cols = slice(128 * t, 128 * (t + 1))
            dhl[x, 0:112, cols] = both_parts
            dhl[x, 112:224, cols] = both_parts
        return c

    over_0.wait()
    over_1.wait()
    share = hand(4, cfar, cboth, mate)
    all_totals(1)
    m2 = fbuf[1, 0:104, :] + add[...]
    b2out[...] = jnp.dot(kx[0:32, :], m2, precision=HIGHEST, preferred_element_type=F32)
    for k in range(4):
        b2_out[0, HALO * k:HALO * (k + 1), :] = b2out[8 * k:8 * k + HALO, :]
        b2_out[1, HALO * k:HALO * (k + 1), :] = b2out[8 * k + X - HALO:8 * k + X, :]
    halo3 = swap(6, b2_out.at[1], b2l, b2_out.at[0], b2r)
    l2[...] = jnp.dot(kx[32:208, :], m2, precision=HIGHEST, preferred_element_type=F32)

    def combine(x):
        aa[x + 2] = jnp.dot(lt[...], dhl[x, 0:224, :], preferred_element_type=F32) + alpha_row(rw, x) * aa[x + 2]

    def middle(x, c):
        combine(x)
        return c

    lax.fori_loop(0, X, spread, 0)
    lax.fori_loop(2, X - 2, middle, 0)
    near.wait()
    share.wait()
    is_upper = (core == 0).astype(F32)
    from_far = 2 + (X - 2) * core
    from_near = 2 + (X - 2) * (1 - core)

    def add_ends(i, carry):
        for t in range(LT):
            c = slice(128 * t, 128 * (t + 1))
            aa[from_near + i, :, c] += cnear[i, :, c]
            aa[from_far + i, mine_v, c] += jnp.where(wanted_of(mine_v) > 0, cfar[i, :, c], 0.0)
            aa[from_far + i, mate_v, c] += jnp.where(wanted_of(mate_v) > 0, cboth[i, :, c], 0.0)
        return carry

    def wanted_of(rows):
        towards = ct[1, rows, :]
        return jnp.where(towards > 0, is_upper, 1.0 - is_upper)

    lax.fori_loop(0, 2, add_ends, 0)

    settle(halo3)
    for k in range(4):
        fill(k, b2l[4 * k:4 * k + 4, :], b2out[8 * k:8 * k + 8, :], b2r[4 * k:4 * k + 4, :])
    last = smooth()
    acc = jnp.zeros((8, CELLS), F32)
    for i in range(9):
        d = l2[32 + 8 * i:40 + 8 * i, :]
        acc = acc + d * d
    for k in range(4):
        d = u[last, k, 8 + HALO:8 + HALO + X, :] - l2[104 + 8 * k:112 + 8 * k, :]
        acc = acc + d * d
    parts = tiles(acc)
    out = parts[0]
    for i in range(1, LT):
        out = out + parts[i]
    nsend[1] = out
    notes = []
    for j in (1, 2, 3):
        c = pltpu.make_async_remote_copy(nsend, nrecv.at[j - 1], s_nm.at[j - 1], r_nm.at[j - 1],
                                         device_id=(v, lax.rem(s + j, 4)), device_id_type=MESH)
        c.start()
        notes.append(c)

    beta, both = gammas(rw[0:X, :], rw[X:2 * X, :])
    for k in range(8):
        f = u[last, k, 8 + HALO:8 + HALO + X, :] if k < 4 else l2[8 * k - 32:8 * k - 24, :]
        g2_out[8 * k:8 * k + 8, :] = f * (both if k in (3, 4) else beta)

    tile = pl.ds(pl.multiple_of(128 * (v // 4), 128), 128)
    turn = lax.rem(128 - 32 * lax.rem(v, 4), 128)
    for r in range(MOM):
        if 1 <= r <= 4:
            f = u[last, r - 1, 8 + HALO:8 + HALO + X, tile]
        elif r == 0:
            f = l2[0:8, tile]
        elif r >= 10:
            f = l2[8 + 8 * (r - 10):16 + 8 * (r - 10), tile]
        else:
            f = l2[136 + 8 * (r - 5):144 + 8 * (r - 5), tile]
        mac_out[r] = pltpu.roll(f, turn, 1)[:, 0:32]

    def outside(j, c):
        combine(lax.rem(j + X - 2, X))
        return c

    lax.fori_loop(0, 4, outside, 0)

    settle(notes)
    for i in range(2):
        norm_out[i] = (nsend[i] + nrecv[0, i]) + (nrecv[1, i] + nrecv[2, i])
    for m in range(2):
        all_sent(m)


def stencil_edge(q_ref, p):
    def rows(o):
        return tiles(q_ref[p, 16 * o:16 * o + 16, :])

    ylo, _ = y_shifts(rows(3))
    _, yhi = y_shifts(rows(4))
    zlo, _ = z_shifts(rows(5))
    _, zhi = z_shifts(rows(6))
    here = rows(0)
    return cat([here[i] + (ylo[i] + yhi[i]) + (zlo[i] + zhi[i]) for i in range(LT)])


PAIRS = 4


def renew(a_ref, g2_ref, vel_ref, mac_ref, sum_ref, out_hbm, mac_out, norm_out, obuf, stage, rhs, lt, sem_out):
    mac_out[...] = mac_ref[...]
    for i in range(2):
        norm_out[i] = jnp.sqrt(jnp.sum(sum_ref[i]))

    vel = speed_range * (2.0 * vel_ref[...].astype(F32) + 1.0 - NVX) / NVX
    _, target, _ = functions_of(vel[0:1], vel[1:2], vel[2:3])
    for k in range(8):
        stage[0, k:k + 1, :] = target[k]
    hi, lo = split(stage[0, 0:8, :])
    hi, lo = hi.astype(F32), lo.astype(F32)
    quad = jnp.concatenate([hi, hi, lo, lo, jnp.zeros((96, LV), F32)], 0)
    lt[...] = jnp.transpose(quad)[:, 0:32].astype(BF16)

    for t in range(LT):
        stage[t] = g2_ref[:, 128 * t:128 * (t + 1)]

    def spread(x, c):
        for t in range(LT):
            hi, lo = split(stage[t, pl.ds(x, 8, stride=X), :])
            both_parts = jnp.concatenate([hi.astype(F32), lo.astype(F32)], 0).astype(BF16)
            cols = slice(128 * t, 128 * (t + 1))
            rhs[x, 0:16, cols] = both_parts
            rhs[x, 16:32, cols] = both_parts
        return c

    lax.fori_loop(0, X, spread, 0)

    puts = []
    for i in range(PAIRS):
        pair = slice(256 * i, 256 * (i + 1))

        def plane(x, c):
            val = jnp.dot(lt[...], rhs[x, :, pair], preferred_element_type=F32) + a_ref[x + 2, :, pair]
            obuf[2 * i, pl.ds(x, LV, stride=X), :] = val[:, 0:128]
            obuf[2 * i + 1, pl.ds(x, LV, stride=X), :] = val[:, 128:256]
            return c

        lax.fori_loop(0, X, plane, 0)
        for t in (2 * i, 2 * i + 1):
            c = pltpu.make_async_copy(obuf.at[t], out_hbm.at[:, pl.ds(128 * t, 128)], sem_out.at[t])
            c.start()
            puts.append(c)
    for c in puts:
        c.wait()


def shards(consts, dist, vel_index, relax, wall_mask, macro_inverse):
    vmem = pl.BlockSpec(memory_space=pltpu.VMEM)
    hbm = pl.BlockSpec(memory_space=pl.ANY)
    smem = pl.BlockSpec(memory_space=pltpu.SMEM)
    dma = pltpu.SemaphoreType.DMA
    sds = jax.ShapeDtypeStruct
    a, g2, mac, norm = pl.pallas_call(
        exchange,
        out_shape=(
            pltpu.VMEM((X + 4, LV, CELLS), F32), pltpu.VMEM((64, CELLS), F32),
            pltpu.VMEM((MOM, X, 32), F32), pltpu.VMEM((2, 8, 128), F32),
        ),
        in_specs=[hbm] + [vmem] * 9,
        out_specs=(vmem,) * 4,
        scratch_shapes=[
            pltpu.VMEM((LT, LV * X, 128), F32),
            pltpu.VMEM((X + 2, LV, CELLS), F32),
            pltpu.VMEM((X + 4, LV, CELLS), F32),
            pltpu.VMEM((X, 2 * LV, CELLS), BF16),
            pltpu.VMEM((X + 2, 2 * LV, CELLS), BF16),
            pltpu.VMEM((X + 2, 112, CELLS), F32),
            pltpu.VMEM((X + 2, 112, CELLS), F32),
            pltpu.VMEM((2, X, 16, CELLS), F32),
            pltpu.VMEM((2, 48, CELLS), F32),
            pltpu.VMEM((48, CELLS), F32),
            pltpu.VMEM((48, CELLS), F32),
            pltpu.VMEM((2 * X, CELLS), F32),
            pltpu.VMEM((2 * X, CELLS), F32),
            pltpu.VMEM((2 * X, CELLS), F32),
            pltpu.VMEM((16, LV), F32),
            pltpu.VMEM((224, 2 * LV), BF16),
            pltpu.VMEM((4, LV, LV), F32),
            pltpu.VMEM((2 * LV, 2 * LV), BF16),
            pltpu.VMEM((26 * X, X * MOM), F32),
            pltpu.VMEM((2, 2 * CH, CELLS), F32),
            pltpu.VMEM((2, PEERS, CH, 128), F32),
            pltpu.VMEM((2, CH, 128), F32),
            pltpu.VMEM((2, CH, 128), F32),
            pltpu.VMEM((2, CH, 128), F32),
            pltpu.VMEM((2, 2 * CH, CELLS), F32),
            pltpu.VMEM((26 * X, CELLS), F32),
            pltpu.VMEM((2, 32, CELLS), F32),
            pltpu.VMEM((32, CELLS), F32),
            pltpu.VMEM((32, CELLS), F32),
            pltpu.VMEM((32, CELLS), F32),
            pltpu.VMEM((2, 16, CELLS), F32),
            pltpu.VMEM((16, CELLS), F32),
            pltpu.VMEM((16, CELLS), F32),
            pltpu.VMEM((2, 4, 32, CELLS), F32),
            pltpu.VMEM((4, EXT, CELLS), F32),
            pltpu.VMEM((8 * EXT, CELLS), F32),
            pltpu.VMEM((256, CELLS), F32),
            pltpu.VMEM((56, LV), F32),
            pltpu.VMEM((LV, 224), BF16),
            pltpu.VMEM((X * MOM, CELLS), F32),
            pltpu.VMEM((22 * X, CELLS), F32),
            pltpu.VMEM((2, 8, 128), F32),
            pltpu.VMEM((3, 2, 8, 128), F32),
            pltpu.VMEM((2, LV // 2, CELLS), F32),
            pltpu.VMEM((2, LV // 2, CELLS), F32),
            pltpu.VMEM((2, LV // 2, CELLS), F32),
            pltpu.VMEM((2, LV // 2, CELLS), F32),
            pltpu.VMEM((2, LV, CELLS), F32),
            dma((LT,)), dma((14,)), dma((14,)), dma((2,)), dma((2,)), dma((2,)), dma((2,)), dma((2,)), dma((2,)),
            dma((3,)), dma((3,)), dma((5,)), dma((5,)),
        ],
        compiler_params=pltpu.CompilerParams(collective_id=0, has_side_effects=True, vmem_limit_bytes=54 * 2 ** 20),
        name="exchange",
    )(dist.reshape(LV * X, CELLS), relax, wall_mask, vel_index, macro_inverse, *consts)

    out, mac, norm = pl.pallas_call(
        renew,
        out_shape=(sds((LV * X, CELLS), F32), sds((MOM, X, 32), F32), sds((2,), F32)),
        in_specs=[vmem] * 5,
        out_specs=(hbm, vmem, smem),
        scratch_shapes=[
            pltpu.VMEM((LT, LV * X, 128), F32),
            pltpu.VMEM((LT, 64, 128), F32),
            pltpu.VMEM((X, 32, CELLS), BF16),
            pltpu.VMEM((LV, 32), BF16),
            dma((LT,)),
        ],
        compiler_params=pltpu.CompilerParams(vmem_limit_bytes=32 * 2 ** 20),
        name="renew",
    )(a, g2, vel_index, mac, norm)
    return (out.reshape(LV, X, CELLS), mac, norm)


def solution(mesh):
    consts = selection() + [coupling_table()]
    return jax.shard_map(
        lambda *args: shards([jnp.asarray(c) for c in consts], *args),
        mesh=mesh,
        in_specs=(P("vel", "space", None), P(None, "vel"), P("space", None), P("space", None), P()),
        out_specs=(P("vel", "space", None), P(None, "space", "vel"), P()),
        check_vma=False,
    )
```

```python
import functools
import math

import jax
import jax.numpy as jnp
import numpy as np
from jax import lax
from jax.experimental import pallas as pl
from jax.experimental.pallas import tpu as pltpu
from jax.sharding import PartitionSpec as P

NVX = 16
NZ = 16
MOM = 13
SWEEPS = 3
speed_range = 4.0
time_step = 0.08
coupling = 0.5

MESH = pl.DeviceIdType.MESH
F32 = jnp.float32
BF16 = jnp.bfloat16
X = 8
CELLS = 1024
LT = CELLS // 128
RING = 4
PEERS = RING * RING
LV = 128
CH = 56
HALO = 4
EXT = X + 2 * HALO
FIELD_ROWS = (1, 2, 3, 4, 0, 10, 11, 12)
OTHER_ROWS = (0, 5, 6, 7, 8, 9, 10, 11, 12)
HIGHEST = lax.Precision.HIGHEST


def functions_of(cx, cy, cz, xp=jnp):
    square = cx * cx + cy * cy + cz * cz
    weights = (2.0 * speed_range / NVX) ** 3 * math.pi ** (-1.5) * xp.exp(-square)
    heat = square - 2.5
    one = xp.ones_like(cx)
    rows = [
        one, cx, cy, cz, 2.0 * square / 3.0 - 1.0,
        2.0 * cx * cy, 2.0 * cx * cz, 2.0 * cy * cz,
        cx * cx - cy * cy, cy * cy - cz * cz,
        cx * heat, cy * heat, cz * heat,
    ]
    factor = 4.0 / 15.0
    target = [2.0 * cx, 2.0 * cy, 2.0 * cz, square - 1.5, one, factor * cx * heat, factor * cy * heat, factor * cz * heat]
    stencil = [1.0 - time_step * (xp.abs(cx) + xp.abs(cy) + xp.abs(cz))]
    for c in (cx, cy, cz):
        stencil += [time_step * xp.maximum(c, 0.0), time_step * xp.maximum(-c, 0.0)]
    return [r * weights for r in rows], target, stencil


def selection():
    sel = np.zeros((26, MOM))
    own = np.zeros((26, MOM))
    for j in range(26):
        if j < 8:
            sel[j, FIELD_ROWS[j]] = 1
        elif j < 17:
            sel[j, OTHER_ROWS[j - 8]] = 1
            own[j, OTHER_ROWS[j - 8]] = -1
        elif j < 21:
            own[j, j - 16] = 1
        else:
            sel[j, j - 16] = 1
    eye = np.eye(X)
    sel = np.repeat(sel, X, 0)
    spread = np.tile(np.eye(MOM), (1, X))
    mask = np.repeat(np.tile(eye, (26, 1)), MOM, 1)
    fixed = np.einsum("jr,xp->jxpr", own, eye).reshape(26 * X, X * MOM)
    return [a.astype(np.float32) for a in (sel, spread, mask, fixed)]


def coupling_table():
    line = speed_range * (2.0 * np.arange(NVX) + 1.0 - NVX) / NVX
    cx, cy, cz = (a.reshape(-1) for a in np.meshgrid(line, line, line, indexing="ij"))
    rows, target, stencil = functions_of(cx, cy, cz, np)
    n = np.einsum("rv,ov,kv->ork", rows, stencil, target)
    near = np.zeros((X, MOM, 8, EXT))
    side = np.zeros((X, MOM, 4, 8, X))
    for x in range(X):
        near[x, :, :, x + HALO] += n[0]
        near[x, :, :, x + HALO - 1] += n[1]
        near[x, :, :, x + HALO + 1] += n[2]
        for j in range(4):
            side[x, :, j, :, x] += n[3 + j]
    table = np.concatenate([near.reshape(X * MOM, 8 * EXT), side.reshape(X * MOM, 32 * X)], 1)
    return table.astype(np.float32)


def split(a):
    hi = a.astype(BF16)
    return hi, (a - hi.astype(F32)).astype(BF16)


def cat(parts):
    return jnp.concatenate(parts, axis=1)


def tiles(x):
    return [x[:, 128 * i:128 * (i + 1)] for i in range(LT)]


def y_shifts(t):
    lane = lax.broadcasted_iota(jnp.int32, t[0].shape, 1)
    up = [pltpu.roll(a, 16, 1) for a in t]
    down = [pltpu.roll(a, 112, 1) for a in t]
    ylo = [jnp.where(lane < 16, up[i - 1], up[i]) for i in range(LT)]
    yhi = [jnp.where(lane >= 112, down[(i + 1) % LT], down[i]) for i in range(LT)]
    return ylo, yhi


def z_shifts(t):
    z = lax.broadcasted_iota(jnp.int32, t[0].shape, 1) % NZ
    zlo = [jnp.where(z == 0, pltpu.roll(a, 113, 1), pltpu.roll(a, 1, 1)) for a in t]
    zhi = [jnp.where(z == NZ - 1, pltpu.roll(a, 15, 1), pltpu.roll(a, 127, 1)) for a in t]
    return zlo, zhi


def yz_shifts(x):
    t = tiles(x)
    return (t,) + y_shifts(t) + z_shifts(t)


def stencil_moments(q_ref, p):
    def rows(o, at=p):
        return tiles(q_ref[at, 16 * o:16 * o + 16, :])

    ylo, _ = y_shifts(rows(3))
    _, yhi = y_shifts(rows(4))
    zlo, _ = z_shifts(rows(5))
    _, zhi = z_shifts(rows(6))
    here, before, after = rows(0), rows(1, p - 1), rows(2, p + 1)
    return cat([(here[i] + before[i] + after[i]) + (ylo[i] + yhi[i]) + (zlo[i] + zhi[i]) for i in range(LT)])


def alpha_of(relax, wall):
    return jnp.where(wall > 0, 0.0, 1.0 - relax)


def stream_plane(src, halves, p, h, ct, zmat, scale=None):
    lane = lax.broadcasted_iota(jnp.int32, (LV, 128), 1)
    k0, cx, cy, cz = (ct[i] for i in range(4))
    px, py, pz = cx > 0, cy > 0, cz > 0
    kx, ky, kz = jnp.abs(cx), jnp.abs(cy), jnp.abs(cz)
    t = [src[p, :, 128 * i:128 * (i + 1)] for i in range(LT)]
    z = [
        jnp.dot(
            cat([halves[h, 0:LV, 128 * i:128 * (i + 1)], halves[h, LV:2 * LV, 128 * i:128 * (i + 1)]]),
            zmat[...],
            preferred_element_type=F32,
        )
        for i in range(LT)
    ]
    up = [pltpu.roll(a, 16, 1) for a in t]
    down = [pltpu.roll(a, 112, 1) for a in t]
    out = []
    for i in range(LT):
        s = slice(128 * i, 128 * (i + 1))
        in_x = jnp.where(px, src[p - 1, :, s], src[p + 1, :, s])
        in_y = jnp.where(
            py,
            jnp.where(lane < 16, up[i - 1], up[i]),
            jnp.where(lane >= 112, down[(i + 1) % LT], down[i]),
        )
        in_z = jnp.where(pz, z[i][:, 0:128], z[i][:, 128:256])
        val = (k0 * t[i] + kx * in_x) + (ky * in_y + kz * in_z)
        out.append(val if scale is None else val * scale[:, s])
    return out


def exchange(dist_hbm, relax_ref, wall_ref, vel_ref, inv_ref, sel_ref, spread_ref, mask_ref, fixed_ref, nc,
             aa, g2_out, mac_out, norm_out,
             dbuf, dt, at_, dhl, ahl, q1, q2, mine, edges, from_left, from_right, rw, rwl, rwr,
             mrows, lm, ct, zmat, kx, pbuf, rsbuf, ssum, xbuf, total, fbuf, l1, h_out, h_left, h_right, b2out, b2_out, b2l, b2r,
             u, b, g1, rhs, lrows, lt, add, l2, nsend, nrecv, cin, cout, cfar, cboth, cnear,
             sem_ld, s_nb, r_nb, s_rs, r_rs, s_ag, r_ag, s_x, r_x, s_nm, r_nm, s_e, r_e):
    v = lax.axis_index("vel")
    s = lax.axis_index("space")
    left = (v, lax.rem(s + 3, 4))
    right = (v, lax.rem(s + 1, 4))
    far = v // PEERS
    place = lax.rem(v, PEERS)
    partner = ((1 - far) * PEERS + place, s)

    def peer(o):
        return (far * PEERS + o, s)

    loads = [pltpu.make_async_copy(dist_hbm.at[:, pl.ds(128 * t, 128)], dbuf.at[t], sem_ld.at[t]) for t in range(LT)]
    for c in loads:
        c.start()

    barrier = pltpu.get_barrier_semaphore()

    def greet(j, c):
        pl.semaphore_signal(barrier, inc=1, device_id=peer(lax.rem(place + j, PEERS)), device_id_type=MESH)
        return c

    lax.fori_loop(1, PEERS, greet, 0)
    pl.semaphore_signal(barrier, inc=1, device_id=partner, device_id_type=MESH)
    for j in (1, 2, 3):
        pl.semaphore_signal(barrier, inc=1, device_id=(v, lax.rem(s + j, 4)), device_id_type=MESH)

    rw[0:X, :] = relax_ref[...]
    rw[X:2 * X, :] = wall_ref[...].astype(F32)
    vel = speed_range * (2.0 * vel_ref[...].astype(F32) + 1.0 - NVX) / NVX
    cx, cy, cz = vel[0:1], vel[1:2], vel[2:3]
    rows, target, stencil = functions_of(cx, cy, cz)
    mrows[...] = jnp.zeros_like(mrows)
    for r in range(MOM):
        mrows[r:r + 1, :] = rows[r]
    for o in range(7):
        hi, lo = split(mrows[...] * stencil[o])
        lm[16 * o:16 * o + 16, 0:LV] = hi
        lm[16 * o:16 * o + 16, LV:2 * LV] = hi
        lm[112 + 16 * o:128 + 16 * o, 0:LV] = lo
        lm[112 + 16 * o:128 + 16 * o, LV:2 * LV] = jnp.zeros_like(lo)
    for i, row in enumerate((stencil[0], time_step * cx, time_step * cy, time_step * cz)):
        ct[i] = jnp.transpose(jnp.broadcast_to(row, (LV, LV)))
    for k in range(8):
        for o in range(7):
            lrows[8 * o + k:8 * o + k + 1, :] = stencil[o] * target[k]
    hi, lo = split(lrows[...])
    hi, lo = hi.astype(F32), lo.astype(F32)
    quad = jnp.concatenate([hi, hi, lo, lo, jnp.zeros((32, LV), F32)], 0)
    lt[:, 0:128] = jnp.transpose(quad[0:128]).astype(BF16)
    lt[:, 128:224] = jnp.transpose(quad[128:256])[:, 0:96].astype(BF16)
    src_lane = lax.broadcasted_iota(jnp.int32, (LV, LV), 0)
    dst_lane = lax.broadcasted_iota(jnp.int32, (LV, LV), 1)
    dst_z = dst_lane % NZ
    lower = jnp.where(src_lane == jnp.where(dst_z == 0, dst_lane + NZ - 1, dst_lane - 1), 1.0, 0.0).astype(BF16)
    upper = jnp.where(src_lane == jnp.where(dst_z == NZ - 1, dst_lane - NZ + 1, dst_lane + 1), 1.0, 0.0).astype(BF16)
    for i in range(2):
        zmat[LV * i:LV * (i + 1), 0:LV] = lower
        zmat[LV * i:LV * (i + 1), LV:2 * LV] = upper
    part = jnp.dot(sel_ref[...], inv_ref[...], precision=HIGHEST, preferred_element_type=F32)
    part = jnp.dot(part, spread_ref[...], precision=HIGHEST, preferred_element_type=F32)
    kx[...] = part * mask_ref[...] + fixed_ref[...]
    zero_plane = jnp.zeros((LV, CELLS), F32)
    for p in (0, 9):
        dt[p] = zero_plane
        q1[p, 16:48, :] = jnp.zeros((32, CELLS), F32)
    for p in (0, 11):
        at_[p] = zero_plane
    for m in range(2):
        pbuf[m, 104:112, :] = jnp.zeros((8, CELLS), F32)

    def swap(i, to_right, right_dst, to_left, left_dst):
        a = pltpu.make_async_remote_copy(to_right, right_dst, s_nb.at[2 * i], r_nb.at[2 * i],
                                         device_id=right, device_id_type=MESH)
        c = pltpu.make_async_remote_copy(to_left, left_dst, s_nb.at[2 * i + 1], r_nb.at[2 * i + 1],
                                         device_id=left, device_id_type=MESH)
        a.start()
        c.start()
        return a, c

    def settle(copies):
        for c in copies:
            c.wait()

    settle(loads)

    def first(x, c):
        val = cat([dbuf[t, pl.ds(x, LV, stride=X), :] for t in range(LT)])
        dt[x + 1] = val
        hi, lo = split(val)
        dhl[x, 0:LV, :] = hi
        dhl[x, LV:2 * LV, :] = lo
        q = jnp.dot(lm[...], dhl[x], preferred_element_type=F32)
        q1[x + 1] = q[0:112] + q[112:224]
        return c

    lax.fori_loop(0, X, first, 0)
    pl.semaphore_wait(barrier, PEERS - 1 + 1 + 3)
    edges[0, 0:16, :] = q1[1, 32:48, :]
    edges[1, 0:16, :] = q1[X, 16:32, :]
    outer1 = swap(1, edges.at[1, pl.ds(0, 16)], from_left.at[pl.ds(0, 16)],
                  edges.at[0, pl.ds(0, 16)], from_right.at[pl.ds(0, 16)])
    halo = swap(0, rw, rwl, rw, rwr)

    def sum_first(x, c):
        mine[0, x] = stencil_moments(q1, x + 1)
        return c

    lax.fori_loop(0, X, sum_first, 0)

    def alpha_row(ref, x):
        return alpha_of(ref[pl.ds(x, 1), :], ref[pl.ds(x + X, 1), :])

    def products(i):
        hi, lo = split(at_[i + 1])
        ahl[i, 0:LV, :] = hi
        ahl[i, LV:2 * LV, :] = lo
        q = jnp.dot(lm[...], ahl[i], preferred_element_type=F32)
        q2[i] = q[0:112] + q[112:224]

    def second(j, c):
        x = lax.rem(X - j, X)

        val = stream_plane(dt, dhl, x + 1, x, ct, zmat, alpha_row(rw, x))
        for i in range(LT):
            at_[x + 2, :, 128 * i:128 * (i + 1)] = val[i]
        products(x + 1)
        return c

    def third(i):
        val = stream_plane(at_, ahl, i + 1, i, ct, zmat)
        for t in range(LT):
            aa[i + 1, :, 128 * t:128 * (t + 1)] = val[t]

    lax.fori_loop(0, 2, second, 0)
    settle(outer1)
    mine[0, 0] += from_left[0:16, :]
    mine[0, X - 1] += from_right[0:16, :]

    def pack(m):
        for x in range(X):
            pbuf[m, 13 * x:13 * x + 13, :] = mine[m, x, 0:13, :]

    def chunk_of(o):
        return (pl.ds(pl.multiple_of(CH * (o // LT), 8), CH), pl.ds(pl.multiple_of(128 * lax.rem(o, LT), 128), 128))

    def send_parts(m):
        def send(j, c):
            o = lax.rem(place + j, PEERS)
            r, k = chunk_of(o)
            pltpu.make_async_remote_copy(pbuf.at[m, r, k], rsbuf.at[m, j], s_rs.at[m], r_rs.at[m],
                                         device_id=peer(o), device_id_type=MESH).start()
            return c

        lax.fori_loop(1, PEERS, send, 0)

    def all_parts(m):
        return rsbuf.at[m, pl.ds(1, PEERS - 1)]

    def across(m):
        return pltpu.make_async_remote_copy(ssum.at[m], xbuf.at[m], s_x.at[m], r_x.at[m],
                                            device_id=partner, device_id_type=MESH)

    def own_sum(m):
        pltpu.make_async_copy(all_parts(m), all_parts(m), r_rs.at[m]).wait()
        r, k = chunk_of(place)
        acc = pbuf[m, r, k]
        for j in range(1, PEERS):
            acc = acc + rsbuf[m, j]
        ssum[m] = acc
        across(m).start()

    def send_total(m):
        across(m).wait()
        val = ssum[m] + xbuf[m]
        total[m] = val
        r, k = chunk_of(place)
        fbuf[m, r, k] = val

        def send(j, c):
            pltpu.make_async_remote_copy(total.at[m], fbuf.at[m, r, k], s_ag.at[m], r_ag.at[m],
                                         device_id=peer(lax.rem(place + j, PEERS)), device_id_type=MESH).start()
            return c

        lax.fori_loop(1, PEERS, send, 0)

    def all_totals(m):
        pltpu.make_async_copy(all_parts(m), all_parts(m), r_ag.at[m]).wait()

    def all_sent(m):
        pltpu.make_async_copy(all_parts(m), all_parts(m), s_rs.at[m]).wait()
        pltpu.make_async_copy(all_parts(m), all_parts(m), s_ag.at[m]).wait()

    pack(0)
    send_parts(0)
    lax.fori_loop(2, X, second, 0)

    settle(halo)
    speed = ct[1]
    to_lower = jnp.where(speed > 0, 0.0, -speed)
    to_upper = jnp.where(speed > 0, speed, 0.0)
    al_l, al_r = alpha_row(rwl, X - 1), alpha_row(rwr, 0)
    for i in range(LT):
        c = slice(128 * i, 128 * (i + 1))
        at_[1, :, c] = to_lower * dt[1, :, c] * al_l[:, c]
        at_[X + 2, :, c] = to_upper * dt[X, :, c] * al_r[:, c]

    def ends(j, c):
        products((X + 1) * j)
        return c

    lax.fori_loop(0, 2, ends, 0)

    edges[0, 16:32, :] = stencil_edge(q2, 0) + q2[1, 32:48, :]
    edges[0, 32:48, :] = q2[0, 32:48, :]
    edges[1, 16:32, :] = stencil_edge(q2, X + 1) + q2[X, 16:32, :]
    edges[1, 32:48, :] = q2[X + 1, 16:32, :]
    outer2 = swap(2, edges.at[1, pl.ds(16, 32)], from_left.at[pl.ds(16, 32)],
                  edges.at[0, pl.ds(16, 32)], from_right.at[pl.ds(16, 32)])

    def sum_second(x, c):
        mine[1, x] = stencil_moments(q2, x + 1)
        return c

    lax.fori_loop(0, X, sum_second, 0)
    own_sum(0)

    def edge_third(j, c):
        third((X + 1) * j)
        return c

    lax.fori_loop(0, 2, edge_third, 0)
    for i in range(LT):
        c = slice(128 * i, 128 * (i + 1))
        aa[0, :, c] = to_lower * at_[1, :, c]
        aa[X + 3, :, c] = to_upper * at_[X + 2, :, c]
    settle(outer2)
    mine[1, 0] += from_left[16:32, :]
    mine[1, 1] += from_left[32:48, :]
    mine[1, X - 1] += from_right[16:32, :]
    mine[1, X - 2] += from_right[32:48, :]
    pack(1)
    send_total(0)
    send_parts(1)

    core = lax.rem(s, 2)
    mate = (v, s + 1 - 2 * core)
    over = (v, lax.rem(s + 2, 4))
    half = LV // 2
    mine_v = pl.ds(pl.multiple_of(half * core, 8), half)
    mate_v = pl.ds(pl.multiple_of(half * (1 - core), 8), half)
    out_end = pl.ds((X + 2) * core, 2)
    in_end = pl.ds((X + 2) * (1 - core), 2)

    def hand(i, src, dst, to):
        c = pltpu.make_async_remote_copy(src, dst, s_e.at[i], r_e.at[i], device_id=to, device_id_type=MESH)
        c.start()
        return c

    give = hand(0, aa.at[out_end, mate_v], cin, mate)
    near = hand(1, aa.at[in_end], cnear, mate)

    def inner_third(i, c):
        third(i)
        return c

    lax.fori_loop(1, 3, inner_third, 0)
    give.wait()
    cout[...] = aa[out_end, mine_v, :] + cin[...]
    over_0 = hand(2, cout.at[0], cfar.at[0], over)
    lax.fori_loop(3, 7, inner_third, 0)

    all_totals(0)
    l1[0:64, :] = jnp.dot(kx[0:64, :], fbuf[0, 0:104, :], precision=HIGHEST, preferred_element_type=F32)
    for k in range(8):
        h_out[0, HALO * k:HALO * (k + 1), :] = l1[8 * k:8 * k + HALO, :]
        h_out[1, HALO * k:HALO * (k + 1), :] = l1[8 * k + X - HALO:8 * k + X, :]
    halo2 = swap(3, h_out.at[1], h_left, h_out.at[0], h_right)
    own_sum(1)
    l1[64:168, :] = jnp.dot(kx[64:168, :], fbuf[0, 0:104, :], precision=HIGHEST, preferred_element_type=F32)
    lax.fori_loop(7, X + 1, inner_third, 0)
    send_total(1)
    over_1 = hand(3, cout.at[1], cfar.at[1], over)
    settle(halo2)

    zero8 = jnp.zeros((8, CELLS), F32)

    def clear_ends(k, c):
        for i in range(2):
            u[i, k, 0:8, :] = zero8
            u[i, k, 24:32, :] = zero8
        return c

    lax.fori_loop(0, 4, clear_ends, 0)

    def fill(k, lo_rows, own, hi_rows):
        b[k, 0:HALO, :] = lo_rows
        b[k, HALO:HALO + X, :] = own
        b[k, HALO + X:EXT, :] = hi_rows

    def smooth():
        def start(k, c):
            u[0, k, 8:24, :] = b[k]
            return c

        lax.fori_loop(0, 4, start, 0)
        for sweep in range(SWEEPS):
            src, dst = sweep % 2, 1 - sweep % 2

            def row(k, c):
                for blk in range(2):
                    lo = 8 + 8 * blk
                    here, ylo, yhi, zlo, zhi = yz_shifts(u[src, k, lo:lo + 8, :])
                    near = u[src, k, lo - 1:lo + 7, :] + u[src, k, lo + 1:lo + 9, :]
                    side = cat([(ylo[i] + yhi[i]) + (zlo[i] + zhi[i]) for i in range(LT)])
                    u[dst, k, lo:lo + 8, :] = (b[k, 8 * blk:8 * blk + 8, :] + coupling * (near + side)) * (1.0 / (1.0 + 6.0 * coupling))
                return c

            lax.fori_loop(0, 4, row, 0)
        return SWEEPS % 2

    for k in range(4):
        fill(k, h_left[4 * k:4 * k + 4, :], l1[8 * k:8 * k + 8, :], h_right[4 * k:4 * k + 4, :])
    last = smooth()

    def gammas(relax, wall):
        return jnp.where(wall > 0, 0.0, relax), jnp.where(wall > 0, 1.0, relax)

    own_alpha = alpha_of(rw[0:X, :], rw[X:2 * X, :])
    factors = [gammas(ref[0:X, :], ref[X:2 * X, :]) for ref in (rwl, rw, rwr)]
    for k in range(8):
        gl, go, gr = (f[1 if k in (3, 4) else 0] for f in factors)
        if k < 4:
            lo_rows = u[last, k, 8:8 + HALO, :]
            own = u[last, k, 8 + HALO:8 + HALO + X, :]
            hi_rows = u[last, k, 8 + HALO + X:8 + EXT, :]
        else:
            lo_rows = h_left[4 * k:4 * k + 4, :]
            own = l1[8 * k:8 * k + 8, :]
            hi_rows = h_right[4 * k:4 * k + 4, :]
        own = own * go
        g1[EXT * k:EXT * k + HALO, :] = lo_rows * gl[4:8]
        g1[EXT * k + HALO:EXT * k + HALO + X, :] = own
        g1[EXT * k + HALO + X:EXT * (k + 1), :] = hi_rows * gr[0:4]
        here, ylo, yhi, zlo, zhi = yz_shifts(own)
        for j, val in enumerate((ylo, yhi, zlo, zhi)):
            rhs[64 * j + 8 * k:64 * j + 8 * k + 8, :] = cat(val)
        at = EXT * k + HALO
        before = tiles(g1[at - 1:at + 7, :])
        after = tiles(g1[at + 1:at + 9, :])
        for t in range(LT):
            al = own_alpha[:, 128 * t:128 * (t + 1)]
            for o, val in enumerate((here, before, after, ylo, yhi, zlo, zhi)):
                dbuf[t, 64 * o + 8 * k:64 * o + 8 * k + 8, :] = val[t] * al

    def squares(l, sm):
        acc = jnp.zeros((8, CELLS), F32)
        for i in range(9):
            d = l[64 + 8 * i:72 + 8 * i, :]
            acc = acc + d * d
        for k in range(4):
            d = u[sm, k, 8 + HALO:8 + HALO + X, :] - l[136 + 8 * k:144 + 8 * k, :]
            acc = acc + d * d
        parts = tiles(acc)
        out = parts[0]
        for i in range(1, LT):
            out = out + parts[i]
        return out

    nsend[0] = squares(l1, last)

    add[...] = (
        jnp.dot(nc[:, 0:128], g1[...], precision=HIGHEST, preferred_element_type=F32)
        + jnp.dot(nc[:, 128:384], rhs[...], precision=HIGHEST, preferred_element_type=F32)
    )

    def spread(x, c):
        for t in range(LT):
            hi, lo = split(dbuf[t, pl.ds(x, 56, stride=X), :])
            both_parts = jnp.concatenate([hi.astype(F32), lo.astype(F32)], 0).astype(BF16)
            cols = slice(128 * t, 128 * (t + 1))
            dhl[x, 0:112, cols] = both_parts
            dhl[x, 112:224, cols] = both_parts
        return c

    over_0.wait()
    over_1.wait()
    share = hand(4, cfar, cboth, mate)
    all_totals(1)
    m2 = fbuf[1, 0:104, :] + add[...]
    b2out[...] = jnp.dot(kx[0:32, :], m2, precision=HIGHEST, preferred_element_type=F32)
    for k in range(4):
        b2_out[0, HALO * k:HALO * (k + 1), :] = b2out[8 * k:8 * k + HALO, :]
        b2_out[1, HALO * k:HALO * (k + 1), :] = b2out[8 * k + X - HALO:8 * k + X, :]
    halo3 = swap(6, b2_out.at[1], b2l, b2_out.at[0], b2r)
    l2[...] = jnp.dot(kx[32:208, :], m2, precision=HIGHEST, preferred_element_type=F32)

    def combine(x):
        aa[x + 2] = jnp.dot(lt[...], dhl[x, 0:224, :], preferred_element_type=F32) + alpha_row(rw, x) * aa[x + 2]

    def middle(x, c):
        combine(x)
        return c

    lax.fori_loop(0, X, spread, 0)
    lax.fori_loop(2, X - 2, middle, 0)
    near.wait()
    share.wait()
    is_upper = (core == 0).astype(F32)
    from_far = 2 + (X - 2) * core
    from_near = 2 + (X - 2) * (1 - core)

    def add_ends(i, carry):
        for t in range(LT):
            c = slice(128 * t, 128 * (t + 1))
            aa[from_near + i, :, c] += cnear[i, :, c]
            aa[from_far + i, mine_v, c] += jnp.where(wanted_of(mine_v) > 0, cfar[i, :, c], 0.0)
            aa[from_far + i, mate_v, c] += jnp.where(wanted_of(mate_v) > 0, cboth[i, :, c], 0.0)
        return carry

    def wanted_of(rows):
        towards = ct[1, rows, :]
        return jnp.where(towards > 0, is_upper, 1.0 - is_upper)

    lax.fori_loop(0, 2, add_ends, 0)

    settle(halo3)
    for k in range(4):
        fill(k, b2l[4 * k:4 * k + 4, :], b2out[8 * k:8 * k + 8, :], b2r[4 * k:4 * k + 4, :])
    last = smooth()
    acc = jnp.zeros((8, CELLS), F32)
    for i in range(9):
        d = l2[32 + 8 * i:40 + 8 * i, :]
        acc = acc + d * d
    for k in range(4):
        d = u[last, k, 8 + HALO:8 + HALO + X, :] - l2[104 + 8 * k:112 + 8 * k, :]
        acc = acc + d * d
    parts = tiles(acc)
    out = parts[0]
    for i in range(1, LT):
        out = out + parts[i]
    nsend[1] = out
    notes = []
    for j in (1, 2, 3):
        c = pltpu.make_async_remote_copy(nsend, nrecv.at[j - 1], s_nm.at[j - 1], r_nm.at[j - 1],
                                         device_id=(v, lax.rem(s + j, 4)), device_id_type=MESH)
        c.start()
        notes.append(c)

    beta, both = gammas(rw[0:X, :], rw[X:2 * X, :])
    for k in range(8):
        f = u[last, k, 8 + HALO:8 + HALO + X, :] if k < 4 else l2[8 * k - 32:8 * k - 24, :]
        g2_out[8 * k:8 * k + 8, :] = f * (both if k in (3, 4) else beta)

    tile = pl.ds(pl.multiple_of(128 * (v // 4), 128), 128)
    turn = lax.rem(128 - 32 * lax.rem(v, 4), 128)
    for r in range(MOM):
        if 1 <= r <= 4:
            f = u[last, r - 1, 8 + HALO:8 + HALO + X, tile]
        elif r == 0:
            f = l2[0:8, tile]
        elif r >= 10:
            f = l2[8 + 8 * (r - 10):16 + 8 * (r - 10), tile]
        else:
            f = l2[136 + 8 * (r - 5):144 + 8 * (r - 5), tile]
        mac_out[r] = pltpu.roll(f, turn, 1)[:, 0:32]

    def outside(j, c):
        combine(lax.rem(j + X - 2, X))
        return c

    lax.fori_loop(0, 4, outside, 0)

    settle(notes)
    for i in range(2):
        norm_out[i] = (nsend[i] + nrecv[0, i]) + (nrecv[1, i] + nrecv[2, i])
    for m in range(2):
        all_sent(m)


def stencil_edge(q_ref, p):
    def rows(o):
        return tiles(q_ref[p, 16 * o:16 * o + 16, :])

    ylo, _ = y_shifts(rows(3))
    _, yhi = y_shifts(rows(4))
    zlo, _ = z_shifts(rows(5))
    _, zhi = z_shifts(rows(6))
    here = rows(0)
    return cat([here[i] + (ylo[i] + yhi[i]) + (zlo[i] + zhi[i]) for i in range(LT)])


PAIRS = 4


def renew(a_ref, g2_ref, vel_ref, mac_ref, sum_ref, out_hbm, mac_out, norm_out, obuf, stage, rhs, lt, sem_out):
    mac_out[...] = mac_ref[...]
    for i in range(2):
        norm_out[i] = jnp.sqrt(jnp.sum(sum_ref[i]))

    vel = speed_range * (2.0 * vel_ref[...].astype(F32) + 1.0 - NVX) / NVX
    _, target, _ = functions_of(vel[0:1], vel[1:2], vel[2:3])
    for k in range(8):
        stage[0, k:k + 1, :] = target[k]
    hi, lo = split(stage[0, 0:8, :])
    hi, lo = hi.astype(F32), lo.astype(F32)
    quad = jnp.concatenate([hi, hi, lo, lo, jnp.zeros((96, LV), F32)], 0)
    lt[...] = jnp.transpose(quad)[:, 0:32].astype(BF16)

    for t in range(LT):
        stage[t] = g2_ref[:, 128 * t:128 * (t + 1)]

    def spread(x, c):
        for t in range(LT):
            hi, lo = split(stage[t, pl.ds(x, 8, stride=X), :])
            both_parts = jnp.concatenate([hi.astype(F32), lo.astype(F32)], 0).astype(BF16)
            cols = slice(128 * t, 128 * (t + 1))
            rhs[x, 0:16, cols] = both_parts
            rhs[x, 16:32, cols] = both_parts
        return c

    lax.fori_loop(0, X, spread, 0)

    puts = []
    for i in range(PAIRS):
        pair = slice(256 * i, 256 * (i + 1))

        def plane(x, c):
            val = jnp.dot(lt[...], rhs[x, :, pair], preferred_element_type=F32) + a_ref[x + 2, :, pair]
            obuf[2 * i, pl.ds(x, LV, stride=X), :] = val[:, 0:128]
            obuf[2 * i + 1, pl.ds(x, LV, stride=X), :] = val[:, 128:256]
            return c

        lax.fori_loop(0, X, plane, 0)
        for t in (2 * i, 2 * i + 1):
            c = pltpu.make_async_copy(obuf.at[t], out_hbm.at[:, pl.ds(128 * t, 128)], sem_out.at[t])
            c.start()
            puts.append(c)
    for c in puts:
        c.wait()


def shards(consts, dist, vel_index, relax, wall_mask, macro_inverse):
    vmem = pl.BlockSpec(memory_space=pltpu.VMEM)
    hbm = pl.BlockSpec(memory_space=pl.ANY)
    smem = pl.BlockSpec(memory_space=pltpu.SMEM)
    dma = pltpu.SemaphoreType.DMA
    sds = jax.ShapeDtypeStruct
    a, g2, mac, norm = pl.pallas_call(
        exchange,
        out_shape=(
            pltpu.VMEM((X + 4, LV, CELLS), F32), pltpu.VMEM((64, CELLS), F32),
            pltpu.VMEM((MOM, X, 32), F32), pltpu.VMEM((2, 8, 128), F32),
        ),
        in_specs=[hbm] + [vmem] * 9,
        out_specs=(vmem,) * 4,
        scratch_shapes=[
            pltpu.VMEM((LT, LV * X, 128), F32),
            pltpu.VMEM((X + 2, LV, CELLS), F32),
            pltpu.VMEM((X + 4, LV, CELLS), F32),
            pltpu.VMEM((X, 2 * LV, CELLS), BF16),
            pltpu.VMEM((X + 2, 2 * LV, CELLS), BF16),
            pltpu.VMEM((X + 2, 112, CELLS), F32),
            pltpu.VMEM((X + 2, 112, CELLS), F32),
            pltpu.VMEM((2, X, 16, CELLS), F32),
            pltpu.VMEM((2, 48, CELLS), F32),
            pltpu.VMEM((48, CELLS), F32),
            pltpu.VMEM((48, CELLS), F32),
            pltpu.VMEM((2 * X, CELLS), F32),
            pltpu.VMEM((2 * X, CELLS), F32),
            pltpu.VMEM((2 * X, CELLS), F32),
            pltpu.VMEM((16, LV), F32),
            pltpu.VMEM((224, 2 * LV), BF16),
            pltpu.VMEM((4, LV, LV), F32),
            pltpu.VMEM((2 * LV, 2 * LV), BF16),
            pltpu.VMEM((26 * X, X * MOM), F32),
            pltpu.VMEM((2, 2 * CH, CELLS), F32),
            pltpu.VMEM((2, PEERS, CH, 128), F32),
            pltpu.VMEM((2, CH, 128), F32),
            pltpu.VMEM((2, CH, 128), F32),
            pltpu.VMEM((2, CH, 128), F32),
            pltpu.VMEM((2, 2 * CH, CELLS), F32),
            pltpu.VMEM((26 * X, CELLS), F32),
            pltpu.VMEM((2, 32, CELLS), F32),
            pltpu.VMEM((32, CELLS), F32),
            pltpu.VMEM((32, CELLS), F32),
            pltpu.VMEM((32, CELLS), F32),
            pltpu.VMEM((2, 16, CELLS), F32),
            pltpu.VMEM((16, CELLS), F32),
            pltpu.VMEM((16, CELLS), F32),
            pltpu.VMEM((2, 4, 32, CELLS), F32),
            pltpu.VMEM((4, EXT, CELLS), F32),
            pltpu.VMEM((8 * EXT, CELLS), F32),
            pltpu.VMEM((256, CELLS), F32),
            pltpu.VMEM((56, LV), F32),
            pltpu.VMEM((LV, 224), BF16),
            pltpu.VMEM((X * MOM, CELLS), F32),
            pltpu.VMEM((22 * X, CELLS), F32),
            pltpu.VMEM((2, 8, 128), F32),
            pltpu.VMEM((3, 2, 8, 128), F32),
            pltpu.VMEM((2, LV // 2, CELLS), F32),
            pltpu.VMEM((2, LV // 2, CELLS), F32),
            pltpu.VMEM((2, LV // 2, CELLS), F32),
            pltpu.VMEM((2, LV // 2, CELLS), F32),
            pltpu.VMEM((2, LV, CELLS), F32),
            dma((LT,)), dma((14,)), dma((14,)), dma((2,)), dma((2,)), dma((2,)), dma((2,)), dma((2,)), dma((2,)),
            dma((3,)), dma((3,)), dma((5,)), dma((5,)),
        ],
        compiler_params=pltpu.CompilerParams(collective_id=0, has_side_effects=True, vmem_limit_bytes=54 * 2 ** 20),
        name="exchange",
    )(dist.reshape(LV * X, CELLS), relax, wall_mask, vel_index, macro_inverse, *consts)

    out, mac, norm = pl.pallas_call(
        renew,
        out_shape=(sds((LV * X, CELLS), F32), sds((MOM, X, 32), F32), sds((2,), F32)),
        in_specs=[vmem] * 5,
        out_specs=(hbm, vmem, smem),
        scratch_shapes=[
            pltpu.VMEM((LT, LV * X, 128), F32),
            pltpu.VMEM((LT, 64, 128), F32),
            pltpu.VMEM((X, 32, CELLS), BF16),
            pltpu.VMEM((LV, 32), BF16),
            dma((LT,)),
        ],
        compiler_params=pltpu.CompilerParams(vmem_limit_bytes=32 * 2 ** 20),
        name="renew",
    )(a, g2, vel_index, mac, norm)
    return (out.reshape(LV, X, CELLS), mac, norm)


def solution(mesh):
    consts = selection() + [coupling_table()]
    return jax.shard_map(
        lambda *args: shards([jnp.asarray(c) for c in consts], *args),
        mesh=mesh,
        in_specs=(P("vel", "space", None), P(None, "vel"), P("space", None), P("space", None), P()),
        out_specs=(P("vel", "space", None), P(None, "space", "vel"), P()),
        check_vma=False,
    )
```

```python
import functools
import math

import jax
import jax.numpy as jnp
import numpy as np
from jax import lax
from jax.experimental import pallas as pl
from jax.experimental.pallas import tpu as pltpu
from jax.sharding import PartitionSpec as P

NVX = 16
NZ = 16
MOM = 13
SWEEPS = 3
speed_range = 4.0
time_step = 0.08
coupling = 0.5

MESH = pl.DeviceIdType.MESH
F32 = jnp.float32
BF16 = jnp.bfloat16
X = 8
CELLS = 1024
LT = CELLS // 128
RING = 4
PEERS = RING * RING
LV = 128
CH = 56
HALO = 4
EXT = X + 2 * HALO
FIELD_ROWS = (1, 2, 3, 4, 0, 10, 11, 12)
OTHER_ROWS = (0, 5, 6, 7, 8, 9, 10, 11, 12)
HIGHEST = lax.Precision.HIGHEST


def functions_of(cx, cy, cz, xp=jnp):
    square = cx * cx + cy * cy + cz * cz
    weights = (2.0 * speed_range / NVX) ** 3 * math.pi ** (-1.5) * xp.exp(-square)
    heat = square - 2.5
    one = xp.ones_like(cx)
    rows = [
        one, cx, cy, cz, 2.0 * square / 3.0 - 1.0,
        2.0 * cx * cy, 2.0 * cx * cz, 2.0 * cy * cz,
        cx * cx - cy * cy, cy * cy - cz * cz,
        cx * heat, cy * heat, cz * heat,
    ]
    factor = 4.0 / 15.0
    target = [2.0 * cx, 2.0 * cy, 2.0 * cz, square - 1.5, one, factor * cx * heat, factor * cy * heat, factor * cz * heat]
    stencil = [1.0 - time_step * (xp.abs(cx) + xp.abs(cy) + xp.abs(cz))]
    for c in (cx, cy, cz):
        stencil += [time_step * xp.maximum(c, 0.0), time_step * xp.maximum(-c, 0.0)]
    return [r * weights for r in rows], target, stencil


def selection():
    sel = np.zeros((26, MOM))
    own = np.zeros((26, MOM))
    for j in range(26):
        if j < 8:
            sel[j, FIELD_ROWS[j]] = 1
        elif j < 17:
            sel[j, OTHER_ROWS[j - 8]] = 1
            own[j, OTHER_ROWS[j - 8]] = -1
        elif j < 21:
            own[j, j - 16] = 1
        else:
            sel[j, j - 16] = 1
    eye = np.eye(X)
    sel = np.repeat(sel, X, 0)
    spread = np.tile(np.eye(MOM), (1, X))
    mask = np.repeat(np.tile(eye, (26, 1)), MOM, 1)
    fixed = np.einsum("jr,xp->jxpr", own, eye).reshape(26 * X, X * MOM)
    return [a.astype(np.float32) for a in (sel, spread, mask, fixed)]


def coupling_table():
    line = speed_range * (2.0 * np.arange(NVX) + 1.0 - NVX) / NVX
    cx, cy, cz = (a.reshape(-1) for a in np.meshgrid(line, line, line, indexing="ij"))
    rows, target, stencil = functions_of(cx, cy, cz, np)
    n = np.einsum("rv,ov,kv->ork", rows, stencil, target)
    near = np.zeros((X, MOM, 8, EXT))
    side = np.zeros((X, MOM, 4, 8, X))
    for x in range(X):
        near[x, :, :, x + HALO] += n[0]
        near[x, :, :, x + HALO - 1] += n[1]
        near[x, :, :, x + HALO + 1] += n[2]
        for j in range(4):
            side[x, :, j, :, x] += n[3 + j]
    table = np.concatenate([near.reshape(X * MOM, 8 * EXT), side.reshape(X * MOM, 32 * X)], 1)
    return table.astype(np.float32)


def split(a):
    hi = a.astype(BF16)
    return hi, (a - hi.astype(F32)).astype(BF16)


def cat(parts):
    return jnp.concatenate(parts, axis=1)


def tiles(x):
    return [x[:, 128 * i:128 * (i + 1)] for i in range(LT)]


def y_shifts(t):
    lane = lax.broadcasted_iota(jnp.int32, t[0].shape, 1)
    up = [pltpu.roll(a, 16, 1) for a in t]
    down = [pltpu.roll(a, 112, 1) for a in t]
    ylo = [jnp.where(lane < 16, up[i - 1], up[i]) for i in range(LT)]
    yhi = [jnp.where(lane >= 112, down[(i + 1) % LT], down[i]) for i in range(LT)]
    return ylo, yhi


def z_shifts(t):
    z = lax.broadcasted_iota(jnp.int32, t[0].shape, 1) % NZ
    zlo = [jnp.where(z == 0, pltpu.roll(a, 113, 1), pltpu.roll(a, 1, 1)) for a in t]
    zhi = [jnp.where(z == NZ - 1, pltpu.roll(a, 15, 1), pltpu.roll(a, 127, 1)) for a in t]
    return zlo, zhi


def yz_shifts(x):
    t = tiles(x)
    return (t,) + y_shifts(t) + z_shifts(t)


def stencil_moments(q_ref, p):
    def rows(o, at=p):
        return tiles(q_ref[at, 16 * o:16 * o + 16, :])

    ylo, _ = y_shifts(rows(3))
    _, yhi = y_shifts(rows(4))
    zlo, _ = z_shifts(rows(5))
    _, zhi = z_shifts(rows(6))
    here, before, after = rows(0), rows(1, p - 1), rows(2, p + 1)
    return cat([(here[i] + before[i] + after[i]) + (ylo[i] + yhi[i]) + (zlo[i] + zhi[i]) for i in range(LT)])


def alpha_of(relax, wall):
    return jnp.where(wall > 0, 0.0, 1.0 - relax)


def stream_plane(src, halves, p, h, ct, zmat, scale=None):
    lane = lax.broadcasted_iota(jnp.int32, (LV, 128), 1)
    k0, cx, cy, cz = (ct[i] for i in range(4))
    px, py, pz = cx > 0, cy > 0, cz > 0
    kx, ky, kz = jnp.abs(cx), jnp.abs(cy), jnp.abs(cz)
    t = [src[p, :, 128 * i:128 * (i + 1)] for i in range(LT)]
    z = [
        jnp.dot(
            cat([halves[h, 0:LV, 128 * i:128 * (i + 1)], halves[h, LV:2 * LV, 128 * i:128 * (i + 1)]]),
            zmat[...],
            preferred_element_type=F32,
        )
        for i in range(LT)
    ]
    up = [pltpu.roll(a, 16, 1) for a in t]
    down = [pltpu.roll(a, 112, 1) for a in t]
    out = []
    for i in range(LT):
        s = slice(128 * i, 128 * (i + 1))
        in_x = jnp.where(px, src[p - 1, :, s], src[p + 1, :, s])
        in_y = jnp.where(
            py,
            jnp.where(lane < 16, up[i - 1], up[i]),
            jnp.where(lane >= 112, down[(i + 1) % LT], down[i]),
        )
        in_z = jnp.where(pz, z[i][:, 0:128], z[i][:, 128:256])
        val = (k0 * t[i] + kx * in_x) + (ky * in_y + kz * in_z)
        out.append(val if scale is None else val * scale[:, s])
    return out


def exchange(dist_hbm, relax_ref, wall_ref, vel_ref, inv_ref, sel_ref, spread_ref, mask_ref, fixed_ref, nc,
             aa, g2_out, mac_out, norm_out,
             dbuf, dt, at_, dhl, ahl, q1, q2, mine, edges, from_left, from_right, rw, rwl, rwr,
             mrows, lm, ct, zmat, kx, pbuf, rsbuf, ssum, xbuf, total, fbuf, l1, h_out, h_left, h_right, b2out, b2_out, b2l, b2r,
             u, b, g1, rhs, lrows, lt, add, l2, nsend, nrecv, cin, cout, cfar, cboth, cnear,
             sem_ld, s_nb, r_nb, s_rs, r_rs, s_ag, r_ag, s_x, r_x, s_nm, r_nm, s_e, r_e):
    v = lax.axis_index("vel")
    s = lax.axis_index("space")
    left = (v, lax.rem(s + 3, 4))
    right = (v, lax.rem(s + 1, 4))
    far = v // PEERS
    place = lax.rem(v, PEERS)
    partner = ((1 - far) * PEERS + place, s)

    def peer(o):
        return (far * PEERS + o, s)

    loads = [pltpu.make_async_copy(dist_hbm.at[:, pl.ds(128 * t, 128)], dbuf.at[t], sem_ld.at[t]) for t in range(LT)]
    for c in loads:
        c.start()

    barrier = pltpu.get_barrier_semaphore()

    def greet(j, c):
        pl.semaphore_signal(barrier, inc=1, device_id=peer(lax.rem(place + j, PEERS)), device_id_type=MESH)
        return c

    lax.fori_loop(1, PEERS, greet, 0)
    pl.semaphore_signal(barrier, inc=1, device_id=partner, device_id_type=MESH)
    for j in (1, 2, 3):
        pl.semaphore_signal(barrier, inc=1, device_id=(v, lax.rem(s + j, 4)), device_id_type=MESH)

    rw[0:X, :] = relax_ref[...]
    rw[X:2 * X, :] = wall_ref[...].astype(F32)
    vel = speed_range * (2.0 * vel_ref[...].astype(F32) + 1.0 - NVX) / NVX
    cx, cy, cz = vel[0:1], vel[1:2], vel[2:3]
    rows, target, stencil = functions_of(cx, cy, cz)
    mrows[...] = jnp.zeros_like(mrows)
    for r in range(MOM):
        mrows[r:r + 1, :] = rows[r]
    for o in range(7):
        hi, lo = split(mrows[...] * stencil[o])
        lm[16 * o:16 * o + 16, 0:LV] = hi
        lm[16 * o:16 * o + 16, LV:2 * LV] = hi
        lm[112 + 16 * o:128 + 16 * o, 0:LV] = lo
        lm[112 + 16 * o:128 + 16 * o, LV:2 * LV] = jnp.zeros_like(lo)
    for i, row in enumerate((stencil[0], time_step * cx, time_step * cy, time_step * cz)):
        ct[i] = jnp.transpose(jnp.broadcast_to(row, (LV, LV)))
    for k in range(8):
        for o in range(7):
            lrows[8 * o + k:8 * o + k + 1, :] = stencil[o] * target[k]
    hi, lo = split(lrows[...])
    hi, lo = hi.astype(F32), lo.astype(F32)
    quad = jnp.concatenate([hi, hi, lo, lo, jnp.zeros((32, LV), F32)], 0)
    lt[:, 0:128] = jnp.transpose(quad[0:128]).astype(BF16)
    lt[:, 128:224] = jnp.transpose(quad[128:256])[:, 0:96].astype(BF16)
    src_lane = lax.broadcasted_iota(jnp.int32, (LV, LV), 0)
    dst_lane = lax.broadcasted_iota(jnp.int32, (LV, LV), 1)
    dst_z = dst_lane % NZ
    lower = jnp.where(src_lane == jnp.where(dst_z == 0, dst_lane + NZ - 1, dst_lane - 1), 1.0, 0.0).astype(BF16)
    upper = jnp.where(src_lane == jnp.where(dst_z == NZ - 1, dst_lane - NZ + 1, dst_lane + 1), 1.0, 0.0).astype(BF16)
    for i in range(2):
        zmat[LV * i:LV * (i + 1), 0:LV] = lower
        zmat[LV * i:LV * (i + 1), LV:2 * LV] = upper
    part = jnp.dot(sel_ref[...], inv_ref[...], precision=HIGHEST, preferred_element_type=F32)
    part = jnp.dot(part, spread_ref[...], precision=HIGHEST, preferred_element_type=F32)
    kx[...] = part * mask_ref[...] + fixed_ref[...]
    zero_plane = jnp.zeros((LV, CELLS), F32)
    for p in (0, 9):
        dt[p] = zero_plane
        q1[p, 16:48, :] = jnp.zeros((32, CELLS), F32)
    for p in (0, 11):
        at_[p] = zero_plane
    for m in range(2):
        pbuf[m, 104:112, :] = jnp.zeros((8, CELLS), F32)

    def swap(i, to_right, right_dst, to_left, left_dst):
        a = pltpu.make_async_remote_copy(to_right, right_dst, s_nb.at[2 * i], r_nb.at[2 * i],
                                         device_id=right, device_id_type=MESH)
        c = pltpu.make_async_remote_copy(to_left, left_dst, s_nb.at[2 * i + 1], r_nb.at[2 * i + 1],
                                         device_id=left, device_id_type=MESH)
        a.start()
        c.start()
        return a, c

    def settle(copies):
        for c in copies:
            c.wait()

    settle(loads)

    def first(x, c):
        val = cat([dbuf[t, pl.ds(x, LV, stride=X), :] for t in range(LT)])
        dt[x + 1] = val
        hi, lo = split(val)
        dhl[x, 0:LV, :] = hi
        dhl[x, LV:2 * LV, :] = lo
        q = jnp.dot(lm[...], dhl[x], preferred_element_type=F32)
        q1[x + 1] = q[0:112] + q[112:224]
        return c

    lax.fori_loop(0, X, first, 0)
    pl.semaphore_wait(barrier, PEERS - 1 + 1 + 3)
    edges[0, 0:16, :] = q1[1, 32:48, :]
    edges[1, 0:16, :] = q1[X, 16:32, :]
    outer1 = swap(1, edges.at[1, pl.ds(0, 16)], from_left.at[pl.ds(0, 16)],
                  edges.at[0, pl.ds(0, 16)], from_right.at[pl.ds(0, 16)])
    halo = swap(0, rw, rwl, rw, rwr)

    def sum_first(x, c):
        mine[0, x] = stencil_moments(q1, x + 1)
        return c

    lax.fori_loop(0, X, sum_first, 0)

    def alpha_row(ref, x):
        return alpha_of(ref[pl.ds(x, 1), :], ref[pl.ds(x + X, 1), :])

    def products(i):
        hi, lo = split(at_[i + 1])
        ahl[i, 0:LV, :] = hi
        ahl[i, LV:2 * LV, :] = lo
        q = jnp.dot(lm[...], ahl[i], preferred_element_type=F32)
        q2[i] = q[0:112] + q[112:224]

    def second(j, c):
        x = lax.rem(X - j, X)

        val = stream_plane(dt, dhl, x + 1, x, ct, zmat, alpha_row(rw, x))
        for i in range(LT):
            at_[x + 2, :, 128 * i:128 * (i + 1)] = val[i]
        products(x + 1)
        return c

    def third(i):
        val = stream_plane(at_, ahl, i + 1, i, ct, zmat)
        for t in range(LT):
            aa[i + 1, :, 128 * t:128 * (t + 1)] = val[t]

    lax.fori_loop(0, 2, second, 0)
    settle(outer1)
    mine[0, 0] += from_left[0:16, :]
    mine[0, X - 1] += from_right[0:16, :]

    def pack(m):
        for x in range(X):
            pbuf[m, 13 * x:13 * x + 13, :] = mine[m, x, 0:13, :]

    def chunk_of(o):
        return (pl.ds(pl.multiple_of(CH * (o // LT), 8), CH), pl.ds(pl.multiple_of(128 * lax.rem(o, LT), 128), 128))

    def send_parts(m):
        def send(j, c):
            o = lax.rem(place + j, PEERS)
            r, k = chunk_of(o)
            pltpu.make_async_remote_copy(pbuf.at[m, r, k], rsbuf.at[m, j], s_rs.at[m], r_rs.at[m],
                                         device_id=peer(o), device_id_type=MESH).start()
            return c

        lax.fori_loop(1, PEERS, send, 0)

    def all_parts(m):
        return rsbuf.at[m, pl.ds(1, PEERS - 1)]

    def across(m):
        return pltpu.make_async_remote_copy(ssum.at[m], xbuf.at[m], s_x.at[m], r_x.at[m],
                                            device_id=partner, device_id_type=MESH)

    def own_sum(m):
        pltpu.make_async_copy(all_parts(m), all_parts(m), r_rs.at[m]).wait()
        r, k = chunk_of(place)
        acc = pbuf[m, r, k]
        for j in range(1, PEERS):
            acc = acc + rsbuf[m, j]
        ssum[m] = acc
        across(m).start()

    def send_total(m):
        across(m).wait()
        val = ssum[m] + xbuf[m]
        total[m] = val
        r, k = chunk_of(place)
        fbuf[m, r, k] = val

        def send(j, c):
            pltpu.make_async_remote_copy(total.at[m], fbuf.at[m, r, k], s_ag.at[m], r_ag.at[m],
                                         device_id=peer(lax.rem(place + j, PEERS)), device_id_type=MESH).start()
            return c

        lax.fori_loop(1, PEERS, send, 0)

    def all_totals(m):
        pltpu.make_async_copy(all_parts(m), all_parts(m), r_ag.at[m]).wait()

    def all_sent(m):
        pltpu.make_async_copy(all_parts(m), all_parts(m), s_rs.at[m]).wait()
        pltpu.make_async_copy(all_parts(m), all_parts(m), s_ag.at[m]).wait()

    pack(0)
    send_parts(0)
    lax.fori_loop(2, X, second, 0)

    settle(halo)
    speed = ct[1]
    to_lower = jnp.where(speed > 0, 0.0, -speed)
    to_upper = jnp.where(speed > 0, speed, 0.0)
    al_l, al_r = alpha_row(rwl, X - 1), alpha_row(rwr, 0)
    for i in range(LT):
        c = slice(128 * i, 128 * (i + 1))
        at_[1, :, c] = to_lower * dt[1, :, c] * al_l[:, c]
        at_[X + 2, :, c] = to_upper * dt[X, :, c] * al_r[:, c]

    def ends(j, c):
        products((X + 1) * j)
        return c

    lax.fori_loop(0, 2, ends, 0)

    edges[0, 16:32, :] = stencil_edge(q2, 0) + q2[1, 32:48, :]
    edges[0, 32:48, :] = q2[0, 32:48, :]
    edges[1, 16:32, :] = stencil_edge(q2, X + 1) + q2[X, 16:32, :]
    edges[1, 32:48, :] = q2[X + 1, 16:32, :]
    outer2 = swap(2, edges.at[1, pl.ds(16, 32)], from_left.at[pl.ds(16, 32)],
                  edges.at[0, pl.ds(16, 32)], from_right.at[pl.ds(16, 32)])

    def sum_second(x, c):
        mine[1, x] = stencil_moments(q2, x + 1)
        return c

    lax.fori_loop(0, X, sum_second, 0)
    own_sum(0)

    def edge_third(j, c):
        third((X + 1) * j)
        return c

    lax.fori_loop(0, 2, edge_third, 0)
    for i in range(LT):
        c = slice(128 * i, 128 * (i + 1))
        aa[0, :, c] = to_lower * at_[1, :, c]
        aa[X + 3, :, c] = to_upper * at_[X + 2, :, c]
    settle(outer2)
    mine[1, 0] += from_left[16:32, :]
    mine[1, 1] += from_left[32:48, :]
    mine[1, X - 1] += from_right[16:32, :]
    mine[1, X - 2] += from_right[32:48, :]
    pack(1)
    send_total(0)
    send_parts(1)

    core = lax.rem(s, 2)
    mate = (v, s + 1 - 2 * core)
    over = (v, lax.rem(s + 2, 4))
    half = LV // 2
    mine_v = pl.ds(pl.multiple_of(half * core, 8), half)
    mate_v = pl.ds(pl.multiple_of(half * (1 - core), 8), half)
    out_end = pl.ds((X + 2) * core, 2)
    in_end = pl.ds((X + 2) * (1 - core), 2)

    def hand(i, src, dst, to):
        c = pltpu.make_async_remote_copy(src, dst, s_e.at[i], r_e.at[i], device_id=to, device_id_type=MESH)
        c.start()
        return c

    give = hand(0, aa.at[out_end, mate_v], cin, mate)
    near = hand(1, aa.at[in_end], cnear, mate)

    def inner_third(i, c):
        third(i)
        return c

    lax.fori_loop(1, 3, inner_third, 0)
    give.wait()
    cout[...] = aa[out_end, mine_v, :] + cin[...]
    over_0 = hand(2, cout.at[0], cfar.at[0], over)
    lax.fori_loop(3, 8, inner_third, 0)

    all_totals(0)
    l1[0:64, :] = jnp.dot(kx[0:64, :], fbuf[0, 0:104, :], precision=HIGHEST, preferred_element_type=F32)
    for k in range(8):
        h_out[0, HALO * k:HALO * (k + 1), :] = l1[8 * k:8 * k + HALO, :]
        h_out[1, HALO * k:HALO * (k + 1), :] = l1[8 * k + X - HALO:8 * k + X, :]
    halo2 = swap(3, h_out.at[1], h_left, h_out.at[0], h_right)
    own_sum(1)
    l1[64:168, :] = jnp.dot(kx[64:168, :], fbuf[0, 0:104, :], precision=HIGHEST, preferred_element_type=F32)
    lax.fori_loop(8, X + 1, inner_third, 0)
    send_total(1)
    over_1 = hand(3, cout.at[1], cfar.at[1], over)
    settle(halo2)

    zero8 = jnp.zeros((8, CELLS), F32)

    def clear_ends(k, c):
        for i in range(2):
            u[i, k, 0:8, :] = zero8
            u[i, k, 24:32, :] = zero8
        return c

    lax.fori_loop(0, 4, clear_ends, 0)

    def fill(k, lo_rows, own, hi_rows):
        b[k, 0:HALO, :] = lo_rows
        b[k, HALO:HALO + X, :] = own
        b[k, HALO + X:EXT, :] = hi_rows

    def smooth():
        def start(k, c):
            u[0, k, 8:24, :] = b[k]
            return c

        lax.fori_loop(0, 4, start, 0)
        for sweep in range(SWEEPS):
            src, dst = sweep % 2, 1 - sweep % 2

            def row(k, c):
                for blk in range(2):
                    lo = 8 + 8 * blk
                    here, ylo, yhi, zlo, zhi = yz_shifts(u[src, k, lo:lo + 8, :])
                    near = u[src, k, lo - 1:lo + 7, :] + u[src, k, lo + 1:lo + 9, :]
                    side = cat([(ylo[i] + yhi[i]) + (zlo[i] + zhi[i]) for i in range(LT)])
                    u[dst, k, lo:lo + 8, :] = (b[k, 8 * blk:8 * blk + 8, :] + coupling * (near + side)) * (1.0 / (1.0 + 6.0 * coupling))
                return c

            lax.fori_loop(0, 4, row, 0)
        return SWEEPS % 2

    for k in range(4):
        fill(k, h_left[4 * k:4 * k + 4, :], l1[8 * k:8 * k + 8, :], h_right[4 * k:4 * k + 4, :])
    last = smooth()

    def gammas(relax, wall):
        return jnp.where(wall > 0, 0.0, relax), jnp.where(wall > 0, 1.0, relax)

    own_alpha = alpha_of(rw[0:X, :], rw[X:2 * X, :])
    factors = [gammas(ref[0:X, :], ref[X:2 * X, :]) for ref in (rwl, rw, rwr)]
    for k in range(8):
        gl, go, gr = (f[1 if k in (3, 4) else 0] for f in factors)
        if k < 4:
            lo_rows = u[last, k, 8:8 + HALO, :]
            own = u[last, k, 8 + HALO:8 + HALO + X, :]
            hi_rows = u[last, k, 8 + HALO + X:8 + EXT, :]
        else:
            lo_rows = h_left[4 * k:4 * k + 4, :]
            own = l1[8 * k:8 * k + 8, :]
            hi_rows = h_right[4 * k:4 * k + 4, :]
        own = own * go
        g1[EXT * k:EXT * k + HALO, :] = lo_rows * gl[4:8]
        g1[EXT * k + HALO:EXT * k + HALO + X, :] = own
        g1[EXT * k + HALO + X:EXT * (k + 1), :] = hi_rows * gr[0:4]
        here, ylo, yhi, zlo, zhi = yz_shifts(own)
        for j, val in enumerate((ylo, yhi, zlo, zhi)):
            rhs[64 * j + 8 * k:64 * j + 8 * k + 8, :] = cat(val)
        at = EXT * k + HALO
        before = tiles(g1[at - 1:at + 7, :])
        after = tiles(g1[at + 1:at + 9, :])
        for t in range(LT):
            al = own_alpha[:, 128 * t:128 * (t + 1)]
            for o, val in enumerate((here, before, after, ylo, yhi, zlo, zhi)):
                dbuf[t, 64 * o + 8 * k:64 * o + 8 * k + 8, :] = val[t] * al

    def squares(l, sm):
        acc = jnp.zeros((8, CELLS), F32)
        for i in range(9):
            d = l[64 + 8 * i:72 + 8 * i, :]
            acc = acc + d * d
        for k in range(4):
            d = u[sm, k, 8 + HALO:8 + HALO + X, :] - l[136 + 8 * k:144 + 8 * k, :]
            acc = acc + d * d
        parts = tiles(acc)
        out = parts[0]
        for i in range(1, LT):
            out = out + parts[i]
        return out

    nsend[0] = squares(l1, last)

    add[...] = (
        jnp.dot(nc[:, 0:128], g1[...], precision=HIGHEST, preferred_element_type=F32)
        + jnp.dot(nc[:, 128:384], rhs[...], precision=HIGHEST, preferred_element_type=F32)
    )

    def spread(x, c):
        for t in range(LT):
            hi, lo = split(dbuf[t, pl.ds(x, 56, stride=X), :])
            both_parts = jnp.concatenate([hi.astype(F32), lo.astype(F32)], 0).astype(BF16)
            cols = slice(128 * t, 128 * (t + 1))
            dhl[x, 0:112, cols] = both_parts
            dhl[x, 112:224, cols] = both_parts
        return c

    over_0.wait()
    over_1.wait()
    share = hand(4, cfar, cboth, mate)
    all_totals(1)
    m2 = fbuf[1, 0:104, :] + add[...]
    b2out[...] = jnp.dot(kx[0:32, :], m2, precision=HIGHEST, preferred_element_type=F32)
    for k in range(4):
        b2_out[0, HALO * k:HALO * (k + 1), :] = b2out[8 * k:8 * k + HALO, :]
        b2_out[1, HALO * k:HALO * (k + 1), :] = b2out[8 * k + X - HALO:8 * k + X, :]
    halo3 = swap(6, b2_out.at[1], b2l, b2_out.at[0], b2r)
    l2[...] = jnp.dot(kx[32:208, :], m2, precision=HIGHEST, preferred_element_type=F32)

    def combine(x):
        aa[x + 2] = jnp.dot(lt[...], dhl[x, 0:224, :], preferred_element_type=F32) + alpha_row(rw, x) * aa[x + 2]

    def middle(x, c):
        combine(x)
        return c

    lax.fori_loop(0, X, spread, 0)
    lax.fori_loop(2, X - 2, middle, 0)
    near.wait()
    share.wait()
    is_upper = (core == 0).astype(F32)
    from_far = 2 + (X - 2) * core
    from_near = 2 + (X - 2) * (1 - core)

    def add_ends(i, carry):
        for t in range(LT):
            c = slice(128 * t, 128 * (t + 1))
            aa[from_near + i, :, c] += cnear[i, :, c]
            aa[from_far + i, mine_v, c] += jnp.where(wanted_of(mine_v) > 0, cfar[i, :, c], 0.0)
            aa[from_far + i, mate_v, c] += jnp.where(wanted_of(mate_v) > 0, cboth[i, :, c], 0.0)
        return carry

    def wanted_of(rows):
        towards = ct[1, rows, :]
        return jnp.where(towards > 0, is_upper, 1.0 - is_upper)

    lax.fori_loop(0, 2, add_ends, 0)

    settle(halo3)
    for k in range(4):
        fill(k, b2l[4 * k:4 * k + 4, :], b2out[8 * k:8 * k + 8, :], b2r[4 * k:4 * k + 4, :])
    last = smooth()
    acc = jnp.zeros((8, CELLS), F32)
    for i in range(9):
        d = l2[32 + 8 * i:40 + 8 * i, :]
        acc = acc + d * d
    for k in range(4):
        d = u[last, k, 8 + HALO:8 + HALO + X, :] - l2[104 + 8 * k:112 + 8 * k, :]
        acc = acc + d * d
    parts = tiles(acc)
    out = parts[0]
    for i in range(1, LT):
        out = out + parts[i]
    nsend[1] = out
    notes = []
    for j in (1, 2, 3):
        c = pltpu.make_async_remote_copy(nsend, nrecv.at[j - 1], s_nm.at[j - 1], r_nm.at[j - 1],
                                         device_id=(v, lax.rem(s + j, 4)), device_id_type=MESH)
        c.start()
        notes.append(c)

    beta, both = gammas(rw[0:X, :], rw[X:2 * X, :])
    for k in range(8):
        f = u[last, k, 8 + HALO:8 + HALO + X, :] if k < 4 else l2[8 * k - 32:8 * k - 24, :]
        g2_out[8 * k:8 * k + 8, :] = f * (both if k in (3, 4) else beta)

    tile = pl.ds(pl.multiple_of(128 * (v // 4), 128), 128)
    turn = lax.rem(128 - 32 * lax.rem(v, 4), 128)
    for r in range(MOM):
        if 1 <= r <= 4:
            f = u[last, r - 1, 8 + HALO:8 + HALO + X, tile]
        elif r == 0:
            f = l2[0:8, tile]
        elif r >= 10:
            f = l2[8 + 8 * (r - 10):16 + 8 * (r - 10), tile]
        else:
            f = l2[136 + 8 * (r - 5):144 + 8 * (r - 5), tile]
        mac_out[r] = pltpu.roll(f, turn, 1)[:, 0:32]

    def outside(j, c):
        combine(lax.rem(j + X - 2, X))
        return c

    lax.fori_loop(0, 4, outside, 0)

    settle(notes)
    for i in range(2):
        norm_out[i] = (nsend[i] + nrecv[0, i]) + (nrecv[1, i] + nrecv[2, i])
    for m in range(2):
        all_sent(m)


def stencil_edge(q_ref, p):
    def rows(o):
        return tiles(q_ref[p, 16 * o:16 * o + 16, :])

    ylo, _ = y_shifts(rows(3))
    _, yhi = y_shifts(rows(4))
    zlo, _ = z_shifts(rows(5))
    _, zhi = z_shifts(rows(6))
    here = rows(0)
    return cat([here[i] + (ylo[i] + yhi[i]) + (zlo[i] + zhi[i]) for i in range(LT)])


PAIRS = 4


def renew(a_ref, g2_ref, vel_ref, mac_ref, sum_ref, out_hbm, mac_out, norm_out, obuf, stage, rhs, lt, sem_out):
    mac_out[...] = mac_ref[...]
    for i in range(2):
        norm_out[i] = jnp.sqrt(jnp.sum(sum_ref[i]))

    vel = speed_range * (2.0 * vel_ref[...].astype(F32) + 1.0 - NVX) / NVX
    _, target, _ = functions_of(vel[0:1], vel[1:2], vel[2:3])
    for k in range(8):
        stage[0, k:k + 1, :] = target[k]
    hi, lo = split(stage[0, 0:8, :])
    hi, lo = hi.astype(F32), lo.astype(F32)
    quad = jnp.concatenate([hi, hi, lo, lo, jnp.zeros((96, LV), F32)], 0)
    lt[...] = jnp.transpose(quad)[:, 0:32].astype(BF16)

    for t in range(LT):
        stage[t] = g2_ref[:, 128 * t:128 * (t + 1)]

    def spread(x, c):
        for t in range(LT):
            hi, lo = split(stage[t, pl.ds(x, 8, stride=X), :])
            both_parts = jnp.concatenate([hi.astype(F32), lo.astype(F32)], 0).astype(BF16)
            cols = slice(128 * t, 128 * (t + 1))
            rhs[x, 0:16, cols] = both_parts
            rhs[x, 16:32, cols] = both_parts
        return c

    lax.fori_loop(0, X, spread, 0)

    puts = []
    for i in range(PAIRS):
        pair = slice(256 * i, 256 * (i + 1))

        def plane(x, c):
            val = jnp.dot(lt[...], rhs[x, :, pair], preferred_element_type=F32) + a_ref[x + 2, :, pair]
            obuf[2 * i, pl.ds(x, LV, stride=X), :] = val[:, 0:128]
            obuf[2 * i + 1, pl.ds(x, LV, stride=X), :] = val[:, 128:256]
            return c

        lax.fori_loop(0, X, plane, 0)
        for t in (2 * i, 2 * i + 1):
            c = pltpu.make_async_copy(obuf.at[t], out_hbm.at[:, pl.ds(128 * t, 128)], sem_out.at[t])
            c.start()
            puts.append(c)
    for c in puts:
        c.wait()


def shards(consts, dist, vel_index, relax, wall_mask, macro_inverse):
    vmem = pl.BlockSpec(memory_space=pltpu.VMEM)
    hbm = pl.BlockSpec(memory_space=pl.ANY)
    smem = pl.BlockSpec(memory_space=pltpu.SMEM)
    dma = pltpu.SemaphoreType.DMA
    sds = jax.ShapeDtypeStruct
    a, g2, mac, norm = pl.pallas_call(
        exchange,
        out_shape=(
            pltpu.VMEM((X + 4, LV, CELLS), F32), pltpu.VMEM((64, CELLS), F32),
            pltpu.VMEM((MOM, X, 32), F32), pltpu.VMEM((2, 8, 128), F32),
        ),
        in_specs=[hbm] + [vmem] * 9,
        out_specs=(vmem,) * 4,
        scratch_shapes=[
            pltpu.VMEM((LT, LV * X, 128), F32),
            pltpu.VMEM((X + 2, LV, CELLS), F32),
            pltpu.VMEM((X + 4, LV, CELLS), F32),
            pltpu.VMEM((X, 2 * LV, CELLS), BF16),
            pltpu.VMEM((X + 2, 2 * LV, CELLS), BF16),
            pltpu.VMEM((X + 2, 112, CELLS), F32),
            pltpu.VMEM((X + 2, 112, CELLS), F32),
            pltpu.VMEM((2, X, 16, CELLS), F32),
            pltpu.VMEM((2, 48, CELLS), F32),
            pltpu.VMEM((48, CELLS), F32),
            pltpu.VMEM((48, CELLS), F32),
            pltpu.VMEM((2 * X, CELLS), F32),
            pltpu.VMEM((2 * X, CELLS), F32),
            pltpu.VMEM((2 * X, CELLS), F32),
            pltpu.VMEM((16, LV), F32),
            pltpu.VMEM((224, 2 * LV), BF16),
            pltpu.VMEM((4, LV, LV), F32),
            pltpu.VMEM((2 * LV, 2 * LV), BF16),
            pltpu.VMEM((26 * X, X * MOM), F32),
            pltpu.VMEM((2, 2 * CH, CELLS), F32),
            pltpu.VMEM((2, PEERS, CH, 128), F32),
            pltpu.VMEM((2, CH, 128), F32),
            pltpu.VMEM((2, CH, 128), F32),
            pltpu.VMEM((2, CH, 128), F32),
            pltpu.VMEM((2, 2 * CH, CELLS), F32),
            pltpu.VMEM((26 * X, CELLS), F32),
            pltpu.VMEM((2, 32, CELLS), F32),
            pltpu.VMEM((32, CELLS), F32),
            pltpu.VMEM((32, CELLS), F32),
            pltpu.VMEM((32, CELLS), F32),
            pltpu.VMEM((2, 16, CELLS), F32),
            pltpu.VMEM((16, CELLS), F32),
            pltpu.VMEM((16, CELLS), F32),
            pltpu.VMEM((2, 4, 32, CELLS), F32),
            pltpu.VMEM((4, EXT, CELLS), F32),
            pltpu.VMEM((8 * EXT, CELLS), F32),
            pltpu.VMEM((256, CELLS), F32),
            pltpu.VMEM((56, LV), F32),
            pltpu.VMEM((LV, 224), BF16),
            pltpu.VMEM((X * MOM, CELLS), F32),
            pltpu.VMEM((22 * X, CELLS), F32),
            pltpu.VMEM((2, 8, 128), F32),
            pltpu.VMEM((3, 2, 8, 128), F32),
            pltpu.VMEM((2, LV // 2, CELLS), F32),
            pltpu.VMEM((2, LV // 2, CELLS), F32),
            pltpu.VMEM((2, LV // 2, CELLS), F32),
            pltpu.VMEM((2, LV // 2, CELLS), F32),
            pltpu.VMEM((2, LV, CELLS), F32),
            dma((LT,)), dma((14,)), dma((14,)), dma((2,)), dma((2,)), dma((2,)), dma((2,)), dma((2,)), dma((2,)),
            dma((3,)), dma((3,)), dma((5,)), dma((5,)),
        ],
        compiler_params=pltpu.CompilerParams(collective_id=0, has_side_effects=True, vmem_limit_bytes=54 * 2 ** 20),
        name="exchange",
    )(dist.reshape(LV * X, CELLS), relax, wall_mask, vel_index, macro_inverse, *consts)

    out, mac, norm = pl.pallas_call(
        renew,
        out_shape=(sds((LV * X, CELLS), F32), sds((MOM, X, 32), F32), sds((2,), F32)),
        in_specs=[vmem] * 5,
        out_specs=(hbm, vmem, smem),
        scratch_shapes=[
            pltpu.VMEM((LT, LV * X, 128), F32),
            pltpu.VMEM((LT, 64, 128), F32),
            pltpu.VMEM((X, 32, CELLS), BF16),
            pltpu.VMEM((LV, 32), BF16),
            dma((LT,)),
        ],
        compiler_params=pltpu.CompilerParams(vmem_limit_bytes=32 * 2 ** 20),
        name="renew",
    )(a, g2, vel_index, mac, norm)
    return (out.reshape(LV, X, CELLS), mac, norm)


def solution(mesh):
    consts = selection() + [coupling_table()]
    return jax.shard_map(
        lambda *args: shards([jnp.asarray(c) for c in consts], *args),
        mesh=mesh,
        in_specs=(P("vel", "space", None), P(None, "vel"), P("space", None), P("space", None), P()),
        out_specs=(P("vel", "space", None), P(None, "space", "vel"), P()),
        check_vma=False,
    )
```
